32 devices in a mesh: doc: 8 (over y, x, core), seq: 4 (over z).
Axes of the slice: x: 2, y: 2, z: 4, core: 2. Of those that a mesh axis runs over, the one named last changes fastest.
Arguments:
- tokens: bfloat16 [8, 2048, 1024], P('doc', 'seq'), may hold values from -6 to 6
- w_query: bfloat16 [1024, 1024], P(('doc', 'seq')), may hold values from -0.1875 to 0.1875
- w_key: bfloat16 [1024, 1024], P(('doc', 'seq')), may hold values from -0.1875 to 0.1875
- w_value: bfloat16 [1024, 1024], P(('doc', 'seq')), may hold values from -0.1875 to 0.1875
- w_out: bfloat16 [1024, 1024], P(('doc', 'seq')), may hold values from -2 to 2
- w_gate: bfloat16 [1024, 2816], P(('doc', 'seq')), may hold values from -0.1875 to 0.1875
- w_up: bfloat16 [1024, 2816], P(('doc', 'seq')), may hold values from -0.1875 to 0.1875
- w_down: bfloat16 [2816, 1024], P(('doc', 'seq')), may hold values from -0.109375 to 0.109375
- gain_attn: bfloat16 [1024], P(('doc', 'seq')), may hold values from 0.5 to 1.5
- gain_ffn: bfloat16 [1024], P(('doc', 'seq')), may hold values from 0.5 to 1.5
- cache_keys: bfloat16 [8, 512, 1024], P('doc', 'seq'), may hold values from -6 to 6
- cache_values: bfloat16 [8, 512, 1024], P('doc', 'seq'), may hold values from -6 to 6
- memory_flags: int32 [8], P('doc'), may hold values 0 or 1
- memory_source: int32 [8], P('doc'), may hold values from 0 to 7
- positions: int32 [8, 2048], P('doc', 'seq'), may hold values from 0 to 5118, as said below
- out_grad: bfloat16 [8, 2048, 1024], P('doc', 'seq'), may hold values from -6 to 6
Outputs:
- layer_out: bfloat16 [8, 2048, 1024], P('doc', 'seq')
- grad_tokens: float32 [8, 2048, 1024], P('doc', 'seq')
- grad_query: float32 [1024, 1024], P(('doc', 'seq'))
- grad_key: float32 [1024, 1024], P(('doc', 'seq'))
- grad_value: float32 [1024, 1024], P(('doc', 'seq'))
- grad_out: float32 [1024, 1024], P(('doc', 'seq'))
- grad_gate: float32 [1024, 2816], P(('doc', 'seq'))
- grad_up: float32 [1024, 2816], P(('doc', 'seq'))
- grad_down: float32 [2816, 1024], P(('doc', 'seq'))
- grad_gain_attn: float32 [1024], P(('doc', 'seq'))
- grad_gain_ffn: float32 [1024], P(('doc', 'seq'))
The draws below stay inside these ranges and needn't reach their ends.
Inputs may be any that keep to these rules, and one draw needn't show every extreme that they name: `positions`: within a segment each position is 1 or 2 more than the one before.
All inputs are finite; a program needn't handle non-finite values. No bound on the sum of `memory_flags` on one device may be relied on, other than what follows from the above.
Results may differ from the reference program's by a relative error of at most 0.04.
Values may be sent and summed in bfloat16 or wider, within the bound.
No kernel may reach another device: no remote copies, remote signals or barrier semaphores. Data moves between devices by JAX's collectives and lax.ppermute only.
A program may use at most 256 MiB of HBM per device.

```python
import math
import jax
import jax.numpy as jnp
from jax import lax

D = 1024
HEADS = 8
HEAD_DIM = 128
FF = 2816
SEG = 2048
CACHE = 512
SEGMENTS = 8


def draw_positions(key, part):
    step_key = jax.random.fold_in(key, 11)
    base_key = jax.random.fold_in(key, 12)
    pick_key = jax.random.fold_in(key, 13)
    step_sizes = jax.random.randint(step_key, (SEGMENTS, SEG), 1, 3)
    offsets = jax.random.randint(base_key, (SEGMENTS,), 0, 1025)
    top_seg = jax.random.randint(pick_key, (), 0, SEGMENTS)
    low_seg = (top_seg + 1) % SEGMENTS
    seg_rows = jnp.arange(SEGMENTS, dtype=jnp.int32)
    columns = jnp.arange(SEG, dtype=jnp.int32)
    step_sizes = jnp.where(seg_rows[:, None] == top_seg, 2, step_sizes)
    step_sizes = jnp.where(columns[None, :] == 0, 0, step_sizes)
    offsets = jnp.where(seg_rows == top_seg, 1024, jnp.where(seg_rows == low_seg, 0, offsets))
    return (offsets[:, None] + jnp.cumsum(step_sizes, axis=1)).astype(jnp.int32)


def set_ends(result, stream_key, smallest, top_value):
    extent = result.shape
    spot = [jax.random.randint(jax.random.fold_in(stream_key, axis), (), 0, extent[axis]) for axis in range(len(extent))]
    result = result.at[tuple(spot)].set(smallest)
    longest = extent.index(max(extent))
    spot[longest] = (spot[longest] + 1) % extent[longest]
    return result.at[tuple(spot)].set(top_value)


def level_of(own_key, shape, cuts, smallest, largest):
    loudness, own = 1.0, jax.random.fold_in(own_key, 6)
    for position, parts in cuts:
        draws = jnp.exp(jax.random.uniform(jax.random.fold_in(own, position), (parts,), jnp.float32, smallest / len(cuts), largest / len(cuts)))
        loudness = loudness * jnp.repeat(draws, shape[position] // parts).reshape([-1 if axis == position else 1 for axis in range(len(shape))])
    return loudness


def gaussian(stream_key, extent, spread, limit, cuts=(), kind=jnp.bfloat16):
    array = spread * jax.random.normal(stream_key, extent, jnp.float32)
    if cuts:
        array = array * level_of(stream_key, extent, cuts, -0.22, 0.18)
    return jnp.clip(array, -limit, limit).astype(kind)


def setup_inputs(seed: int = 0) -> dict:
    seeds = jax.random.split(jax.random.key(seed), 17)
    tokens = gaussian(seeds[0], (SEGMENTS, SEG, D), 1.0, 6.0, ((0, 8), (1, 4)))
    w_query = gaussian(seeds[1], (D, D), D ** -0.5, 0.1875, ((0, 32),))
    w_key = gaussian(seeds[2], (D, D), D ** -0.5, 0.1875, ((0, 32),))
    w_value = gaussian(seeds[3], (D, D), D ** -0.5, 0.1875, ((0, 32),))
    w_out = gaussian(seeds[4], (D, D), (D // 128) ** -0.5, 2.0, ((0, 32),))
    w_gate = gaussian(seeds[5], (D, FF), D ** -0.5, 0.1875, ((0, 32),))
    w_up = gaussian(seeds[6], (D, FF), D ** -0.5, 0.1875, ((0, 32),))
    w_down = gaussian(seeds[7], (FF, D), FF ** -0.5, 0.109375, ((0, 32),))
    gain_attn = jnp.clip(1.0 + 0.1 * jax.random.normal(seeds[8], (D,), jnp.float32), 0.5, 1.5).astype(jnp.bfloat16)
    gain_ffn = jnp.clip(1.0 + 0.1 * jax.random.normal(seeds[9], (D,), jnp.float32), 0.5, 1.5).astype(jnp.bfloat16)
    cache_keys = gaussian(seeds[10], (SEGMENTS, CACHE, D), 1.0, 6.0, ((0, 8), (1, 4)))
    cache_values = gaussian(seeds[11], (SEGMENTS, CACHE, D), 1.0, 6.0, ((0, 8), (1, 4)))
    memory_flags = set_ends((jax.random.randint(seeds[12], (SEGMENTS,), 0, 2) < 1).astype(jnp.int32), jax.random.fold_in(seeds[12], 1), 0, 1)
    memory_source = set_ends(jax.random.randint(seeds[13], (SEGMENTS,), 0, SEGMENTS), jax.random.fold_in(seeds[13], 1), 0, SEGMENTS - 1).astype(jnp.int32)
    positions = draw_positions(jax.random.fold_in(seeds[16], 71), 0)
    out_grad = gaussian(seeds[15], (SEGMENTS, SEG, D), 1.0, 6.0, ((0, 8), (1, 4)))
    return {"tokens": tokens, "w_query": w_query, "w_key": w_key, "w_value": w_value, "w_out": w_out, "w_gate": w_gate, "w_up": w_up, "w_down": w_down, "gain_attn": gain_attn, "gain_ffn": gain_ffn, "cache_keys": cache_keys, "cache_values": cache_values, "memory_flags": memory_flags, "memory_source": memory_source, "positions": positions, "out_grad": out_grad}


@jax.custom_vjp
def low(v):
    return lax.optimization_barrier(v.astype(jnp.bfloat16)).astype(jnp.float32)

@jax.custom_vjp
def low_back(v):
    return v

def low_keep(v):
    return (low(v), None)

def low_pass(kept, grad):
    return (grad,)

def back_keep(v):
    return (v, None)

def back_low(kept, grad):
    return (low(grad),)
low.defvjp(low_keep, low_pass)
low_back.defvjp(back_keep, back_low)
EPS_NORM = 1e-05
NEG_FILL = -1e+30

def rms_norm(values):
    return values * lax.rsqrt(lax.optimization_barrier(jnp.mean(values * values, -1, keepdims=True)) + EPS_NORM)

def rotary_tables(token_pos):
    half_dim = HEAD_DIM // 2
    frequency = jnp.exp(jnp.arange(half_dim, dtype=jnp.float32) * (-2.0 * math.log(10000.0) / HEAD_DIM))
    angles = token_pos.astype(jnp.float32)[..., None] * frequency
    return (jnp.cos(angles), jnp.sin(angles))

def rotate(values, cos_vals, sin_vals):
    half_dim = values.shape[-1] // 2
    first_half = values[..., :half_dim]
    second_half = values[..., half_dim:]
    cos_b = cos_vals[..., None, :]
    sin_b = sin_vals[..., None, :]
    return jnp.concatenate([first_half * cos_b - second_half * sin_b, second_half * cos_b + first_half * sin_b], -1)

def forward(weights_all, tokens_seg, mem_keys, mem_values, mem_flag, cos_vals, sin_vals):
    w_query, w_key, w_value, w_out, w_gate, w_up, w_down, gain_attn, gain_ffn = weights_all
    highest = lax.Precision.HIGHEST
    score_scale = 1.0 / math.sqrt(HEAD_DIM)
    attn_in = low(rms_norm(tokens_seg) * gain_attn)
    query_f = low_back(jnp.dot(attn_in, w_query, precision=highest))
    keys_f = low_back(jnp.dot(attn_in, w_key, precision=highest))
    value_f = low(low_back(jnp.dot(attn_in, w_value, precision=highest)))
    q_heads = query_f.reshape(SEG, HEADS, HEAD_DIM)
    q_rot = low(rotate(q_heads, cos_vals, sin_vals))
    q_mem = low(q_heads)
    k_rot = low(rotate(keys_f.reshape(SEG, HEADS, HEAD_DIM), cos_vals, sin_vals))
    v_heads = value_f.reshape(SEG, HEADS, HEAD_DIM)
    mk_heads = mem_keys.reshape(-1, HEADS, HEAD_DIM)
    mv_heads = mem_values.reshape(-1, HEADS, HEAD_DIM)
    q_len = min(512, SEG)
    n_blocks = SEG // q_len

    def q_block(block_num):
        row_start = block_num * q_len
        qr_part = lax.dynamic_slice_in_dim(q_rot, row_start, q_len, 0)
        qm_part = lax.dynamic_slice_in_dim(q_mem, row_start, q_len, 0)
        local_scores = low_back(jnp.einsum('qhd,khd->hqk', qr_part, k_rot, precision=highest) * score_scale)
        query_rows = row_start + jnp.arange(q_len, dtype=jnp.int32)
        key_cols = jnp.arange(SEG, dtype=jnp.int32)
        local_scores = jnp.where(key_cols[None, :] <= query_rows[:, None], local_scores, NEG_FILL)
        remote_scores = low_back(jnp.einsum('qhd,khd->hqk', qm_part, mk_heads, precision=highest) * score_scale)
        remote_scores = jnp.where(mem_flag > 0, remote_scores, NEG_FILL)
        probabilities = low(jax.nn.softmax(jnp.concatenate([local_scores, remote_scores], -1), axis=-1))
        local_part = jnp.einsum('hqk,khd->qhd', probabilities[..., :SEG], v_heads, precision=highest)
        remote_part = jnp.einsum('hqk,khd->qhd', probabilities[..., SEG:], mv_heads, precision=highest)
        return local_part + remote_part
    attended = lax.map(jax.checkpoint(q_block), jnp.arange(n_blocks, dtype=jnp.int32)).reshape(SEG, D)
    attn_low = low(low_back(attended))
    resid_mid = tokens_seg + low_back(jnp.dot(attn_low, w_out, precision=highest))
    ffn_in = low(rms_norm(resid_mid) * gain_ffn)
    gate_act = low_back(jnp.dot(ffn_in, w_gate, precision=highest))
    up_act = low_back(jnp.dot(ffn_in, w_up, precision=highest))
    hidden = low(jax.nn.silu(gate_act) * up_act)
    return resid_mid + jnp.dot(hidden, w_down, precision=highest)

def reference(tokens, w_query, w_key, w_value, w_out, w_gate, w_up, w_down, gain_attn, gain_ffn, cache_keys, cache_values, memory_flags, memory_source, positions, out_grad):
    weights_all = tuple((weight.astype(jnp.float32) for weight in (w_query, w_key, w_value, w_out, w_gate, w_up, w_down, gain_attn, gain_ffn)))

    def seg_step(running, seg_index):
        tokens_seg = tokens[seg_index].astype(jnp.float32)
        source_seg = memory_source[seg_index]
        mem_keys = jnp.concatenate([cache_keys[seg_index], cache_keys[source_seg]], 0).astype(jnp.float32)
        mem_values = jnp.concatenate([cache_values[seg_index], cache_values[source_seg]], 0).astype(jnp.float32)
        cos_vals, sin_vals = rotary_tables(positions[seg_index])
        mem_flag = memory_flags[seg_index]

        def forward_seg(weights_in, tokens_in):
            return forward(weights_in, tokens_in, mem_keys, mem_values, mem_flag, cos_vals, sin_vals)
        seg_out, pullback = jax.vjp(forward_seg, weights_all, tokens_seg)
        grad_w, grad_x = pullback(out_grad[seg_index].astype(jnp.float32))
        running = tuple((total + part for total, part in zip(running, grad_w)))
        return (running, (seg_out.astype(jnp.bfloat16), grad_x))
    zero_grads = tuple((jnp.zeros(weight.shape, jnp.float32) for weight in weights_all))
    totals, (outputs, grad_inputs) = lax.scan(seg_step, zero_grads, jnp.arange(SEGMENTS, dtype=jnp.int32))
    return (outputs, grad_inputs, totals[0], totals[1], totals[2], totals[3], totals[4], totals[5], totals[6], totals[7], totals[8])
```

```python
import functools
import math

import jax
import jax.numpy as jnp
from jax import lax
from jax.experimental import pallas as pl
from jax.experimental.pallas import tpu as pltpu
from jax.sharding import PartitionSpec as P

HEADS = 8
HEAD_DIM = 128


EPS_NORM = 1e-05
NEG_FILL = -1e30


def rms_factor(values):
    return lax.rsqrt(jnp.mean(values * values, -1, keepdims=True) + EPS_NORM)


def rotary_tables(token_pos):
    half_dim = HEAD_DIM // 2
    frequency = jnp.exp(
        jnp.arange(half_dim, dtype=jnp.float32) * (-2.0 * math.log(10000.0) / HEAD_DIM)
    )
    angles = token_pos.astype(jnp.float32)[..., None] * frequency
    return (jnp.cos(angles), jnp.sin(angles))


def rotate(values, cos_vals, sin_vals):
    half_dim = values.shape[-1] // 2
    first_half = values[..., :half_dim]
    second_half = values[..., half_dim:]
    cos_b = cos_vals[..., None, :]
    sin_b = sin_vals[..., None, :]
    return jnp.concatenate(
        [first_half * cos_b - second_half * sin_b, second_half * cos_b + first_half * sin_b], -1
    )


def rotate_back(grads, cos_vals, sin_vals):
    half_dim = grads.shape[-1] // 2
    first_half = grads[..., :half_dim]
    second_half = grads[..., half_dim:]
    cos_b = cos_vals[..., None, :]
    sin_b = sin_vals[..., None, :]
    return jnp.concatenate(
        [first_half * cos_b + second_half * sin_b, second_half * cos_b - first_half * sin_b], -1
    )


def online_step(fold_state, scores, allowed, value_heads):
    row_max, row_sum, weighted = fold_state
    masked = jnp.where(allowed, scores, NEG_FILL)
    new_max = jnp.maximum(row_max, jnp.max(masked, -1))
    weights_p = jnp.where(allowed, jnp.exp(scores - new_max[..., None]), 0.0)
    rescale = jnp.exp(row_max - new_max)
    row_sum = row_sum * rescale + jnp.sum(weights_p, -1)
    weighted = weighted * jnp.transpose(rescale, (0, 2, 1))[..., None] + jnp.einsum(
        "shqk,skhd->sqhd",
        weights_p.astype(jnp.bfloat16),
        value_heads,
        preferred_element_type=jnp.float32,
    )
    return (new_max, row_sum, weighted)


def norm_back(d_normed, normed, factor):
    return factor * (d_normed - normed * jnp.mean(d_normed * normed, -1, keepdims=True))


def on_device(
    tokens,
    w_query,
    w_key,
    w_value,
    w_out,
    w_gate,
    w_up,
    w_down,
    gain_attn,
    gain_ffn,
    cache_keys,
    cache_values,
    memory_flags,
    memory_source,
    positions,
    out_grad,
):
    fwd_weights = (
        lax.all_gather(w_query, ("doc", "seq"), axis=0, tiled=True),
        lax.all_gather(w_key, ("doc", "seq"), axis=0, tiled=True),
        lax.all_gather(w_value, ("doc", "seq"), axis=0, tiled=True),
        lax.all_gather(w_out, ("doc", "seq"), axis=0, tiled=True),
        lax.all_gather(w_gate, ("doc", "seq"), axis=0, tiled=True),
        lax.all_gather(w_up, ("doc", "seq"), axis=0, tiled=True),
        lax.all_gather(w_down, ("doc", "seq"), axis=0, tiled=True),
        lax.all_gather(gain_attn, ("doc", "seq"), axis=0, tiled=True),
        lax.all_gather(gain_ffn, ("doc", "seq"), axis=0, tiled=True),
    )
    seg_count, tok_local, model_width = tokens.shape
    ff_width = w_gate.shape[1]
    flat_rows = seg_count * tok_local
    score_scale = 1.0 / math.sqrt(HEAD_DIM)
    total_len = tok_local * lax.axis_size("seq")
    state_shape = (seg_count, HEADS, tok_local)
    head_shape = (seg_count, tok_local, HEADS, HEAD_DIM)
    inputs = tokens.astype(jnp.float32)
    factor_one = rms_factor(inputs)
    normed_one = inputs * factor_one
    attn_in = (normed_one * fwd_weights[7].astype(jnp.float32)).astype(jnp.bfloat16)
    query_f = jnp.dot(attn_in, fwd_weights[0], preferred_element_type=jnp.float32)
    keys_f = jnp.dot(attn_in, fwd_weights[1], preferred_element_type=jnp.float32)
    v_low = jnp.dot(attn_in, fwd_weights[2], preferred_element_type=jnp.float32).astype(
        jnp.bfloat16
    )
    cos_vals, sin_vals = rotary_tables(positions)
    q_heads = query_f.reshape(head_shape)
    q_rot = rotate(q_heads, cos_vals, sin_vals).astype(jnp.bfloat16)
    q_mem = q_heads.astype(jnp.bfloat16)
    k_rot = (
        rotate(keys_f.reshape(head_shape), cos_vals, sin_vals)
        .astype(jnp.bfloat16)
        .reshape(seg_count, tok_local, model_width)
    )
    query_rows = lax.axis_index("seq") * tok_local + jnp.arange(tok_local, dtype=jnp.int32)
    initial = (
        jnp.full(state_shape, NEG_FILL, jnp.float32),
        jnp.zeros(state_shape, jnp.float32),
        jnp.zeros(head_shape, jnp.float32),
    )
    key_part = lax.all_gather(k_rot, "seq", axis=1, tiled=True)
    value_part = lax.all_gather(v_low, "seq", axis=1, tiled=True)
    key_span = key_part.shape[1]
    key_heads = key_part.reshape(seg_count, key_span, HEADS, HEAD_DIM)
    scores = (
        jnp.einsum("sqhd,skhd->shqk", q_rot, key_heads, preferred_element_type=jnp.float32)
        * score_scale
    )
    key_cols = jnp.arange(key_span, dtype=jnp.int32)
    allowed = (key_cols[None, :] <= query_rows[:, None])[None, None]
    fold_state = online_step(
        initial, scores, allowed, value_part.reshape(seg_count, key_span, HEADS, HEAD_DIM)
    )
    every_keys, every_values = (
        lax.all_gather(cache_keys, "doc", axis=0, tiled=True),
        lax.all_gather(cache_values, "doc", axis=0, tiled=True),
    )
    mem_keys = jnp.concatenate([cache_keys, jnp.take(every_keys, memory_source, axis=0)], 1)
    mem_values = jnp.concatenate([cache_values, jnp.take(every_values, memory_source, axis=0)], 1)
    flag_on = (memory_flags > 0)[:, None, None, None]
    key_part = lax.all_gather(mem_keys, "seq", axis=1, tiled=True)
    value_part = lax.all_gather(mem_values, "seq", axis=1, tiled=True)
    key_span = key_part.shape[1]
    key_heads = key_part.reshape(seg_count, key_span, HEADS, HEAD_DIM)
    scores = (
        jnp.einsum("sqhd,skhd->shqk", q_mem, key_heads, preferred_element_type=jnp.float32)
        * score_scale
    )
    row_max, row_sum, weighted = online_step(
        fold_state, scores, flag_on, value_part.reshape(seg_count, key_span, HEADS, HEAD_DIM)
    )
    log_total = row_max + jnp.log(row_sum)
    attended = weighted / jnp.transpose(row_sum, (0, 2, 1))[..., None]
    attn_low = attended.reshape(flat_rows, model_width).astype(jnp.bfloat16)
    resid_mid = inputs.reshape(flat_rows, model_width) + jnp.dot(
        attn_low, fwd_weights[3], preferred_element_type=jnp.float32
    )
    factor_two = rms_factor(resid_mid)
    normed_two = resid_mid * factor_two
    ffn_in = (normed_two * fwd_weights[8].astype(jnp.float32)).astype(jnp.bfloat16)
    gate_act = jnp.dot(ffn_in, fwd_weights[4], preferred_element_type=jnp.float32)
    up_act = jnp.dot(ffn_in, fwd_weights[5], preferred_element_type=jnp.float32)
    sig_gate = jax.nn.sigmoid(gate_act)
    silu_gate = jax.nn.silu(gate_act)
    hidden = (silu_gate * up_act).astype(jnp.bfloat16)
    result = (
        resid_mid + jnp.dot(hidden, fwd_weights[6], preferred_element_type=jnp.float32)
    ).astype(jnp.bfloat16)
    back_weights = (
        lax.all_gather(w_query, ("doc", "seq"), axis=0, tiled=True),
        lax.all_gather(w_key, ("doc", "seq"), axis=0, tiled=True),
        lax.all_gather(w_value, ("doc", "seq"), axis=0, tiled=True),
        lax.all_gather(w_out, ("doc", "seq"), axis=0, tiled=True),
        lax.all_gather(w_gate, ("doc", "seq"), axis=0, tiled=True),
        lax.all_gather(w_up, ("doc", "seq"), axis=0, tiled=True),
        lax.all_gather(w_down, ("doc", "seq"), axis=0, tiled=True),
        lax.all_gather(gain_attn, ("doc", "seq"), axis=0, tiled=True),
        lax.all_gather(gain_ffn, ("doc", "seq"), axis=0, tiled=True),
    )
    grad_y = out_grad.reshape(flat_rows, model_width)
    d_hidden = jnp.einsum("td,fd->tf", grad_y, back_weights[6], preferred_element_type=jnp.float32)
    d_gate = (d_hidden * up_act * (sig_gate * (1.0 + gate_act * (1.0 - sig_gate)))).astype(
        jnp.bfloat16
    )
    d_up = (d_hidden * silu_gate).astype(jnp.bfloat16)
    d_ffn_in = jnp.einsum(
        "tf,df->td", d_gate, back_weights[4], preferred_element_type=jnp.float32
    ) + jnp.einsum("tf,df->td", d_up, back_weights[5], preferred_element_type=jnp.float32)
    g_gain_ffn = jnp.sum(d_ffn_in * normed_two, 0)
    d_mid = grad_y.astype(jnp.float32) + norm_back(
        d_ffn_in * back_weights[8].astype(jnp.float32), normed_two, factor_two
    )
    d_branch = d_mid.astype(jnp.bfloat16)
    d_att = (
        jnp.einsum("te,de->td", d_branch, back_weights[3], preferred_element_type=jnp.float32)
        .astype(jnp.bfloat16)
        .reshape(head_shape)
    )
    delta_rows = jnp.transpose(jnp.sum(d_att.astype(jnp.float32) * attended, -1), (0, 2, 1))
    gathered_keys, gathered_values = (
        lax.all_gather(k_rot, "seq", axis=1, tiled=True),
        lax.all_gather(v_low, "seq", axis=1, tiled=True),
    )
    block_len = min(512, total_len)
    n_blocks = total_len // block_len
    key_blocks = jnp.transpose(
        gathered_keys.reshape(seg_count, n_blocks, block_len, HEADS, HEAD_DIM), (1, 0, 2, 3, 4)
    )
    value_blocks = jnp.transpose(
        gathered_values.reshape(seg_count, n_blocks, block_len, HEADS, HEAD_DIM), (1, 0, 2, 3, 4)
    )

    def block_grads(key_heads, value_heads, block_num):
        scores = (
            jnp.einsum("sqhd,skhd->shqk", q_rot, key_heads, preferred_element_type=jnp.float32)
            * score_scale
        )
        key_cols = block_num * block_len + jnp.arange(block_len, dtype=jnp.int32)
        allowed = (key_cols[None, :] <= query_rows[:, None])[None, None]
        probabilities = jnp.where(allowed, jnp.exp(scores - log_total[..., None]), 0.0)
        d_probs = jnp.einsum(
            "sqhd,skhd->shqk", d_att, value_heads, preferred_element_type=jnp.float32
        )
        d_scores = (probabilities * (d_probs - delta_rows[..., None])).astype(jnp.bfloat16)
        return (probabilities, d_scores)

    def query_step(d_query_acc, block_inputs):
        key_heads, value_heads, block_num = block_inputs
        probabilities, d_scores = block_grads(key_heads, value_heads, block_num)
        return (
            d_query_acc
            + jnp.einsum(
                "shqk,skhd->sqhd", d_scores, key_heads, preferred_element_type=jnp.float32
            ),
            None,
        )

    d_qrot, unused_out = lax.scan(
        query_step,
        jnp.zeros(head_shape, jnp.float32),
        (key_blocks, value_blocks, jnp.arange(n_blocks, dtype=jnp.int32)),
    )
    own_keys = k_rot.reshape(head_shape)
    own_values = v_low.reshape(head_shape)
    lse_rows = jnp.transpose(log_total, (0, 2, 1))
    delta_tok = jnp.transpose(delta_rows, (0, 2, 1))
    q_part = lax.all_gather(q_rot, "seq", axis=1, tiled=True)
    datt_part = lax.all_gather(d_att, "seq", axis=1, tiled=True)
    lse_part = lax.all_gather(lse_rows.astype(jnp.bfloat16), "seq", axis=1, tiled=True).astype(
        jnp.float32
    )
    delta_part = lax.all_gather(delta_tok.astype(jnp.bfloat16), "seq", axis=1, tiled=True).astype(
        jnp.float32
    )
    row_span = q_part.shape[1]
    scores = (
        jnp.einsum("sqhd,skhd->shqk", q_part, own_keys, preferred_element_type=jnp.float32)
        * score_scale
    )
    visit_rows = jnp.arange(row_span, dtype=jnp.int32)
    allowed = (query_rows[None, :] <= visit_rows[:, None])[None, None]
    lse_heads = jnp.transpose(lse_part, (0, 2, 1))
    delta_heads = jnp.transpose(delta_part, (0, 2, 1))
    probabilities = jnp.where(allowed, jnp.exp(scores - lse_heads[..., None]), 0.0)
    d_probs = jnp.einsum(
        "sqhd,skhd->shqk", datt_part, own_values, preferred_element_type=jnp.float32
    )
    d_scores = (probabilities * (d_probs - delta_heads[..., None])).astype(jnp.bfloat16)
    key_acc = jnp.einsum("shqk,sqhd->skhd", d_scores, q_part, preferred_element_type=jnp.float32)
    value_acc = jnp.einsum(
        "shqk,sqhd->skhd",
        probabilities.astype(jnp.bfloat16),
        datt_part,
        preferred_element_type=jnp.float32,
    )
    key_acc, value_acc = (key_acc, value_acc)
    key_sum = key_acc.reshape(seg_count, tok_local, model_width)
    value_sum = value_acc.reshape(seg_count, tok_local, model_width)
    key_part = lax.all_gather(mem_keys, "seq", axis=1, tiled=True)
    value_part = lax.all_gather(mem_values, "seq", axis=1, tiled=True)
    key_span = key_part.shape[1]
    key_heads = key_part.reshape(seg_count, key_span, HEADS, HEAD_DIM)
    value_heads = value_part.reshape(seg_count, key_span, HEADS, HEAD_DIM)
    scores = (
        jnp.einsum("sqhd,skhd->shqk", q_mem, key_heads, preferred_element_type=jnp.float32)
        * score_scale
    )
    probabilities = jnp.where(flag_on, jnp.exp(scores - log_total[..., None]), 0.0)
    d_probs = jnp.einsum("sqhd,skhd->shqk", d_att, value_heads, preferred_element_type=jnp.float32)
    d_scores = (probabilities * (d_probs - delta_rows[..., None])).astype(jnp.bfloat16)
    d_qmem = jnp.einsum("shqk,skhd->sqhd", d_scores, key_heads, preferred_element_type=jnp.float32)
    d_query = (
        ((rotate_back(d_qrot, cos_vals, sin_vals) + d_qmem) * score_scale)
        .astype(jnp.bfloat16)
        .reshape(flat_rows, model_width)
    )
    d_key = (
        (rotate_back(key_sum.reshape(head_shape), cos_vals, sin_vals) * score_scale)
        .astype(jnp.bfloat16)
        .reshape(flat_rows, model_width)
    )
    d_value = value_sum.astype(jnp.bfloat16).reshape(flat_rows, model_width)
    attn_in_flat = attn_in.reshape(flat_rows, model_width)
    d_attn_in = jnp.einsum(
        "te,de->td", d_query, back_weights[0], preferred_element_type=jnp.float32
    )
    d_attn_in = d_attn_in + jnp.einsum(
        "te,de->td", d_key, back_weights[1], preferred_element_type=jnp.float32
    )
    d_attn_in = d_attn_in + jnp.einsum(
        "te,de->td", d_value, back_weights[2], preferred_element_type=jnp.float32
    )
    normed_flat = normed_one.reshape(flat_rows, model_width)
    g_gain_attn = jnp.sum(d_attn_in * normed_flat, 0)
    grad_in = d_mid + norm_back(
        d_attn_in * back_weights[7].astype(jnp.float32),
        normed_flat,
        factor_one.reshape(flat_rows, 1),
    )
    grad_tokens = grad_in.reshape(seg_count, tok_local, model_width)
    gate_part = jnp.einsum("td,tf->df", ffn_in, d_gate, preferred_element_type=jnp.float32)
    up_part = jnp.einsum("td,tf->df", ffn_in, d_up, preferred_element_type=jnp.float32)
    both_parts = lax.psum_scatter(
        jnp.concatenate([gate_part, up_part], 1), ("doc", "seq"), scatter_dimension=0, tiled=True
    )
    down_part = lax.psum_scatter(
        jnp.einsum("tf,td->fd", hidden, grad_y, preferred_element_type=jnp.float32),
        ("doc", "seq"),
        scatter_dimension=0,
        tiled=True,
    )
    query_part = jnp.einsum("td,te->de", attn_in_flat, d_query, preferred_element_type=jnp.float32)
    key_part = jnp.einsum("td,te->de", attn_in_flat, d_key, preferred_element_type=jnp.float32)
    value_part = jnp.einsum("td,te->de", attn_in_flat, d_value, preferred_element_type=jnp.float32)
    out_part = jnp.einsum("td,te->de", attn_low, d_branch, preferred_element_type=jnp.float32)
    attn_sums = lax.psum_scatter(
        jnp.concatenate([query_part, key_part, value_part, out_part], 1),
        ("doc", "seq"),
        scatter_dimension=0,
        tiled=True,
    )
    gain_attn_sum, gain_ffn_sum = (
        lax.psum_scatter(g_gain_attn, ("doc", "seq"), scatter_dimension=0, tiled=True),
        lax.psum_scatter(g_gain_ffn, ("doc", "seq"), scatter_dimension=0, tiled=True),
    )
    layer_out = result.reshape(seg_count, tok_local, model_width)
    return (
        layer_out,
        grad_tokens,
        attn_sums[:, :model_width],
        attn_sums[:, model_width : 2 * model_width],
        attn_sums[:, 2 * model_width : 3 * model_width],
        attn_sums[:, 3 * model_width :],
        both_parts[:, :ff_width],
        both_parts[:, ff_width:],
        down_part,
        gain_attn_sum,
        gain_ffn_sum,
    )


LINE = ("doc", "seq")
MXU = dict(preferred_element_type=jnp.float32)
LOG2E = 1.4426950408889634


def dot_nt(left, right):
    return lax.dot_general(left, right, (((1,), (1,)), ((), ())), **MXU)


def dot_tn(left, right):
    return lax.dot_general(left, right, (((0,), (0,)), ((), ())), **MXU)


def dot_nn(left, right):
    return jnp.dot(left, right, **MXU)


def whole(count):
    return [pl.BlockSpec(memory_space=pltpu.VMEM)] * count


def hbm(count):
    return [pl.BlockSpec(memory_space=pl.ANY)] * count


def smem():
    return pl.BlockSpec(memory_space=pltpu.SMEM)


def attend_kernel(
    place, b0, b1, b2, b3, mem_own, mem_src, cos_ref, sin_ref,
    qr_ref, qm_ref, kr_ref, v_ref, att_ref, lse_ref, o0, o1, o2, o3,
    max_s, sum_s, acc_s,
):
    quarter, flag = place[0], place[1]
    rows_q = b0.shape[0]
    width = o0.shape[1]
    heads = width // HEAD_DIM
    tiles = qr_ref.shape[0] // rows_q
    scale2 = LOG2E / math.sqrt(HEAD_DIM)
    half = HEAD_DIM // 2

    for rel, block in enumerate((b0, b1, b2, b3)):
        rows = pl.ds(pl.multiple_of((quarter ^ rel) * rows_q, rows_q), rows_q)
        cos_t, sin_t = cos_ref[rows, :], sin_ref[rows, :]
        for head in range(heads):
            cols = slice(head * HEAD_DIM, (head + 1) * HEAD_DIM)
            query = block[:, head * HEAD_DIM : (head + 1) * HEAD_DIM]
            qm_ref[rows, cols] = query
            wide = query.astype(jnp.float32)
            qr_ref[rows, cols] = (wide * cos_t + pltpu.roll(wide, half, 1) * sin_t).astype(
                jnp.bfloat16
            )
            wide = block[:, width + head * HEAD_DIM : width + (head + 1) * HEAD_DIM].astype(
                jnp.float32
            )
            kr_ref[rows, cols] = (wide * cos_t + pltpu.roll(wide, half, 1) * sin_t).astype(
                jnp.bfloat16
            )
            v_ref[rows, cols] = block[
                :, 2 * width + head * HEAD_DIM : 2 * width + (head + 1) * HEAD_DIM
            ]

    for head in range(heads):
        cols = slice(head * HEAD_DIM, (head + 1) * HEAD_DIM)
        vcols = slice(width + head * HEAD_DIM, width + (head + 1) * HEAD_DIM)

        def fold(scores, values):
            old_max = max_s[...]
            new_max = jnp.maximum(old_max, jnp.max(scores, 1, keepdims=True))
            spread = jnp.concatenate([new_max] * (scores.shape[1] // HEAD_DIM), 1)
            weights = jnp.exp2((scores - spread) * scale2)
            shrink = jnp.exp2((old_max - new_max) * scale2)
            sum_s[...] = sum_s[...] * shrink + jnp.sum(weights, 1, keepdims=True)
            acc_s[...] = acc_s[...] * shrink + dot_nn(weights.astype(jnp.bfloat16), values)
            max_s[...] = new_max

        def tile(index, carry):
            rows = pl.ds(pl.multiple_of(index * rows_q, rows_q), rows_q)
            query = qr_ref[rows, cols]
            max_s[...] = jnp.full_like(max_s, NEG_FILL)
            sum_s[...] = jnp.zeros_like(sum_s)
            acc_s[...] = jnp.zeros_like(acc_s)

            def earlier(block, inner):
                keys = pl.ds(pl.multiple_of(block * rows_q, rows_q), rows_q)
                fold(dot_nt(query, kr_ref[keys, cols]), v_ref[keys, cols])
                return inner

            lax.fori_loop(0, index, earlier, 0)
            scores = dot_nt(query, kr_ref[rows, cols])
            row_i = lax.broadcasted_iota(jnp.int32, scores.shape, 0)
            col_i = lax.broadcasted_iota(jnp.int32, scores.shape, 1)
            fold(jnp.where(col_i <= row_i, scores, NEG_FILL), v_ref[rows, cols])

            @pl.when(flag > 0)
            def _():
                plain = qm_ref[rows, cols]
                for mem in (mem_own, mem_src):
                    fold(dot_nt(plain, mem[:, cols]), mem[:, vcols])

            total = sum_s[...]
            att_ref[rows, cols] = (acc_s[...] / total).astype(jnp.bfloat16)
            lse = max_s[...] * scale2 + jnp.log(total) * LOG2E
            lse_ref[head, :, rows] = jnp.transpose(lse)[:8]
            return carry

        lax.fori_loop(0, tiles, tile, 0)

    for rel, out in enumerate((o0, o1, o2, o3)):
        rows = pl.ds(pl.multiple_of((quarter ^ rel) * rows_q, rows_q), rows_q)
        out[...] = att_ref[rows, :]


def attend(place, blocks, mem_own, mem_src, cos_t, sin_t):
    rows_q, three = blocks[0].shape
    width = three // 3
    length = cos_t.shape[0]
    low = jnp.bfloat16
    full = jax.ShapeDtypeStruct((length, width), low)
    part = jax.ShapeDtypeStruct((rows_q, width), low)
    return pl.pallas_call(
        attend_kernel,
        out_shape=[full] * 5
        + [jax.ShapeDtypeStruct((width // HEAD_DIM, 8, length), jnp.float32)]
        + [part] * 4,
        in_specs=[smem()] + whole(8),
        out_specs=whole(10),
        scratch_shapes=[pltpu.VMEM((rows_q, HEAD_DIM), jnp.float32)] * 3,
        compiler_params=pltpu.CompilerParams(vmem_limit_bytes=40 << 20),
        cost_estimate=pl.CostEstimate(
            flops=length * length * width * 4, bytes_accessed=14 << 20, transcendentals=length * length * 4
        ),
        name="attend",
    )(place, *blocks, mem_own, mem_src, cos_t, sin_t)


def attend_back_kernel(
    place, qr_ref, qm_ref, kr_ref, v_ref, att_ref, lse_ref, d0, d1, d2, d3, mem_own, mem_src,
    cos_ref, sin_ref, g0, g1, g2, g3, datt, dkey, dval, dqr, dqm, grads,
):
    quarter, flag = place[0], place[1]
    rows_q, width = d0.shape
    heads = width // HEAD_DIM
    tiles = qr_ref.shape[0] // rows_q
    scale = 1.0 / math.sqrt(HEAD_DIM)
    scale2 = LOG2E * scale
    half = HEAD_DIM // 2
    low = jnp.bfloat16

    def unrotate(grad, rows):
        return grad * cos_ref[rows, :] - pltpu.roll(grad, half, 1) * sin_ref[rows, :]

    for rel, block in enumerate((d0, d1, d2, d3)):
        rows = pl.ds(pl.multiple_of((quarter ^ rel) * rows_q, rows_q), rows_q)
        datt[rows, :] = block[...]

    for head in range(heads):
        cols = slice(head * HEAD_DIM, (head + 1) * HEAD_DIM)
        vcols = slice(width + head * HEAD_DIM, width + (head + 1) * HEAD_DIM)
        dkey[...] = jnp.zeros_like(dkey)
        dval[...] = jnp.zeros_like(dval)

        def tile(index, carry):
            rows = pl.ds(pl.multiple_of(index * rows_q, rows_q), rows_q)
            query = qr_ref[rows, cols]
            d_out = datt[rows, cols]
            delta = jnp.sum(
                jnp.transpose(d_out.astype(jnp.float32) * att_ref[rows, cols].astype(jnp.float32)),
                0,
                keepdims=True,
            )
            lse = lse_ref[head, 0:1, rows]
            dqr[...] = jnp.zeros_like(dqr)
            dqm[...] = jnp.zeros_like(dqm)

            def block_grads(keys, values, queries, masked):
                power = dot_nt(keys, queries) * scale2 - lse
                if masked:
                    key_i = lax.broadcasted_iota(jnp.int32, power.shape, 0)
                    query_i = lax.broadcasted_iota(jnp.int32, power.shape, 1)
                    power = jnp.where(key_i <= query_i, power, NEG_FILL)
                probs = jnp.exp2(power)
                d_scores = probs * (dot_nt(values, d_out) - delta)
                return probs.astype(low), d_scores.astype(low)

            def local(keys_at, masked):
                keys = kr_ref[keys_at, cols]
                probs, d_scores = block_grads(keys, v_ref[keys_at, cols], query, masked)
                dval[keys_at, :] += dot_nn(probs, d_out)
                dkey[keys_at, :] += dot_nn(d_scores, query)
                dqr[...] += dot_tn(d_scores, keys)

            def earlier(block, inner):
                local(pl.ds(pl.multiple_of(block * rows_q, rows_q), rows_q), False)
                return inner

            lax.fori_loop(0, index, earlier, 0)
            local(rows, True)

            @pl.when(flag > 0)
            def _():
                plain = qm_ref[rows, cols]
                for mem in (mem_own, mem_src):
                    keys = mem[:, cols]
                    probs, d_scores = block_grads(keys, mem[:, vcols], plain, False)
                    dqm[...] += dot_tn(d_scores, keys)

            grads[rows, cols] = ((unrotate(dqr[...], rows) + dqm[...]) * scale).astype(low)
            return carry

        lax.fori_loop(0, tiles, tile, 0)
        for index in range(tiles):
            rows = pl.ds(index * rows_q, rows_q)
            grads[rows, vcols] = (unrotate(dkey[rows, :], rows) * scale).astype(low)
            grads[rows, 2 * width + head * HEAD_DIM : 2 * width + (head + 1) * HEAD_DIM] = dval[
                rows, :
            ].astype(low)

    for rel, out in enumerate((g0, g1, g2, g3)):
        rows = pl.ds(pl.multiple_of((quarter ^ rel) * rows_q, rows_q), rows_q)
        out[...] = grads[rows, :]


def attend_back(place, saved, d_blocks, mem_own, mem_src, cos_t, sin_t):
    rows_q, width = d_blocks[0].shape
    length = cos_t.shape[0]
    low = jnp.bfloat16
    return pl.pallas_call(
        attend_back_kernel,
        out_shape=[jax.ShapeDtypeStruct((rows_q, 3 * width), low)] * 4,
        in_specs=[smem()] + whole(14),
        out_specs=whole(4),
        scratch_shapes=[
            pltpu.VMEM((length, width), low),
            pltpu.VMEM((length, HEAD_DIM), jnp.float32),
            pltpu.VMEM((length, HEAD_DIM), jnp.float32),
            pltpu.VMEM((rows_q, HEAD_DIM), jnp.float32),
            pltpu.VMEM((rows_q, HEAD_DIM), jnp.float32),
            pltpu.VMEM((length, 3 * width), low),
        ],
        compiler_params=pltpu.CompilerParams(vmem_limit_bytes=48 << 20),
        cost_estimate=pl.CostEstimate(
            flops=length * length * width * 10, bytes_accessed=14 << 20, transcendentals=length * length * 4
        ),
        name="attend_back",
    )(place, *saved, *d_blocks, mem_own, mem_src, cos_t, sin_t)


def settle_kernel(plan, widths, rows, n_pieces, *refs):
    where = refs[0]
    pieces = refs[1 : 1 + n_pieces]
    outs = refs[1 + n_pieces : 1 + n_pieces + len(widths)]
    sems = refs[-1]
    copies = []
    for piece, (rel, first, count) in zip(pieces, plan):
        start = pl.multiple_of((where[0] ^ rel) * rows + first, 16)
        left = 0
        for out, width in zip(outs, widths):
            copy = pltpu.make_async_copy(
                piece.at[:, pl.ds(left, width)],
                out.at[pl.ds(start, count), :],
                sems.at[len(copies)],
            )
            copy.start()
            copies.append(copy)
            left += width
    for copy in copies:
        copy.wait()


def settle(where, plan, pieces, widths, rows, n_doc):
    low = jnp.bfloat16
    return pl.pallas_call(
        functools.partial(settle_kernel, plan, widths, rows, len(pieces)),
        out_shape=[jax.ShapeDtypeStruct((n_doc * rows, width), low) for width in widths],
        in_specs=[smem()] + hbm(len(pieces)),
        out_specs=hbm(len(widths)),
        scratch_shapes=[pltpu.SemaphoreType.DMA((len(pieces) * len(widths),))],
        compiler_params=pltpu.CompilerParams(vmem_limit_bytes=4 << 20),
        cost_estimate=pl.CostEstimate(
            flops=0, bytes_accessed=4 * n_doc * rows * sum(widths), transcendentals=0
        ),
        name="settle",
    )(where, *pieces)


def segment_pairs(n_doc, n_seq):
    places = [(d, z) for d in range(n_doc) for z in range(n_seq)]

    def route(target):
        return [(d * n_seq + z, target(d, z)[0] * n_seq + target(d, z)[1]) for d, z in places]

    def regroup(d, z):
        return ((d & ~1) | (z >> 1), 2 * (d & 1) + (z & 1))

    return {
        "regroup": route(regroup),
        "core": route(lambda d, z: (d ^ 1, z)),
        "x": route(lambda d, z: (d ^ 2, z)),
        "y": route(lambda d, z: (d ^ 4, z)),
        1: route(lambda d, z: (d, z ^ 1)),
        2: route(lambda d, z: (d ^ 1, z)),
        3: route(lambda d, z: (d ^ 1, z ^ 1)),
        "z1": route(lambda d, z: (d, (z + 1) % n_seq)),
        "z2": route(lambda d, z: (d, (z + 2) % n_seq)),
        "z3": route(lambda d, z: (d, (z + 3) % n_seq)),
    }


def on_pair(
    routes,
    tokens,
    w_query,
    w_key,
    w_value,
    w_out,
    w_gate,
    w_up,
    w_down,
    gain_attn,
    gain_ffn,
    cache_keys,
    cache_values,
    memory_flags,
    memory_source,
    positions,
    out_grad,
):
    low, wide = jnp.bfloat16, jnp.float32
    n_doc, n_seq = lax.axis_size("doc"), lax.axis_size("seq")
    d, z = lax.axis_index("doc"), lax.axis_index("seq")
    core, odd, pair = d & 1, z & 1, z >> 1
    quarter = 2 * core + odd
    heads_at = 2 * odd + core
    turn = (0, 2, 1, 3)
    tok_local, width = tokens.shape[1:]
    ff_width = w_gate.shape[1]
    share = width // n_seq
    where = d.astype(jnp.int32).reshape(1)

    def move(array, name):
        return lax.ppermute(array, LINE, routes[name])

    def pick(array, index, axis=0):
        return lax.dynamic_index_in_dim(array, index, axis, keepdims=False)

    def gather(shard):
        block = lax.all_gather(shard, "seq", axis=0, tiled=True)
        rows = block.shape[0]
        cut = rows // 2
        by_x, by_y = move(block, "x"), move(block, "y")
        far_a, far_b = move(by_x[:cut], "y"), move(by_y[cut:], "x")
        mine = (block, by_x, by_y, far_a, far_b)
        plan = ((0, 0, rows), (2, 0, rows), (4, 0, rows), (6, 0, cut), (6, cut, cut))
        other = tuple(move(piece, "core") for piece in mine)
        plan = plan + tuple((rel ^ 1, first, count) for rel, first, count in plan)
        return plan, mine + other, rows

    cols = []
    for index in range(n_seq):
        for weight in (w_query, w_key, w_value):
            cols.append(weight[:, index * share : (index + 1) * share])
    gains = jnp.concatenate([gain_attn[:, None], gain_ffn[:, None]], 1)
    cols.append(jnp.pad(gains, ((0, 0), (0, HEAD_DIM - 2))))
    shard_qkv = jnp.concatenate(cols, 1)
    shard_ffn = jnp.concatenate([w_out, w_gate, w_up], 1)

    plan, pieces, rows = gather(shard_qkv)
    w_qkv, gain_cols = settle(where, plan, pieces, (3 * width, HEAD_DIM), rows, n_doc)
    plan, pieces, rows = gather(shard_ffn)
    w_out_f, w_gate_f, w_up_f = settle(
        where, plan, pieces, (width, ff_width, ff_width), rows, n_doc
    )
    plan, pieces, rows_down = gather(w_down)
    (w_down_f,) = settle(where, plan, pieces, (width,), rows_down, n_doc)
    gain_a = gain_cols[:, 0].astype(wide)
    gain_f = gain_cols[:, 1].astype(wide)

    tok = move(tokens[0], "regroup")
    grad_y = move(out_grad[0], "regroup")

    notes = jnp.concatenate([memory_flags, memory_source])
    notes = jnp.where(pair == core, notes, move(notes, "core"))
    notes_y = move(notes, "y")
    flag, source, source_y = notes[0], notes[1], notes_y[1]
    pos = lax.all_gather(positions[0], "seq", axis=0, tiled=True)
    pos = jnp.where(pair == core, pos, move(pos, "core"))
    cos_h, sin_h = rotary_tables(pos)
    cos_t = jnp.concatenate([cos_h, cos_h], -1)
    sin_t = jnp.concatenate([-sin_h, sin_h], -1)
    place = jnp.stack([quarter, flag]).astype(jnp.int32)

    def half_of(which):
        at = which * (width // 2)
        return jnp.concatenate(
            [
                lax.dynamic_slice_in_dim(cache[0], at, width // 2, 1)
                for cache in (cache_keys, cache_values)
            ],
            1,
        )

    same, cross = half_of(odd), half_of(1 - odd)
    column = jnp.concatenate(
        [same, move(cross, "z1"), move(same, "z2"), move(cross, "z3")], 0
    )
    parts = column.reshape(column.shape[0], 2, 2, share)
    kept = pick(parts, core, 2).reshape(-1, 2 * share)
    sent = move(pick(parts, 1 - core, 2).reshape(-1, 2 * share), "core")
    here = jnp.stack([kept, sent])
    four = jnp.concatenate([here, move(here, "x")], 0)

    def rel_of(src):
        return 2 * (((src ^ d) >> 1) & 1) + ((src ^ d) & 1)

    from_y = move(pick(four, rel_of(source_y)), "y")
    mem_src = jnp.where(((source ^ d) >> 2) == 0, pick(four, rel_of(source)), from_y)
    mem_own = pick(here, pair ^ core)

    inputs = tok.astype(wide)
    factor_one = rms_factor(inputs)
    normed_one = inputs * factor_one
    attn_in = (normed_one * gain_a).astype(low)
    qkv = dot_nn(attn_in, w_qkv).astype(low)

    def part_for(array, rel, size):
        return lax.dynamic_slice_in_dim(array, (heads_at ^ turn[rel]) * size, size, 1)

    def spread(blocks):
        size = blocks[0].shape[1]
        out = jnp.zeros((blocks[0].shape[0], n_seq * size), low)
        for rel, block in enumerate(blocks):
            out = lax.dynamic_update_slice_in_dim(out, block, (heads_at ^ turn[rel]) * size, 1)
        return out

    def exchange(blocks):
        return [blocks[0]] + [move(blocks[rel], rel) for rel in (1, 2, 3)]

    blocks = exchange([part_for(qkv, rel, 3 * share) for rel in range(4)])
    *saved, o0, o1, o2, o3 = attend(place, blocks, mem_own, mem_src, cos_t, sin_t)
    attn_low = spread(exchange([o0, o1, o2, o3]))
    resid_mid = inputs + dot_nn(attn_low, w_out_f)
    factor_two = rms_factor(resid_mid)
    normed_two = resid_mid * factor_two
    ffn_in = (normed_two * gain_f).astype(low)
    gate_act = dot_nn(ffn_in, w_gate_f)
    up_act = dot_nn(ffn_in, w_up_f)
    sig_gate = jax.nn.sigmoid(gate_act)
    silu_gate = gate_act * sig_gate
    hidden = (silu_gate * up_act).astype(low)
    layer_out = move((resid_mid + dot_nn(hidden, w_down_f)).astype(low), "regroup")

    def reduce(grads, block_rows):
        cut = block_rows // 2

        def side(which):
            picked = [
                pick(grad.reshape(n_doc // 2, 2, block_rows, grad.shape[1]), which, 1)
                for grad in grads
            ]
            return picked[0] if len(picked) == 1 else jnp.concatenate(picked, 2)

        met = move(side(1 - core), "core")
        both = (side(core).astype(wide) + met.astype(wide)).astype(low)
        at = d >> 1
        far = pick(both, at ^ 3)
        in_a, in_b = move(far[:cut], "y"), move(far[cut:], "x")
        to_x, to_y = pick(both, at ^ 1), pick(both, at ^ 2)
        to_x = jnp.concatenate(
            [(to_x[:cut].astype(wide) + in_a.astype(wide)).astype(low), to_x[cut:]], 0
        )
        to_y = jnp.concatenate(
            [to_y[:cut], (to_y[cut:].astype(wide) + in_b.astype(wide)).astype(low)], 0
        )
        in_x, in_y = move(to_x, "x"), move(to_y, "y")
        total = (
            pick(both, at).astype(wide) + in_x.astype(wide) + in_y.astype(wide)
        ).astype(low)
        return lax.psum_scatter(total, "seq", scatter_dimension=0, tiled=True).astype(wide)

    def row_sums(product):
        ones = jnp.ones((product.shape[0], HEAD_DIM), low)
        return dot_tn(product.astype(low), ones).astype(low)

    d_hidden = dot_nt(grad_y, w_down_f)
    grad_down = dot_tn(hidden, grad_y).astype(low)
    out_down = reduce([grad_down], rows_down)
    d_gate = (d_hidden * up_act * (sig_gate * (1.0 + gate_act * (1.0 - sig_gate)))).astype(low)
    d_up = (d_hidden * silu_gate).astype(low)
    d_ffn_in = dot_nt(d_gate, w_gate_f) + dot_nt(d_up, w_up_f)
    d_mid = grad_y.astype(wide) + norm_back(d_ffn_in * gain_f, normed_two, factor_two)
    d_branch = d_mid.astype(low)
    d_att = dot_nt(d_branch, w_out_f).astype(low)
    d_blocks = exchange([part_for(d_att, rel, share) for rel in range(4)])
    grad_gate = dot_tn(ffn_in, d_gate).astype(low)
    grad_up = dot_tn(ffn_in, d_up).astype(low)
    grad_out = dot_tn(attn_low, d_branch).astype(low)
    gain_f_cols = row_sums(d_ffn_in * normed_two)
    out_ffn = reduce([grad_gate, grad_up], rows)
    out_mid = reduce([grad_out, gain_f_cols], rows)
    d_parts = attend_back(place, saved, d_blocks, mem_own, mem_src, cos_t, sin_t)
    d_qkv = spread(exchange(d_parts))
    d_attn_in = dot_nt(d_qkv, w_qkv)
    grad_qkv = dot_tn(attn_in, d_qkv).astype(low)
    gain_a_cols = row_sums(d_attn_in * normed_one)
    out_qkv = reduce([grad_qkv, gain_a_cols], rows)
    grad_in = d_mid + norm_back(d_attn_in * gain_a, normed_one, factor_one)
    grad_tokens = move(grad_in.astype(low), "regroup").astype(wide)

    split = out_qkv[:, : 3 * width].reshape(-1, n_seq, 3, share)
    out_q, out_k, out_v = (split[:, :, which].reshape(-1, width) for which in range(3))
    return (
        layer_out[None],
        grad_tokens[None],
        out_q,
        out_k,
        out_v,
        out_mid[:, :width],
        out_ffn[:, :ff_width],
        out_ffn[:, ff_width:],
        out_down,
        out_qkv[:, 3 * width],
        out_mid[:, width],
    )


def solution(mesh):
    in_specs = (
        P("doc", "seq", None),
        P(("doc", "seq"), None),
        P(("doc", "seq"), None),
        P(("doc", "seq"), None),
        P(("doc", "seq"), None),
        P(("doc", "seq"), None),
        P(("doc", "seq"), None),
        P(("doc", "seq"), None),
        P(("doc", "seq")),
        P(("doc", "seq")),
        P("doc", "seq", None),
        P("doc", "seq", None),
        P("doc"),
        P("doc"),
        P("doc", "seq"),
        P("doc", "seq", None),
    )
    out_specs = (
        P("doc", "seq", None),
        P("doc", "seq", None),
        P(("doc", "seq"), None),
        P(("doc", "seq"), None),
        P(("doc", "seq"), None),
        P(("doc", "seq"), None),
        P(("doc", "seq"), None),
        P(("doc", "seq"), None),
        P(("doc", "seq"), None),
        P(("doc", "seq")),
        P(("doc", "seq")),
    )
    n_doc, n_seq = mesh.shape["doc"], mesh.shape["seq"]
    step = on_device
    if (n_doc, n_seq) == (8, 4):
        step = functools.partial(on_pair, segment_pairs(n_doc, n_seq))
    return jax.shard_map(
        step, mesh=mesh, in_specs=in_specs, out_specs=out_specs, check_vma=False
    )
```

```python
import functools
import math

import jax
import jax.numpy as jnp
from jax import lax
from jax.experimental import pallas as pl
from jax.experimental.pallas import tpu as pltpu
from jax.sharding import PartitionSpec as P

HEADS = 8
HEAD_DIM = 128


EPS_NORM = 1e-05
NEG_FILL = -1e30


def rms_factor(values):
    return lax.rsqrt(jnp.mean(values * values, -1, keepdims=True) + EPS_NORM)


def rotary_tables(token_pos):
    half_dim = HEAD_DIM // 2
    frequency = jnp.exp(
        jnp.arange(half_dim, dtype=jnp.float32) * (-2.0 * math.log(10000.0) / HEAD_DIM)
    )
    angles = token_pos.astype(jnp.float32)[..., None] * frequency
    return (jnp.cos(angles), jnp.sin(angles))


def rotate(values, cos_vals, sin_vals):
    half_dim = values.shape[-1] // 2
    first_half = values[..., :half_dim]
    second_half = values[..., half_dim:]
    cos_b = cos_vals[..., None, :]
    sin_b = sin_vals[..., None, :]
    return jnp.concatenate(
        [first_half * cos_b - second_half * sin_b, second_half * cos_b + first_half * sin_b], -1
    )


def rotate_back(grads, cos_vals, sin_vals):
    half_dim = grads.shape[-1] // 2
    first_half = grads[..., :half_dim]
    second_half = grads[..., half_dim:]
    cos_b = cos_vals[..., None, :]
    sin_b = sin_vals[..., None, :]
    return jnp.concatenate(
        [first_half * cos_b + second_half * sin_b, second_half * cos_b - first_half * sin_b], -1
    )


def online_step(fold_state, scores, allowed, value_heads):
    row_max, row_sum, weighted = fold_state
    masked = jnp.where(allowed, scores, NEG_FILL)
    new_max = jnp.maximum(row_max, jnp.max(masked, -1))
    weights_p = jnp.where(allowed, jnp.exp(scores - new_max[..., None]), 0.0)
    rescale = jnp.exp(row_max - new_max)
    row_sum = row_sum * rescale + jnp.sum(weights_p, -1)
    weighted = weighted * jnp.transpose(rescale, (0, 2, 1))[..., None] + jnp.einsum(
        "shqk,skhd->sqhd",
        weights_p.astype(jnp.bfloat16),
        value_heads,
        preferred_element_type=jnp.float32,
    )
    return (new_max, row_sum, weighted)


def norm_back(d_normed, normed, factor):
    return factor * (d_normed - normed * jnp.mean(d_normed * normed, -1, keepdims=True))


def on_device(
    tokens,
    w_query,
    w_key,
    w_value,
    w_out,
    w_gate,
    w_up,
    w_down,
    gain_attn,
    gain_ffn,
    cache_keys,
    cache_values,
    memory_flags,
    memory_source,
    positions,
    out_grad,
):
    fwd_weights = (
        lax.all_gather(w_query, ("doc", "seq"), axis=0, tiled=True),
        lax.all_gather(w_key, ("doc", "seq"), axis=0, tiled=True),
        lax.all_gather(w_value, ("doc", "seq"), axis=0, tiled=True),
        lax.all_gather(w_out, ("doc", "seq"), axis=0, tiled=True),
        lax.all_gather(w_gate, ("doc", "seq"), axis=0, tiled=True),
        lax.all_gather(w_up, ("doc", "seq"), axis=0, tiled=True),
        lax.all_gather(w_down, ("doc", "seq"), axis=0, tiled=True),
        lax.all_gather(gain_attn, ("doc", "seq"), axis=0, tiled=True),
        lax.all_gather(gain_ffn, ("doc", "seq"), axis=0, tiled=True),
    )
    seg_count, tok_local, model_width = tokens.shape
    ff_width = w_gate.shape[1]
    flat_rows = seg_count * tok_local
    score_scale = 1.0 / math.sqrt(HEAD_DIM)
    total_len = tok_local * lax.axis_size("seq")
    state_shape = (seg_count, HEADS, tok_local)
    head_shape = (seg_count, tok_local, HEADS, HEAD_DIM)
    inputs = tokens.astype(jnp.float32)
    factor_one = rms_factor(inputs)
    normed_one = inputs * factor_one
    attn_in = (normed_one * fwd_weights[7].astype(jnp.float32)).astype(jnp.bfloat16)
    query_f = jnp.dot(attn_in, fwd_weights[0], preferred_element_type=jnp.float32)
    keys_f = jnp.dot(attn_in, fwd_weights[1], preferred_element_type=jnp.float32)
    v_low = jnp.dot(attn_in, fwd_weights[2], preferred_element_type=jnp.float32).astype(
        jnp.bfloat16
    )
    cos_vals, sin_vals = rotary_tables(positions)
    q_heads = query_f.reshape(head_shape)
    q_rot = rotate(q_heads, cos_vals, sin_vals).astype(jnp.bfloat16)
    q_mem = q_heads.astype(jnp.bfloat16)
    k_rot = (
        rotate(keys_f.reshape(head_shape), cos_vals, sin_vals)
        .astype(jnp.bfloat16)
        .reshape(seg_count, tok_local, model_width)
    )
    query_rows = lax.axis_index("seq") * tok_local + jnp.arange(tok_local, dtype=jnp.int32)
    initial = (
        jnp.full(state_shape, NEG_FILL, jnp.float32),
        jnp.zeros(state_shape, jnp.float32),
        jnp.zeros(head_shape, jnp.float32),
    )
    key_part = lax.all_gather(k_rot, "seq", axis=1, tiled=True)
    value_part = lax.all_gather(v_low, "seq", axis=1, tiled=True)
    key_span = key_part.shape[1]
    key_heads = key_part.reshape(seg_count, key_span, HEADS, HEAD_DIM)
    scores = (
        jnp.einsum("sqhd,skhd->shqk", q_rot, key_heads, preferred_element_type=jnp.float32)
        * score_scale
    )
    key_cols = jnp.arange(key_span, dtype=jnp.int32)
    allowed = (key_cols[None, :] <= query_rows[:, None])[None, None]
    fold_state = online_step(
        initial, scores, allowed, value_part.reshape(seg_count, key_span, HEADS, HEAD_DIM)
    )
    every_keys, every_values = (
        lax.all_gather(cache_keys, "doc", axis=0, tiled=True),
        lax.all_gather(cache_values, "doc", axis=0, tiled=True),
    )
    mem_keys = jnp.concatenate([cache_keys, jnp.take(every_keys, memory_source, axis=0)], 1)
    mem_values = jnp.concatenate([cache_values, jnp.take(every_values, memory_source, axis=0)], 1)
    flag_on = (memory_flags > 0)[:, None, None, None]
    key_part = lax.all_gather(mem_keys, "seq", axis=1, tiled=True)
    value_part = lax.all_gather(mem_values, "seq", axis=1, tiled=True)
    key_span = key_part.shape[1]
    key_heads = key_part.reshape(seg_count, key_span, HEADS, HEAD_DIM)
    scores = (
        jnp.einsum("sqhd,skhd->shqk", q_mem, key_heads, preferred_element_type=jnp.float32)
        * score_scale
    )
    row_max, row_sum, weighted = online_step(
        fold_state, scores, flag_on, value_part.reshape(seg_count, key_span, HEADS, HEAD_DIM)
    )
    log_total = row_max + jnp.log(row_sum)
    attended = weighted / jnp.transpose(row_sum, (0, 2, 1))[..., None]
    attn_low = attended.reshape(flat_rows, model_width).astype(jnp.bfloat16)
    resid_mid = inputs.reshape(flat_rows, model_width) + jnp.dot(
        attn_low, fwd_weights[3], preferred_element_type=jnp.float32
    )
    factor_two = rms_factor(resid_mid)
    normed_two = resid_mid * factor_two
    ffn_in = (normed_two * fwd_weights[8].astype(jnp.float32)).astype(jnp.bfloat16)
    gate_act = jnp.dot(ffn_in, fwd_weights[4], preferred_element_type=jnp.float32)
    up_act = jnp.dot(ffn_in, fwd_weights[5], preferred_element_type=jnp.float32)
    sig_gate = jax.nn.sigmoid(gate_act)
    silu_gate = jax.nn.silu(gate_act)
    hidden = (silu_gate * up_act).astype(jnp.bfloat16)
    result = (
        resid_mid + jnp.dot(hidden, fwd_weights[6], preferred_element_type=jnp.float32)
    ).astype(jnp.bfloat16)
    back_weights = (
        lax.all_gather(w_query, ("doc", "seq"), axis=0, tiled=True),
        lax.all_gather(w_key, ("doc", "seq"), axis=0, tiled=True),
        lax.all_gather(w_value, ("doc", "seq"), axis=0, tiled=True),
        lax.all_gather(w_out, ("doc", "seq"), axis=0, tiled=True),
        lax.all_gather(w_gate, ("doc", "seq"), axis=0, tiled=True),
        lax.all_gather(w_up, ("doc", "seq"), axis=0, tiled=True),
        lax.all_gather(w_down, ("doc", "seq"), axis=0, tiled=True),
        lax.all_gather(gain_attn, ("doc", "seq"), axis=0, tiled=True),
        lax.all_gather(gain_ffn, ("doc", "seq"), axis=0, tiled=True),
    )
    grad_y = out_grad.reshape(flat_rows, model_width)
    d_hidden = jnp.einsum("td,fd->tf", grad_y, back_weights[6], preferred_element_type=jnp.float32)
    d_gate = (d_hidden * up_act * (sig_gate * (1.0 + gate_act * (1.0 - sig_gate)))).astype(
        jnp.bfloat16
    )
    d_up = (d_hidden * silu_gate).astype(jnp.bfloat16)
    d_ffn_in = jnp.einsum(
        "tf,df->td", d_gate, back_weights[4], preferred_element_type=jnp.float32
    ) + jnp.einsum("tf,df->td", d_up, back_weights[5], preferred_element_type=jnp.float32)
    g_gain_ffn = jnp.sum(d_ffn_in * normed_two, 0)
    d_mid = grad_y.astype(jnp.float32) + norm_back(
        d_ffn_in * back_weights[8].astype(jnp.float32), normed_two, factor_two
    )
    d_branch = d_mid.astype(jnp.bfloat16)
    d_att = (
        jnp.einsum("te,de->td", d_branch, back_weights[3], preferred_element_type=jnp.float32)
        .astype(jnp.bfloat16)
        .reshape(head_shape)
    )
    delta_rows = jnp.transpose(jnp.sum(d_att.astype(jnp.float32) * attended, -1), (0, 2, 1))
    gathered_keys, gathered_values = (
        lax.all_gather(k_rot, "seq", axis=1, tiled=True),
        lax.all_gather(v_low, "seq", axis=1, tiled=True),
    )
    block_len = min(512, total_len)
    n_blocks = total_len // block_len
    key_blocks = jnp.transpose(
        gathered_keys.reshape(seg_count, n_blocks, block_len, HEADS, HEAD_DIM), (1, 0, 2, 3, 4)
    )
    value_blocks = jnp.transpose(
        gathered_values.reshape(seg_count, n_blocks, block_len, HEADS, HEAD_DIM), (1, 0, 2, 3, 4)
    )

    def block_grads(key_heads, value_heads, block_num):
        scores = (
            jnp.einsum("sqhd,skhd->shqk", q_rot, key_heads, preferred_element_type=jnp.float32)
            * score_scale
        )
        key_cols = block_num * block_len + jnp.arange(block_len, dtype=jnp.int32)
        allowed = (key_cols[None, :] <= query_rows[:, None])[None, None]
        probabilities = jnp.where(allowed, jnp.exp(scores - log_total[..., None]), 0.0)
        d_probs = jnp.einsum(
            "sqhd,skhd->shqk", d_att, value_heads, preferred_element_type=jnp.float32
        )
        d_scores = (probabilities * (d_probs - delta_rows[..., None])).astype(jnp.bfloat16)
        return (probabilities, d_scores)

    def query_step(d_query_acc, block_inputs):
        key_heads, value_heads, block_num = block_inputs
        probabilities, d_scores = block_grads(key_heads, value_heads, block_num)
        return (
            d_query_acc
            + jnp.einsum(
                "shqk,skhd->sqhd", d_scores, key_heads, preferred_element_type=jnp.float32
            ),
            None,
        )

    d_qrot, unused_out = lax.scan(
        query_step,
        jnp.zeros(head_shape, jnp.float32),
        (key_blocks, value_blocks, jnp.arange(n_blocks, dtype=jnp.int32)),
    )
    own_keys = k_rot.reshape(head_shape)
    own_values = v_low.reshape(head_shape)
    lse_rows = jnp.transpose(log_total, (0, 2, 1))
    delta_tok = jnp.transpose(delta_rows, (0, 2, 1))
    q_part = lax.all_gather(q_rot, "seq", axis=1, tiled=True)
    datt_part = lax.all_gather(d_att, "seq", axis=1, tiled=True)
    lse_part = lax.all_gather(lse_rows.astype(jnp.bfloat16), "seq", axis=1, tiled=True).astype(
        jnp.float32
    )
    delta_part = lax.all_gather(delta_tok.astype(jnp.bfloat16), "seq", axis=1, tiled=True).astype(
        jnp.float32
    )
    row_span = q_part.shape[1]
    scores = (
        jnp.einsum("sqhd,skhd->shqk", q_part, own_keys, preferred_element_type=jnp.float32)
        * score_scale
    )
    visit_rows = jnp.arange(row_span, dtype=jnp.int32)
    allowed = (query_rows[None, :] <= visit_rows[:, None])[None, None]
    lse_heads = jnp.transpose(lse_part, (0, 2, 1))
    delta_heads = jnp.transpose(delta_part, (0, 2, 1))
    probabilities = jnp.where(allowed, jnp.exp(scores - lse_heads[..., None]), 0.0)
    d_probs = jnp.einsum(
        "sqhd,skhd->shqk", datt_part, own_values, preferred_element_type=jnp.float32
    )
    d_scores = (probabilities * (d_probs - delta_heads[..., None])).astype(jnp.bfloat16)
    key_acc = jnp.einsum("shqk,sqhd->skhd", d_scores, q_part, preferred_element_type=jnp.float32)
    value_acc = jnp.einsum(
        "shqk,sqhd->skhd",
        probabilities.astype(jnp.bfloat16),
        datt_part,
        preferred_element_type=jnp.float32,
    )
    key_acc, value_acc = (key_acc, value_acc)
    key_sum = key_acc.reshape(seg_count, tok_local, model_width)
    value_sum = value_acc.reshape(seg_count, tok_local, model_width)
    key_part = lax.all_gather(mem_keys, "seq", axis=1, tiled=True)
    value_part = lax.all_gather(mem_values, "seq", axis=1, tiled=True)
    key_span = key_part.shape[1]
    key_heads = key_part.reshape(seg_count, key_span, HEADS, HEAD_DIM)
    value_heads = value_part.reshape(seg_count, key_span, HEADS, HEAD_DIM)
    scores = (
        jnp.einsum("sqhd,skhd->shqk", q_mem, key_heads, preferred_element_type=jnp.float32)
        * score_scale
    )
    probabilities = jnp.where(flag_on, jnp.exp(scores - log_total[..., None]), 0.0)
    d_probs = jnp.einsum("sqhd,skhd->shqk", d_att, value_heads, preferred_element_type=jnp.float32)
    d_scores = (probabilities * (d_probs - delta_rows[..., None])).astype(jnp.bfloat16)
    d_qmem = jnp.einsum("shqk,skhd->sqhd", d_scores, key_heads, preferred_element_type=jnp.float32)
    d_query = (
        ((rotate_back(d_qrot, cos_vals, sin_vals) + d_qmem) * score_scale)
        .astype(jnp.bfloat16)
        .reshape(flat_rows, model_width)
    )
    d_key = (
        (rotate_back(key_sum.reshape(head_shape), cos_vals, sin_vals) * score_scale)
        .astype(jnp.bfloat16)
        .reshape(flat_rows, model_width)
    )
    d_value = value_sum.astype(jnp.bfloat16).reshape(flat_rows, model_width)
    attn_in_flat = attn_in.reshape(flat_rows, model_width)
    d_attn_in = jnp.einsum(
        "te,de->td", d_query, back_weights[0], preferred_element_type=jnp.float32
    )
    d_attn_in = d_attn_in + jnp.einsum(
        "te,de->td", d_key, back_weights[1], preferred_element_type=jnp.float32
    )
    d_attn_in = d_attn_in + jnp.einsum(
        "te,de->td", d_value, back_weights[2], preferred_element_type=jnp.float32
    )
    normed_flat = normed_one.reshape(flat_rows, model_width)
    g_gain_attn = jnp.sum(d_attn_in * normed_flat, 0)
    grad_in = d_mid + norm_back(
        d_attn_in * back_weights[7].astype(jnp.float32),
        normed_flat,
        factor_one.reshape(flat_rows, 1),
    )
    grad_tokens = grad_in.reshape(seg_count, tok_local, model_width)
    gate_part = jnp.einsum("td,tf->df", ffn_in, d_gate, preferred_element_type=jnp.float32)
    up_part = jnp.einsum("td,tf->df", ffn_in, d_up, preferred_element_type=jnp.float32)
    both_parts = lax.psum_scatter(
        jnp.concatenate([gate_part, up_part], 1), ("doc", "seq"), scatter_dimension=0, tiled=True
    )
    down_part = lax.psum_scatter(
        jnp.einsum("tf,td->fd", hidden, grad_y, preferred_element_type=jnp.float32),
        ("doc", "seq"),
        scatter_dimension=0,
        tiled=True,
    )
    query_part = jnp.einsum("td,te->de", attn_in_flat, d_query, preferred_element_type=jnp.float32)
    key_part = jnp.einsum("td,te->de", attn_in_flat, d_key, preferred_element_type=jnp.float32)
    value_part = jnp.einsum("td,te->de", attn_in_flat, d_value, preferred_element_type=jnp.float32)
    out_part = jnp.einsum("td,te->de", attn_low, d_branch, preferred_element_type=jnp.float32)
    attn_sums = lax.psum_scatter(
        jnp.concatenate([query_part, key_part, value_part, out_part], 1),
        ("doc", "seq"),
        scatter_dimension=0,
        tiled=True,
    )
    gain_attn_sum, gain_ffn_sum = (
        lax.psum_scatter(g_gain_attn, ("doc", "seq"), scatter_dimension=0, tiled=True),
        lax.psum_scatter(g_gain_ffn, ("doc", "seq"), scatter_dimension=0, tiled=True),
    )
    layer_out = result.reshape(seg_count, tok_local, model_width)
    return (
        layer_out,
        grad_tokens,
        attn_sums[:, :model_width],
        attn_sums[:, model_width : 2 * model_width],
        attn_sums[:, 2 * model_width : 3 * model_width],
        attn_sums[:, 3 * model_width :],
        both_parts[:, :ff_width],
        both_parts[:, ff_width:],
        down_part,
        gain_attn_sum,
        gain_ffn_sum,
    )


LINE = ("doc", "seq")
MXU = dict(preferred_element_type=jnp.float32)
LOG2E = 1.4426950408889634


def dot_nt(left, right):
    return lax.dot_general(left, right, (((1,), (1,)), ((), ())), **MXU)


def dot_tn(left, right):
    return lax.dot_general(left, right, (((0,), (0,)), ((), ())), **MXU)


def dot_nn(left, right):
    return jnp.dot(left, right, **MXU)


def whole(count):
    return [pl.BlockSpec(memory_space=pltpu.VMEM)] * count


def hbm(count):
    return [pl.BlockSpec(memory_space=pl.ANY)] * count


def smem():
    return pl.BlockSpec(memory_space=pltpu.SMEM)


def place_rows(quarter, rel, rows_q):
    return pl.ds(pl.multiple_of((quarter ^ rel) * rows_q, rows_q), rows_q)


def stack_memory(pieces, head, keys_ref, vals_ref):
    count = keys_ref.shape[0] // (2 * len(pieces))
    span = pieces[0].shape[1] // 4
    at = 0
    for piece in pieces:
        for part in (0, 2):
            left = part * span + head * HEAD_DIM
            keys_ref[at : at + count, :] = piece[:count, left : left + HEAD_DIM]
            vals_ref[at : at + count, :] = piece[:count, left + span : left + span + HEAD_DIM]
            at += count


def fetch(sources, targets, sems):
    copies = [
        pltpu.make_async_copy(source, target, sems.at[index])
        for index, (source, target) in enumerate(zip(sources, targets))
    ]
    for copy in copies:
        copy.start()
    return copies


def attend_kernel(head, n_in, *refs):
    place = refs[0]
    given, refs = refs[1 : 1 + n_in], refs[1 + n_in :]
    n_kept = n_in - 10
    saved, outs, refs = refs[:6], refs[6 : 6 + 4 * n_kept], refs[6 + 4 * n_kept :]
    held, refs = refs[:n_in], refs[n_in:]
    b0, b1, b2, b3, m0, m1, m2, m3, cos_ref, sin_ref = held[:10]
    kept = held[10:]
    qr_ref, qm_ref, kr_ref, v_ref, att_ref, lse_ref = refs[:6]
    max_s, sum_s, acc_s, mkey, mval, in_sems, out_sems = refs[6:]
    quarter, flag = place[0], place[1]
    rows_q = b0.shape[0]
    tiles = qr_ref.shape[0] // rows_q
    scale2 = LOG2E / math.sqrt(HEAD_DIM)
    half = HEAD_DIM // 2
    low = jnp.bfloat16

    for copy in fetch(given, held, in_sems):
        copy.wait()
    stack_memory((m0, m1, m2, m3), head, mkey, mval)
    for rel, block in enumerate((b0, b1, b2, b3)):
        rows = place_rows(quarter, rel, rows_q)
        turned = pl.ds(rel * rows_q, rows_q)
        cos_t, sin_t = cos_ref[turned, :], sin_ref[turned, :]
        query = block[:, :HEAD_DIM]
        qm_ref[rows, :] = query
        wide = query.astype(jnp.float32)
        qr_ref[rows, :] = (wide * cos_t + pltpu.roll(wide, half, 1) * sin_t).astype(low)
        wide = block[:, HEAD_DIM : 2 * HEAD_DIM].astype(jnp.float32)
        kr_ref[rows, :] = (wide * cos_t + pltpu.roll(wide, half, 1) * sin_t).astype(low)
        v_ref[rows, :] = block[:, 2 * HEAD_DIM :]
    leaving = fetch((qr_ref, qm_ref, kr_ref, v_ref), saved[:4], out_sems)

    def fold(scores, values):
        old_max = max_s[...]
        new_max = jnp.maximum(old_max, jnp.max(scores, 1, keepdims=True))
        spread = jnp.concatenate([new_max] * (scores.shape[1] // HEAD_DIM), 1)
        weights = jnp.exp2((scores - spread) * scale2)
        shrink = jnp.exp2((old_max - new_max) * scale2)
        sum_s[...] = sum_s[...] * shrink + jnp.sum(weights, 1, keepdims=True)
        acc_s[...] = acc_s[...] * shrink + dot_nn(weights.astype(low), values)
        max_s[...] = new_max

    def tile(index, carry):
        rows = pl.ds(pl.multiple_of(index * rows_q, rows_q), rows_q)
        query = qr_ref[rows, :]
        max_s[...] = jnp.full_like(max_s, NEG_FILL)
        sum_s[...] = jnp.zeros_like(sum_s)
        acc_s[...] = jnp.zeros_like(acc_s)

        def earlier(block, inner):
            keys = pl.ds(pl.multiple_of(block * rows_q, rows_q), rows_q)
            fold(dot_nt(query, kr_ref[keys, :]), v_ref[keys, :])
            return inner

        lax.fori_loop(0, index, earlier, 0)
        scores = dot_nt(query, kr_ref[rows, :])
        row_i = lax.broadcasted_iota(jnp.int32, scores.shape, 0)
        col_i = lax.broadcasted_iota(jnp.int32, scores.shape, 1)
        fold(jnp.where(col_i <= row_i, scores, NEG_FILL), v_ref[rows, :])

        @pl.when(flag > 0)
        def _():
            plain = qm_ref[rows, :]
            for at in range(0, mkey.shape[0], rows_q):
                fold(dot_nt(plain, mkey[at : at + rows_q, :]), mval[at : at + rows_q, :])

        total = sum_s[...]
        att_ref[rows, :] = (acc_s[...] / total).astype(low)
        lse = max_s[...] * scale2 + jnp.log(total) * LOG2E
        lse_ref[:, rows] = jnp.transpose(lse)[:8]
        return carry

    lax.fori_loop(0, tiles, tile, 0)

    for rel in range(4 * n_kept // max(n_kept, 1)):
        rows = place_rows(quarter, rel, rows_q)
        for at, source in enumerate((*kept, att_ref)):
            if n_kept:
                outs[rel][:, at * HEAD_DIM : (at + 1) * HEAD_DIM] = source[rows, :]
    for at, (source, target) in enumerate(((att_ref, saved[4]), (lse_ref, saved[5]))):
        copy = pltpu.make_async_copy(source, target, out_sems.at[4 + at])
        copy.start()
        leaving.append(copy)
    for copy in leaving:
        copy.wait()


def attend(head, place, blocks, memory, mem_rows, cos_t, sin_t, kept=()):
    rows_q = blocks[0].shape[0]
    length = cos_t.shape[0]
    low = jnp.bfloat16
    given = (*blocks, *memory, cos_t, sin_t, *kept)
    saved = [((length, HEAD_DIM), low)] * 5 + [((8, length), jnp.float32)]
    part = jax.ShapeDtypeStruct((rows_q, (len(kept) + 1) * HEAD_DIM), low)
    n_out = 4 if kept else 0
    return pl.pallas_call(
        functools.partial(attend_kernel, head, len(given)),
        out_shape=[jax.ShapeDtypeStruct(*kind) for kind in saved] + [part] * n_out,
        in_specs=[smem()] + hbm(len(given)),
        out_specs=hbm(6) + whole(n_out),
        scratch_shapes=[pltpu.VMEM(array.shape, array.dtype) for array in given]
        + [pltpu.VMEM(*kind) for kind in saved]
        + [pltpu.VMEM((rows_q, HEAD_DIM), jnp.float32)] * 3
        + [pltpu.VMEM((mem_rows, HEAD_DIM), low)] * 2
        + [pltpu.SemaphoreType.DMA((len(given),)), pltpu.SemaphoreType.DMA((6,))],
        compiler_params=pltpu.CompilerParams(vmem_limit_bytes=24 << 20),
        cost_estimate=pl.CostEstimate(flops=1, bytes_accessed=1, transcendentals=0),
        name="attend",
    )(place, *given)


def attend_back_kernel(head, n_in, *refs):
    place = refs[0]
    given, refs = refs[1 : 1 + n_in], refs[1 + n_in :]
    g0, g1, g2, g3 = refs[:4]
    held, refs = refs[4 : 4 + n_in], refs[4 + n_in :]
    qr_ref, qm_ref, kr_ref, v_ref, att_ref, lse_ref = held[:6]
    d0, d1, d2, d3, m0, m1, m2, m3, cos_ref, sin_ref = held[6:]
    datt, dkey, dval, dqr, dqm, grads, mkey, mval, in_sems = refs
    coming = fetch(given, held, in_sems)
    quarter, flag = place[0], place[1]
    rows_q = d0.shape[0]
    tiles = qr_ref.shape[0] // rows_q
    scale = 1.0 / math.sqrt(HEAD_DIM)
    scale2 = LOG2E * scale
    half = HEAD_DIM // 2
    low = jnp.bfloat16

    def unrotate(grad, index):
        turned = place_rows(quarter, index, rows_q)
        return grad * cos_ref[turned, :] - pltpu.roll(grad, half, 1) * sin_ref[turned, :]

    for copy in coming:
        copy.wait()
    stack_memory((m0, m1, m2, m3), head, mkey, mval)
    cols = slice(head * HEAD_DIM, (head + 1) * HEAD_DIM)
    for rel, block in enumerate((d0, d1, d2, d3)):
        datt[place_rows(quarter, rel, rows_q), :] = block[:, cols]
    dkey[...] = jnp.zeros_like(dkey)
    dval[...] = jnp.zeros_like(dval)

    def tile(index, carry):
        rows = pl.ds(pl.multiple_of(index * rows_q, rows_q), rows_q)
        query = qr_ref[rows, :]
        d_out = datt[rows, :]
        delta = jnp.sum(
            jnp.transpose(d_out.astype(jnp.float32) * att_ref[rows, :].astype(jnp.float32)),
            0,
            keepdims=True,
        )
        lse = lse_ref[0:1, rows]
        dqr[...] = jnp.zeros_like(dqr)
        dqm[...] = jnp.zeros_like(dqm)

        def block_grads(keys, values, queries, masked):
            power = dot_nt(keys, queries) * scale2 - lse
            if masked:
                key_i = lax.broadcasted_iota(jnp.int32, power.shape, 0)
                query_i = lax.broadcasted_iota(jnp.int32, power.shape, 1)
                power = jnp.where(key_i <= query_i, power, NEG_FILL)
            probs = jnp.exp2(power)
            d_scores = probs * (dot_nt(values, d_out) - delta)
            return probs.astype(low), d_scores.astype(low)

        def local(keys_at, masked):
            keys = kr_ref[keys_at, :]
            probs, d_scores = block_grads(keys, v_ref[keys_at, :], query, masked)
            dval[keys_at, :] += dot_nn(probs, d_out)
            dkey[keys_at, :] += dot_nn(d_scores, query)
            dqr[...] += dot_tn(d_scores, keys)

        def earlier(block, inner):
            local(pl.ds(pl.multiple_of(block * rows_q, rows_q), rows_q), False)
            return inner

        lax.fori_loop(0, index, earlier, 0)
        local(rows, True)

        @pl.when(flag > 0)
        def _():
            plain = qm_ref[rows, :]
            for at in range(0, mkey.shape[0], rows_q):
                keys = mkey[at : at + rows_q, :]
                _, d_scores = block_grads(keys, mval[at : at + rows_q, :], plain, False)
                dqm[...] += dot_tn(d_scores, keys)

        grads[rows, :HEAD_DIM] = ((unrotate(dqr[...], index) + dqm[...]) * scale).astype(low)
        return carry

    lax.fori_loop(0, tiles, tile, 0)
    for index in range(tiles):
        rows = pl.ds(index * rows_q, rows_q)
        grads[rows, HEAD_DIM : 2 * HEAD_DIM] = (unrotate(dkey[rows, :], index) * scale).astype(low)
        grads[rows, 2 * HEAD_DIM :] = dval[rows, :].astype(low)

    for rel, out in enumerate((g0, g1, g2, g3)):
        out[...] = grads[place_rows(quarter, rel, rows_q), :]


def attend_back(head, place, saved, d_blocks, memory, mem_rows, cos_t, sin_t):
    rows_q = d_blocks[0].shape[0]
    length = cos_t.shape[0]
    low, wide = jnp.bfloat16, jnp.float32
    given = (*saved, *d_blocks, *memory, cos_t, sin_t)
    return pl.pallas_call(
        functools.partial(attend_back_kernel, head, len(given)),
        out_shape=[jax.ShapeDtypeStruct((rows_q, 3 * HEAD_DIM), low)] * 4,
        in_specs=[smem()] + hbm(len(given)),
        out_specs=whole(4),
        scratch_shapes=[pltpu.VMEM(array.shape, array.dtype) for array in given]
        + [
            pltpu.VMEM((length, HEAD_DIM), low),
            pltpu.VMEM((length, HEAD_DIM), wide),
            pltpu.VMEM((length, HEAD_DIM), wide),
            pltpu.VMEM((rows_q, HEAD_DIM), wide),
            pltpu.VMEM((rows_q, HEAD_DIM), wide),
            pltpu.VMEM((length, 3 * HEAD_DIM), low),
            pltpu.VMEM((mem_rows, HEAD_DIM), low),
            pltpu.VMEM((mem_rows, HEAD_DIM), low),
            pltpu.SemaphoreType.DMA((len(given),)),
        ],
        compiler_params=pltpu.CompilerParams(vmem_limit_bytes=28 << 20),
        cost_estimate=pl.CostEstimate(flops=1, bytes_accessed=1, transcendentals=0),
        name="attend_back",
    )(place, *given)


def deal_kernel(n_heads, n_owners, wq, wk, wv, gains, out):
    at = 0
    for head in range(n_heads):
        for owner in range(n_owners):
            left = (owner * n_heads + head) * HEAD_DIM
            for weight in (wq, wk, wv):
                out[:, at : at + HEAD_DIM] = weight[:, left : left + HEAD_DIM]
                at += HEAD_DIM
    out[:, at:] = gains[...]


def deal(n_heads, n_owners, wq, wk, wv, gains):
    rows, width = wq.shape
    return pl.pallas_call(
        functools.partial(deal_kernel, n_heads, n_owners),
        out_shape=jax.ShapeDtypeStruct((rows, 3 * width + gains.shape[1]), wq.dtype),
        in_specs=whole(4),
        out_specs=whole(1)[0],
        compiler_params=pltpu.CompilerParams(vmem_limit_bytes=4 << 20),
        cost_estimate=pl.CostEstimate(flops=1, bytes_accessed=1, transcendentals=0),
        name="deal",
    )(wq, wk, wv, gains)


def join_kernel(turn, *refs):
    where, blocks, out, sems = refs[0], refs[1:-2], refs[-2], refs[-1]
    size = blocks[0].shape[1]
    targets = [
        out.at[:, pl.ds(pl.multiple_of((where[0] ^ flip) * size, HEAD_DIM), size)] for flip in turn
    ]
    for copy in fetch(blocks, targets, sems):
        copy.wait()


def join(where, turn, blocks):
    rows, size = blocks[0].shape
    return pl.pallas_call(
        functools.partial(join_kernel, turn),
        out_shape=jax.ShapeDtypeStruct((rows, len(blocks) * size), blocks[0].dtype),
        in_specs=[smem()] + hbm(len(blocks)),
        out_specs=hbm(1)[0],
        scratch_shapes=[pltpu.SemaphoreType.DMA((len(blocks),))],
        compiler_params=pltpu.CompilerParams(vmem_limit_bytes=4 << 20),
        cost_estimate=pl.CostEstimate(flops=1, bytes_accessed=1, transcendentals=0),
        name="join",
    )(where, *blocks)


def settle_kernel(rels, widths, chunks, *refs):
    where = refs[0]
    pieces = refs[1 : 1 + len(rels)]
    outs = refs[1 + len(rels) : 1 + len(rels) + len(widths)]
    sems = refs[-1]
    rows = pieces[0].shape[0]
    count = rows // chunks
    copies = []
    for piece, rel in zip(pieces, rels):
        rel, half = rel if isinstance(rel, tuple) else (rel, 0)
        hops = piece.shape[0] // count
        for hop in range(hops):
            chunk = (where[1] + chunks - half * hops - hop) % chunks
            start = pl.multiple_of((where[0] ^ rel) * rows + chunk * count, 16)
            left = 0
            for out, width in zip(outs, widths):
                copy = pltpu.make_async_copy(
                    piece.at[pl.ds(hop * count, count), pl.ds(left, width)],
                    out.at[pl.ds(start, count), :],
                    sems.at[len(copies)],
                )
                copy.start()
                copies.append(copy)
                left += width
    for copy in copies:
        copy.wait()


def settle(where, rels, pieces, widths, chunks):
    low = jnp.bfloat16
    total = sum(piece.shape[0] for piece in pieces)
    return pl.pallas_call(
        functools.partial(settle_kernel, rels, widths, chunks),
        out_shape=[jax.ShapeDtypeStruct((total, width), low) for width in widths],
        in_specs=[smem()] + hbm(len(pieces)),
        out_specs=hbm(len(widths)),
        scratch_shapes=[pltpu.SemaphoreType.DMA((len(pieces) * chunks * len(widths),))],
        compiler_params=pltpu.CompilerParams(vmem_limit_bytes=4 << 20),
        cost_estimate=pl.CostEstimate(flops=1, bytes_accessed=1, transcendentals=0),
        name="settle",
    )(where, *pieces)


def segment_pairs(n_doc, n_seq):
    places = [(d, z) for d in range(n_doc) for z in range(n_seq)]

    def route(target):
        pairs = [(d * n_seq + z, target(d, z)[0] * n_seq + target(d, z)[1]) for d, z in places]
        return [(source, goal) for source, goal in pairs if source != goal]

    def regroup(rel):
        def target(d, z):
            spot = z ^ rel
            return ((d & ~1) | (spot >> 1), 2 * (d & 1) + (spot & 1))

        return target

    routes = {
        "core": route(lambda d, z: (d ^ 1, z)),
        "x": route(lambda d, z: (d ^ 2, z)),
        "y": route(lambda d, z: (d ^ 4, z)),
        "xy": route(lambda d, z: (d ^ 6, z)),
        "z1": route(lambda d, z: (d, (z + 1) % n_seq)),
        "z2": route(lambda d, z: (d, (z + 2) % n_seq)),
        "z3": route(lambda d, z: (d, (z + 3) % n_seq)),
    }
    for rel in range(n_seq):
        routes["group", rel] = route(regroup(rel))
        routes["part", rel] = route(
            lambda d, z, rel=rel: (d ^ (rel >> 1), z ^ (rel & 1))
        )
    return routes


def later(values, *others):
    return lax.optimization_barrier((values, others))[0]


def on_pair(
    routes,
    tokens,
    w_query,
    w_key,
    w_value,
    w_out,
    w_gate,
    w_up,
    w_down,
    gain_attn,
    gain_ffn,
    cache_keys,
    cache_values,
    memory_flags,
    memory_source,
    positions,
    out_grad,
):
    low, wide = jnp.bfloat16, jnp.float32
    n_doc, n_seq = lax.axis_size("doc"), lax.axis_size("seq")
    d, z = lax.axis_index("doc"), lax.axis_index("seq")
    core, odd, pair, plane = d & 1, z & 1, z >> 1, d >> 1
    quarter = 2 * core + odd
    heads_at = 2 * odd + core
    turn = (0, 2, 1, 3)
    width = tokens.shape[2]
    ff_width = w_gate.shape[1]
    share = width // n_seq
    n_heads = share // HEAD_DIM
    where = jnp.stack([d, z]).astype(jnp.int32)
    mem_rows = 2 * n_seq * cache_keys.shape[1]

    def move(array, name):
        return lax.ppermute(array, LINE, routes[name])

    def to_group(array, rel=0):
        moved = move(array, ("group", rel))
        return moved if rel else jnp.where(pair == core, array, moved)

    def pick(array, index, axis=0):
        return lax.dynamic_index_in_dim(array, index, axis, keepdims=False)

    def plus(*terms):
        total = terms[0].astype(wide)
        for term in terms[1:]:
            total = total + term.astype(wide)
        return total.astype(low)

    def along_z(shard):
        return [shard] + [move(shard, f"z{hop}") for hop in range(1, n_seq)]

    def in_plane(block):
        return [block, move(block, "x"), move(block, "y"), move(block, "xy")]

    def swap_halves(pieces):
        cut = pieces[1].shape[0] // 2
        return [move(pieces[1][:cut], "y"), move(pieces[2][cut:], "x")]

    def other_core(pieces):
        return pieces + [move(piece, "core") for piece in pieces]

    rels = (0, 2, 4, 6, 1, 3, 5, 7)

    def part_for(array, rel, size):
        return lax.dynamic_slice_in_dim(array, (heads_at ^ turn[rel]) * size, size, 1)

    heads_where = heads_at.astype(jnp.int32).reshape(1)

    def spread(blocks):
        return join(heads_where, turn, blocks)

    def exchange(blocks):
        return [blocks[0]] + [move(blocks[rel], ("part", rel)) for rel in range(1, n_seq)]

    gains = jnp.concatenate([gain_attn[:, None], gain_ffn[:, None]], 1)
    gains = jnp.pad(gains, ((0, 0), (0, HEAD_DIM - 2)))
    lines = along_z(deal(n_heads, n_seq, w_query, w_key, w_value, gains))

    own_kv = jnp.concatenate([cache_keys[0], cache_values[0]], 1)
    two = jnp.stack([own_kv, move(own_kv, "x")])
    notes = jnp.concatenate([memory_flags, memory_source])
    notes_core, notes_y = later((move(notes, "core"), move(notes, "y")), two)
    flag = jnp.where(pair == core, notes[0], notes_core[0])
    source, source_y = notes[1], notes_y[1]
    place = jnp.stack([quarter, flag]).astype(jnp.int32)
    pos = [to_group(later(positions[0], two), rel) for rel in range(n_seq)]

    four = jnp.concatenate([two, move(two, "core")])

    def spot(src):
        return 2 * ((src ^ d) & 1) + (((src ^ d) >> 1) & 1)

    for_y = pick(four, spot(source_y))
    from_y = move(for_y, "y")
    block = jnp.concatenate(later(lines, for_y))
    rows = block.shape[0]
    projections = in_plane(block)
    lines_ab = along_z(later(jnp.concatenate([w_out, w_gate, w_up], 1), block))
    from_y = later(from_y, block)
    src_kv = jnp.where(((source ^ d) >> 2) == 0, pick(four, spot(source)), from_y)

    def heads_for(rel):
        to = z ^ rel
        at = (2 * (to & 1) + (to >> 1)) * share
        picked = [
            lax.dynamic_slice_in_dim(kv, side * width + at, share, 1)
            for kv in (own_kv, src_kv)
            for side in (0, 1)
        ]
        return jnp.concatenate(picked, 1)

    parts = [heads_for(rel) for rel in range(n_seq)]
    cos_h, sin_h = rotary_tables(jnp.concatenate(later(pos, parts)))
    cos_t = jnp.concatenate([cos_h, cos_h], -1)
    sin_t = jnp.concatenate([-sin_h, sin_h], -1)
    block_ab = jnp.concatenate(later(lines_ab, cos_t, sin_t))
    tok = to_group(later(tokens[0], block_ab))
    projections = later(projections, block_ab)
    pieces_ab = in_plane(later(block_ab, projections))[:3]
    *w_heads, gain_cols = settle(
        where,
        rels,
        other_core(projections),
        (3 * n_seq * HEAD_DIM,) * n_heads + (HEAD_DIM,),
        n_seq,
    )
    gain_a = gain_cols[:, 0].astype(wide)
    gain_f = gain_cols[:, 1].astype(wide)

    inputs = later(tok, w_heads).astype(wide)
    factor_one = rms_factor(inputs)
    normed_one = inputs * factor_one
    attn_in = (normed_one * gain_a).astype(low)

    def projected(head, *others):
        weight = later(w_heads[head], *others) if others else w_heads[head]
        qkv = dot_nn(attn_in, weight).astype(low)
        return [part_for(qkv, rel, 3 * HEAD_DIM) for rel in range(n_seq)]

    first = projected(0)
    first_own = first[0]
    first = exchange(first)
    parts = later(parts, first_own)
    memory = [to_group(part, rel) for rel, part in enumerate(parts)]
    second = projected(1, parts)
    second_own = second[0]
    second = exchange(second)
    pieces_ab = later(pieces_ab, second_own)
    far_ab = swap_halves(pieces_ab)
    first, memory = later((first, memory), pieces_ab)
    saved_0 = attend(0, place, first, memory, mem_rows, cos_t, sin_t)
    att_0 = saved_0[4]
    lines_c = along_z(later(w_down, att_0))
    *saved_1, o0, o1, o2, o3 = attend(
        1, place, later(second, att_0), memory, mem_rows, cos_t, sin_t, (att_0,)
    )
    block_c = jnp.stack(later(lines_c, o0))
    block_c = jnp.concatenate([pick(block_c, (z - at) % n_seq) for at in range(n_seq)])
    rows_c = block_c.shape[0]
    att = exchange(later([o0, o1, o2, o3], block_c))
    far_ab = later(far_ab, block_c)
    pieces_c = in_plane(later(block_c, far_ab))
    w_out_f, w_gate_f, w_up_f = settle(
        where,
        (0, 2, 4, 1, 3, 5, (6, 0), (6, 1), (7, 0), (7, 1)),
        other_core(later(pieces_ab, block_c)) + other_core(far_ab),
        (width, ff_width, ff_width),
        n_seq,
    )
    attn_low = spread(later(att, w_out_f))
    grad_y = to_group(later(out_grad[0], attn_low))
    resid_mid = inputs + dot_nn(attn_low, w_out_f)
    factor_two = rms_factor(resid_mid)
    normed_two = resid_mid * factor_two
    ffn_in = (normed_two * gain_f).astype(low)
    gate_act = dot_nn(ffn_in, w_gate_f)
    up_act = dot_nn(ffn_in, w_up_f)
    sig_gate = jax.nn.sigmoid(gate_act)
    silu_gate = gate_act * sig_gate
    hidden = (silu_gate * up_act).astype(low)
    grad_y, pieces_c = later((grad_y, pieces_c), hidden)

    def side(array, which, turned=True):
        return jnp.concatenate(
            [
                lax.dynamic_slice_in_dim(
                    array, (2 * (plane ^ rel if turned else rel) + which) * rows, rows, 1
                )
                for rel in range(n_doc // 2)
            ],
            1,
        )

    def met_in_plane(both):
        size = both.shape[0] // (n_doc // 2)
        parts = [both[rel * size : (rel + 1) * size] for rel in range(n_doc // 2)]
        return [parts[0]] + [move(parts[rel + 1], name) for rel, name in enumerate(("x", "y", "xy"))]

    def finish_by_hops(total):
        chunks = total.reshape(n_seq, -1, total.shape[1])
        return sum(
            (
                move(pick(chunks, (z + hop) % n_seq), f"z{hop}").astype(wide)
                for hop in range(1, n_seq)
            ),
            pick(chunks, z).astype(wide),
        )

    def kept(mine, array, met):
        return (dot_tn(mine, array) + met.astype(wide)).astype(low)

    pieces_c = other_core(pieces_c)
    grad_down = dot_tn(hidden, grad_y).astype(low).reshape(n_doc // 2, 2, rows_c, width)
    down_sent = pick(grad_down, 1 - core, 1)
    met_down = move(down_sent, "core")
    (w_down_f,) = settle(where, rels, later(pieces_c, down_sent), (width,), 1)
    d_hidden = dot_nt(grad_y, w_down_f)
    d_gate = (d_hidden * up_act * (sig_gate * (1.0 + gate_act * (1.0 - sig_gate)))).astype(low)
    d_up = (d_hidden * silu_gate).astype(low)
    d_ffn_in = dot_nt(d_gate, w_gate_f) + dot_nt(d_up, w_up_f)
    d_mid = grad_y.astype(wide) + norm_back(d_ffn_in * gain_f, normed_two, factor_two)
    d_branch = d_mid.astype(low)
    d_att = dot_nt(d_branch, w_out_f).astype(low)
    d_blocks = [part_for(d_att, rel, share) for rel in range(n_seq)]
    d_sent = d_blocks[0]
    d_blocks = exchange(d_blocks)
    met_down = later(met_down, d_sent)
    both_down = plus(pick(grad_down, core, 1), met_down)
    both_down = jnp.concatenate([pick(both_down, plane ^ rel) for rel in range(n_doc // 2)])
    total_down = met_in_plane(both_down)
    away, home = side(ffn_in, 1 - core), side(ffn_in, core)
    away_gate = dot_tn(later(away, both_down), d_gate).astype(low)
    met_gate = move(away_gate, "core")
    away_up = dot_tn(later(away, away_gate), d_up).astype(low)
    met_up = move(away_up, "core")
    d_blocks = later(d_blocks, away_up)
    g_0 = attend_back(0, place, saved_0, d_blocks, memory, mem_rows, cos_t, sin_t)
    d_set_0 = exchange(g_0)
    both_gate = kept(home, d_gate, later(met_gate, g_0))
    total_down = later(total_down, both_gate)
    total_gate = met_in_plane(later(both_gate, total_down))
    g_1 = attend_back(
        1, place, saved_1, later(d_blocks, both_gate, total_down), memory, mem_rows, cos_t, sin_t
    )
    g_1 = later(g_1, d_set_0)
    d_set_1 = exchange(g_1)

    away, home_in = side(attn_in, 1 - core), side(attn_in, core)
    d_qkv_0 = spread(later(d_set_0, g_1))
    away_0 = dot_tn(away, d_qkv_0).astype(low)
    met_0 = move(away_0, "core")
    both_up = kept(home, d_up, later(met_up, away_0))
    total_gate = later(total_gate, both_up)
    total_up = met_in_plane(later(both_up, total_gate))
    d_set_1 = later(d_set_1, both_up)
    d_qkv_1 = spread(d_set_1)
    away_1 = dot_tn(away, d_qkv_1).astype(low)
    met_1 = move(away_1, "core")
    out_down = finish_by_hops(plus(*later(total_down, away_1)))
    both_0 = kept(home_in, d_qkv_0, later(met_0, away_1))
    away_out = dot_tn(later(side(attn_low, 1 - core), both_0), d_branch).astype(low)
    met_out = move(away_out, "core")
    out_gate = finish_by_hops(plus(*later(total_gate, away_out)))
    both_1 = kept(home_in, d_qkv_1, later(met_1, away_out))
    layer_out = (resid_mid + dot_nn(later(hidden, both_1), w_down_f)).astype(low)
    both_out = kept(side(attn_low, core), later(d_branch, layer_out), later(met_out, layer_out))
    total_up = later(total_up, both_out)
    last = met_in_plane(later(jnp.concatenate([both_0, both_1, both_out], 1), total_up))
    d_attn_in = dot_nt(later(d_qkv_0, total_up), w_heads[0]) + dot_nt(
        later(d_qkv_1, total_up), w_heads[1]
    )
    layer_out = to_group(later(layer_out, total_up))
    grad_in = d_mid + norm_back(d_attn_in * gain_a, normed_one, factor_one)
    grad_in = grad_in.astype(low)
    grad_tokens = to_group(grad_in).astype(wide)
    out_up = finish_by_hops(plus(*later(total_up, grad_in)))
    both = finish_by_hops(plus(*later(last, grad_in)))
    out_out = both[:, 3 * width :]
    split = both[:, : 3 * width].reshape(-1, n_heads, n_seq, 3, HEAD_DIM)
    split = jnp.swapaxes(split, 1, 2)
    out_q, out_k, out_v = (split[:, :, :, which].reshape(-1, width) for which in range(3))

    def gain_grad(gain, pairs):
        total = sum(jnp.sum(weight.astype(wide) * grad, 1) for weight, grad in pairs)
        return total / gain.astype(wide)

    return (
        layer_out[None],
        grad_tokens[None],
        out_q,
        out_k,
        out_v,
        out_out,
        out_gate,
        out_up,
        out_down,
        gain_grad(gain_attn, ((w_query, out_q), (w_key, out_k), (w_value, out_v))),
        gain_grad(gain_ffn, ((w_gate, out_gate), (w_up, out_up))),
    )


def solution(mesh):
    in_specs = (
        P("doc", "seq", None),
        P(("doc", "seq"), None),
        P(("doc", "seq"), None),
        P(("doc", "seq"), None),
        P(("doc", "seq"), None),
        P(("doc", "seq"), None),
        P(("doc", "seq"), None),
        P(("doc", "seq"), None),
        P(("doc", "seq")),
        P(("doc", "seq")),
        P("doc", "seq", None),
        P("doc", "seq", None),
        P("doc"),
        P("doc"),
        P("doc", "seq"),
        P("doc", "seq", None),
    )
    out_specs = (
        P("doc", "seq", None),
        P("doc", "seq", None),
        P(("doc", "seq"), None),
        P(("doc", "seq"), None),
        P(("doc", "seq"), None),
        P(("doc", "seq"), None),
        P(("doc", "seq"), None),
        P(("doc", "seq"), None),
        P(("doc", "seq"), None),
        P(("doc", "seq")),
        P(("doc", "seq")),
    )
    n_doc, n_seq = mesh.shape["doc"], mesh.shape["seq"]
    step = on_device
    if (n_doc, n_seq) == (8, 4):
        step = functools.partial(on_pair, segment_pairs(n_doc, n_seq))
    return jax.shard_map(
        step, mesh=mesh, in_specs=in_specs, out_specs=out_specs, check_vma=False
    )
```

```python
import functools
import math

import jax
import jax.numpy as jnp
from jax import lax
from jax.experimental import pallas as pl
from jax.experimental.pallas import tpu as pltpu
from jax.sharding import PartitionSpec as P

HEADS = 8
HEAD_DIM = 128


EPS_NORM = 1e-05
NEG_FILL = -1e30


def rms_factor(values):
    return lax.rsqrt(jnp.mean(values * values, -1, keepdims=True) + EPS_NORM)


def rotary_tables(token_pos):
    half_dim = HEAD_DIM // 2
    frequency = jnp.exp(
        jnp.arange(half_dim, dtype=jnp.float32) * (-2.0 * math.log(10000.0) / HEAD_DIM)
    )
    angles = token_pos.astype(jnp.float32)[..., None] * frequency
    return (jnp.cos(angles), jnp.sin(angles))


def rotate(values, cos_vals, sin_vals):
    half_dim = values.shape[-1] // 2
    first_half = values[..., :half_dim]
    second_half = values[..., half_dim:]
    cos_b = cos_vals[..., None, :]
    sin_b = sin_vals[..., None, :]
    return jnp.concatenate(
        [first_half * cos_b - second_half * sin_b, second_half * cos_b + first_half * sin_b], -1
    )


def rotate_back(grads, cos_vals, sin_vals):
    half_dim = grads.shape[-1] // 2
    first_half = grads[..., :half_dim]
    second_half = grads[..., half_dim:]
    cos_b = cos_vals[..., None, :]
    sin_b = sin_vals[..., None, :]
    return jnp.concatenate(
        [first_half * cos_b + second_half * sin_b, second_half * cos_b - first_half * sin_b], -1
    )


def online_step(fold_state, scores, allowed, value_heads):
    row_max, row_sum, weighted = fold_state
    masked = jnp.where(allowed, scores, NEG_FILL)
    new_max = jnp.maximum(row_max, jnp.max(masked, -1))
    weights_p = jnp.where(allowed, jnp.exp(scores - new_max[..., None]), 0.0)
    rescale = jnp.exp(row_max - new_max)
    row_sum = row_sum * rescale + jnp.sum(weights_p, -1)
    weighted = weighted * jnp.transpose(rescale, (0, 2, 1))[..., None] + jnp.einsum(
        "shqk,skhd->sqhd",
        weights_p.astype(jnp.bfloat16),
        value_heads,
        preferred_element_type=jnp.float32,
    )
    return (new_max, row_sum, weighted)


def norm_back(d_normed, normed, factor):
    return factor * (d_normed - normed * jnp.mean(d_normed * normed, -1, keepdims=True))


def on_device(
    tokens,
    w_query,
    w_key,
    w_value,
    w_out,
    w_gate,
    w_up,
    w_down,
    gain_attn,
    gain_ffn,
    cache_keys,
    cache_values,
    memory_flags,
    memory_source,
    positions,
    out_grad,
):
    fwd_weights = (
        lax.all_gather(w_query, ("doc", "seq"), axis=0, tiled=True),
        lax.all_gather(w_key, ("doc", "seq"), axis=0, tiled=True),
        lax.all_gather(w_value, ("doc", "seq"), axis=0, tiled=True),
        lax.all_gather(w_out, ("doc", "seq"), axis=0, tiled=True),
        lax.all_gather(w_gate, ("doc", "seq"), axis=0, tiled=True),
        lax.all_gather(w_up, ("doc", "seq"), axis=0, tiled=True),
        lax.all_gather(w_down, ("doc", "seq"), axis=0, tiled=True),
        lax.all_gather(gain_attn, ("doc", "seq"), axis=0, tiled=True),
        lax.all_gather(gain_ffn, ("doc", "seq"), axis=0, tiled=True),
    )
    seg_count, tok_local, model_width = tokens.shape
    ff_width = w_gate.shape[1]
    flat_rows = seg_count * tok_local
    score_scale = 1.0 / math.sqrt(HEAD_DIM)
    total_len = tok_local * lax.axis_size("seq")
    state_shape = (seg_count, HEADS, tok_local)
    head_shape = (seg_count, tok_local, HEADS, HEAD_DIM)
    inputs = tokens.astype(jnp.float32)
    factor_one = rms_factor(inputs)
    normed_one = inputs * factor_one
    attn_in = (normed_one * fwd_weights[7].astype(jnp.float32)).astype(jnp.bfloat16)
    query_f = jnp.dot(attn_in, fwd_weights[0], preferred_element_type=jnp.float32)
    keys_f = jnp.dot(attn_in, fwd_weights[1], preferred_element_type=jnp.float32)
    v_low = jnp.dot(attn_in, fwd_weights[2], preferred_element_type=jnp.float32).astype(
        jnp.bfloat16
    )
    cos_vals, sin_vals = rotary_tables(positions)
    q_heads = query_f.reshape(head_shape)
    q_rot = rotate(q_heads, cos_vals, sin_vals).astype(jnp.bfloat16)
    q_mem = q_heads.astype(jnp.bfloat16)
    k_rot = (
        rotate(keys_f.reshape(head_shape), cos_vals, sin_vals)
        .astype(jnp.bfloat16)
        .reshape(seg_count, tok_local, model_width)
    )
    query_rows = lax.axis_index("seq") * tok_local + jnp.arange(tok_local, dtype=jnp.int32)
    initial = (
        jnp.full(state_shape, NEG_FILL, jnp.float32),
        jnp.zeros(state_shape, jnp.float32),
        jnp.zeros(head_shape, jnp.float32),
    )
    key_part = lax.all_gather(k_rot, "seq", axis=1, tiled=True)
    value_part = lax.all_gather(v_low, "seq", axis=1, tiled=True)
    key_span = key_part.shape[1]
    key_heads = key_part.reshape(seg_count, key_span, HEADS, HEAD_DIM)
    scores = (
        jnp.einsum("sqhd,skhd->shqk", q_rot, key_heads, preferred_element_type=jnp.float32)
        * score_scale
    )
    key_cols = jnp.arange(key_span, dtype=jnp.int32)
    allowed = (key_cols[None, :] <= query_rows[:, None])[None, None]
    fold_state = online_step(
        initial, scores, allowed, value_part.reshape(seg_count, key_span, HEADS, HEAD_DIM)
    )
    every_keys, every_values = (
        lax.all_gather(cache_keys, "doc", axis=0, tiled=True),
        lax.all_gather(cache_values, "doc", axis=0, tiled=True),
    )
    mem_keys = jnp.concatenate([cache_keys, jnp.take(every_keys, memory_source, axis=0)], 1)
    mem_values = jnp.concatenate([cache_values, jnp.take(every_values, memory_source, axis=0)], 1)
    flag_on = (memory_flags > 0)[:, None, None, None]
    key_part = lax.all_gather(mem_keys, "seq", axis=1, tiled=True)
    value_part = lax.all_gather(mem_values, "seq", axis=1, tiled=True)
    key_span = key_part.shape[1]
    key_heads = key_part.reshape(seg_count, key_span, HEADS, HEAD_DIM)
    scores = (
        jnp.einsum("sqhd,skhd->shqk", q_mem, key_heads, preferred_element_type=jnp.float32)
        * score_scale
    )
    row_max, row_sum, weighted = online_step(
        fold_state, scores, flag_on, value_part.reshape(seg_count, key_span, HEADS, HEAD_DIM)
    )
    log_total = row_max + jnp.log(row_sum)
    attended = weighted / jnp.transpose(row_sum, (0, 2, 1))[..., None]
    attn_low = attended.reshape(flat_rows, model_width).astype(jnp.bfloat16)
    resid_mid = inputs.reshape(flat_rows, model_width) + jnp.dot(
        attn_low, fwd_weights[3], preferred_element_type=jnp.float32
    )
    factor_two = rms_factor(resid_mid)
    normed_two = resid_mid * factor_two
    ffn_in = (normed_two * fwd_weights[8].astype(jnp.float32)).astype(jnp.bfloat16)
    gate_act = jnp.dot(ffn_in, fwd_weights[4], preferred_element_type=jnp.float32)
    up_act = jnp.dot(ffn_in, fwd_weights[5], preferred_element_type=jnp.float32)
    sig_gate = jax.nn.sigmoid(gate_act)
    silu_gate = jax.nn.silu(gate_act)
    hidden = (silu_gate * up_act).astype(jnp.bfloat16)
    result = (
        resid_mid + jnp.dot(hidden, fwd_weights[6], preferred_element_type=jnp.float32)
    ).astype(jnp.bfloat16)
    back_weights = (
        lax.all_gather(w_query, ("doc", "seq"), axis=0, tiled=True),
        lax.all_gather(w_key, ("doc", "seq"), axis=0, tiled=True),
        lax.all_gather(w_value, ("doc", "seq"), axis=0, tiled=True),
        lax.all_gather(w_out, ("doc", "seq"), axis=0, tiled=True),
        lax.all_gather(w_gate, ("doc", "seq"), axis=0, tiled=True),
        lax.all_gather(w_up, ("doc", "seq"), axis=0, tiled=True),
        lax.all_gather(w_down, ("doc", "seq"), axis=0, tiled=True),
        lax.all_gather(gain_attn, ("doc", "seq"), axis=0, tiled=True),
        lax.all_gather(gain_ffn, ("doc", "seq"), axis=0, tiled=True),
    )
    grad_y = out_grad.reshape(flat_rows, model_width)
    d_hidden = jnp.einsum("td,fd->tf", grad_y, back_weights[6], preferred_element_type=jnp.float32)
    d_gate = (d_hidden * up_act * (sig_gate * (1.0 + gate_act * (1.0 - sig_gate)))).astype(
        jnp.bfloat16
    )
    d_up = (d_hidden * silu_gate).astype(jnp.bfloat16)
    d_ffn_in = jnp.einsum(
        "tf,df->td", d_gate, back_weights[4], preferred_element_type=jnp.float32
    ) + jnp.einsum("tf,df->td", d_up, back_weights[5], preferred_element_type=jnp.float32)
    g_gain_ffn = jnp.sum(d_ffn_in * normed_two, 0)
    d_mid = grad_y.astype(jnp.float32) + norm_back(
        d_ffn_in * back_weights[8].astype(jnp.float32), normed_two, factor_two
    )
    d_branch = d_mid.astype(jnp.bfloat16)
    d_att = (
        jnp.einsum("te,de->td", d_branch, back_weights[3], preferred_element_type=jnp.float32)
        .astype(jnp.bfloat16)
        .reshape(head_shape)
    )
    delta_rows = jnp.transpose(jnp.sum(d_att.astype(jnp.float32) * attended, -1), (0, 2, 1))
    gathered_keys, gathered_values = (
        lax.all_gather(k_rot, "seq", axis=1, tiled=True),
        lax.all_gather(v_low, "seq", axis=1, tiled=True),
    )
    block_len = min(512, total_len)
    n_blocks = total_len // block_len
    key_blocks = jnp.transpose(
        gathered_keys.reshape(seg_count, n_blocks, block_len, HEADS, HEAD_DIM), (1, 0, 2, 3, 4)
    )
    value_blocks = jnp.transpose(
        gathered_values.reshape(seg_count, n_blocks, block_len, HEADS, HEAD_DIM), (1, 0, 2, 3, 4)
    )

    def block_grads(key_heads, value_heads, block_num):
        scores = (
            jnp.einsum("sqhd,skhd->shqk", q_rot, key_heads, preferred_element_type=jnp.float32)
            * score_scale
        )
        key_cols = block_num * block_len + jnp.arange(block_len, dtype=jnp.int32)
        allowed = (key_cols[None, :] <= query_rows[:, None])[None, None]
        probabilities = jnp.where(allowed, jnp.exp(scores - log_total[..., None]), 0.0)
        d_probs = jnp.einsum(
            "sqhd,skhd->shqk", d_att, value_heads, preferred_element_type=jnp.float32
        )
        d_scores = (probabilities * (d_probs - delta_rows[..., None])).astype(jnp.bfloat16)
        return (probabilities, d_scores)

    def query_step(d_query_acc, block_inputs):
        key_heads, value_heads, block_num = block_inputs
        probabilities, d_scores = block_grads(key_heads, value_heads, block_num)
        return (
            d_query_acc
            + jnp.einsum(
                "shqk,skhd->sqhd", d_scores, key_heads, preferred_element_type=jnp.float32
            ),
            None,
        )

    d_qrot, unused_out = lax.scan(
        query_step,
        jnp.zeros(head_shape, jnp.float32),
        (key_blocks, value_blocks, jnp.arange(n_blocks, dtype=jnp.int32)),
    )
    own_keys = k_rot.reshape(head_shape)
    own_values = v_low.reshape(head_shape)
    lse_rows = jnp.transpose(log_total, (0, 2, 1))
    delta_tok = jnp.transpose(delta_rows, (0, 2, 1))
    q_part = lax.all_gather(q_rot, "seq", axis=1, tiled=True)
    datt_part = lax.all_gather(d_att, "seq", axis=1, tiled=True)
    lse_part = lax.all_gather(lse_rows.astype(jnp.bfloat16), "seq", axis=1, tiled=True).astype(
        jnp.float32
    )
    delta_part = lax.all_gather(delta_tok.astype(jnp.bfloat16), "seq", axis=1, tiled=True).astype(
        jnp.float32
    )
    row_span = q_part.shape[1]
    scores = (
        jnp.einsum("sqhd,skhd->shqk", q_part, own_keys, preferred_element_type=jnp.float32)
        * score_scale
    )
    visit_rows = jnp.arange(row_span, dtype=jnp.int32)
    allowed = (query_rows[None, :] <= visit_rows[:, None])[None, None]
    lse_heads = jnp.transpose(lse_part, (0, 2, 1))
    delta_heads = jnp.transpose(delta_part, (0, 2, 1))
    probabilities = jnp.where(allowed, jnp.exp(scores - lse_heads[..., None]), 0.0)
    d_probs = jnp.einsum(
        "sqhd,skhd->shqk", datt_part, own_values, preferred_element_type=jnp.float32
    )
    d_scores = (probabilities * (d_probs - delta_heads[..., None])).astype(jnp.bfloat16)
    key_acc = jnp.einsum("shqk,sqhd->skhd", d_scores, q_part, preferred_element_type=jnp.float32)
    value_acc = jnp.einsum(
        "shqk,sqhd->skhd",
        probabilities.astype(jnp.bfloat16),
        datt_part,
        preferred_element_type=jnp.float32,
    )
    key_acc, value_acc = (key_acc, value_acc)
    key_sum = key_acc.reshape(seg_count, tok_local, model_width)
    value_sum = value_acc.reshape(seg_count, tok_local, model_width)
    key_part = lax.all_gather(mem_keys, "seq", axis=1, tiled=True)
    value_part = lax.all_gather(mem_values, "seq", axis=1, tiled=True)
    key_span = key_part.shape[1]
    key_heads = key_part.reshape(seg_count, key_span, HEADS, HEAD_DIM)
    value_heads = value_part.reshape(seg_count, key_span, HEADS, HEAD_DIM)
    scores = (
        jnp.einsum("sqhd,skhd->shqk", q_mem, key_heads, preferred_element_type=jnp.float32)
        * score_scale
    )
    probabilities = jnp.where(flag_on, jnp.exp(scores - log_total[..., None]), 0.0)
    d_probs = jnp.einsum("sqhd,skhd->shqk", d_att, value_heads, preferred_element_type=jnp.float32)
    d_scores = (probabilities * (d_probs - delta_rows[..., None])).astype(jnp.bfloat16)
    d_qmem = jnp.einsum("shqk,skhd->sqhd", d_scores, key_heads, preferred_element_type=jnp.float32)
    d_query = (
        ((rotate_back(d_qrot, cos_vals, sin_vals) + d_qmem) * score_scale)
        .astype(jnp.bfloat16)
        .reshape(flat_rows, model_width)
    )
    d_key = (
        (rotate_back(key_sum.reshape(head_shape), cos_vals, sin_vals) * score_scale)
        .astype(jnp.bfloat16)
        .reshape(flat_rows, model_width)
    )
    d_value = value_sum.astype(jnp.bfloat16).reshape(flat_rows, model_width)
    attn_in_flat = attn_in.reshape(flat_rows, model_width)
    d_attn_in = jnp.einsum(
        "te,de->td", d_query, back_weights[0], preferred_element_type=jnp.float32
    )
    d_attn_in = d_attn_in + jnp.einsum(
        "te,de->td", d_key, back_weights[1], preferred_element_type=jnp.float32
    )
    d_attn_in = d_attn_in + jnp.einsum(
        "te,de->td", d_value, back_weights[2], preferred_element_type=jnp.float32
    )
    normed_flat = normed_one.reshape(flat_rows, model_width)
    g_gain_attn = jnp.sum(d_attn_in * normed_flat, 0)
    grad_in = d_mid + norm_back(
        d_attn_in * back_weights[7].astype(jnp.float32),
        normed_flat,
        factor_one.reshape(flat_rows, 1),
    )
    grad_tokens = grad_in.reshape(seg_count, tok_local, model_width)
    gate_part = jnp.einsum("td,tf->df", ffn_in, d_gate, preferred_element_type=jnp.float32)
    up_part = jnp.einsum("td,tf->df", ffn_in, d_up, preferred_element_type=jnp.float32)
    both_parts = lax.psum_scatter(
        jnp.concatenate([gate_part, up_part], 1), ("doc", "seq"), scatter_dimension=0, tiled=True
    )
    down_part = lax.psum_scatter(
        jnp.einsum("tf,td->fd", hidden, grad_y, preferred_element_type=jnp.float32),
        ("doc", "seq"),
        scatter_dimension=0,
        tiled=True,
    )
    query_part = jnp.einsum("td,te->de", attn_in_flat, d_query, preferred_element_type=jnp.float32)
    key_part = jnp.einsum("td,te->de", attn_in_flat, d_key, preferred_element_type=jnp.float32)
    value_part = jnp.einsum("td,te->de", attn_in_flat, d_value, preferred_element_type=jnp.float32)
    out_part = jnp.einsum("td,te->de", attn_low, d_branch, preferred_element_type=jnp.float32)
    attn_sums = lax.psum_scatter(
        jnp.concatenate([query_part, key_part, value_part, out_part], 1),
        ("doc", "seq"),
        scatter_dimension=0,
        tiled=True,
    )
    gain_attn_sum, gain_ffn_sum = (
        lax.psum_scatter(g_gain_attn, ("doc", "seq"), scatter_dimension=0, tiled=True),
        lax.psum_scatter(g_gain_ffn, ("doc", "seq"), scatter_dimension=0, tiled=True),
    )
    layer_out = result.reshape(seg_count, tok_local, model_width)
    return (
        layer_out,
        grad_tokens,
        attn_sums[:, :model_width],
        attn_sums[:, model_width : 2 * model_width],
        attn_sums[:, 2 * model_width : 3 * model_width],
        attn_sums[:, 3 * model_width :],
        both_parts[:, :ff_width],
        both_parts[:, ff_width:],
        down_part,
        gain_attn_sum,
        gain_ffn_sum,
    )


LINE = ("doc", "seq")
MXU = dict(preferred_element_type=jnp.float32)
LOG2E = 1.4426950408889634


def dot_nt(left, right):
    return lax.dot_general(left, right, (((1,), (1,)), ((), ())), **MXU)


def dot_tn(left, right):
    return lax.dot_general(left, right, (((0,), (0,)), ((), ())), **MXU)


def dot_nn(left, right):
    return jnp.dot(left, right, **MXU)


def whole(count):
    return [pl.BlockSpec(memory_space=pltpu.VMEM)] * count


def hbm(count):
    return [pl.BlockSpec(memory_space=pl.ANY)] * count


def smem():
    return pl.BlockSpec(memory_space=pltpu.SMEM)


def place_rows(quarter, rel, rows_q):
    return pl.ds(pl.multiple_of((quarter ^ rel) * rows_q, rows_q), rows_q)


def stack_memory(pieces, head, keys_ref, vals_ref):
    count = keys_ref.shape[0] // (2 * len(pieces))
    span = pieces[0].shape[1] // 4
    at = 0
    for piece in pieces:
        for part in (0, 2):
            left = part * span + head * HEAD_DIM
            keys_ref[at : at + count, :] = piece[:count, left : left + HEAD_DIM]
            vals_ref[at : at + count, :] = piece[:count, left + span : left + span + HEAD_DIM]
            at += count


def fetch(sources, targets, sems):
    copies = [
        pltpu.make_async_copy(source, target, sems.at[index])
        for index, (source, target) in enumerate(zip(sources, targets))
    ]
    for copy in copies:
        copy.start()
    return copies


def attend_kernel(head, n_in, n_first, *refs):
    place = refs[0]
    given, refs = refs[1 : 1 + n_in], refs[1 + n_in + n_first :]
    n_kept = n_in - 10
    saved, outs, refs = refs[:6], refs[6 : 6 + 4 * n_kept], refs[6 + 4 * n_kept :]
    held, refs = refs[:n_in], refs[n_in:]
    b0, b1, b2, b3, m0, m1, m2, m3, cos_ref, sin_ref = held[:10]
    kept = held[10:]
    qr_ref, qm_ref, kr_ref, v_ref, att_ref, lse_ref = refs[:6]
    max_s, sum_s, acc_s, mkey, mval, in_sems, out_sems = refs[6:]
    quarter, flag = place[0], place[1]
    rows_q = b0.shape[0]
    tiles = qr_ref.shape[0] // rows_q
    scale2 = LOG2E / math.sqrt(HEAD_DIM)
    half = HEAD_DIM // 2
    low = jnp.bfloat16

    for copy in fetch(given, held, in_sems):
        copy.wait()
    stack_memory((m0, m1, m2, m3), head, mkey, mval)
    for rel, block in enumerate((b0, b1, b2, b3)):
        rows = place_rows(quarter, rel, rows_q)
        turned = pl.ds(rel * rows_q, rows_q)
        cos_t, sin_t = cos_ref[turned, :], sin_ref[turned, :]
        query = block[:, :HEAD_DIM]
        qm_ref[rows, :] = query
        wide = query.astype(jnp.float32)
        qr_ref[rows, :] = (wide * cos_t + pltpu.roll(wide, half, 1) * sin_t).astype(low)
        wide = block[:, HEAD_DIM : 2 * HEAD_DIM].astype(jnp.float32)
        kr_ref[rows, :] = (wide * cos_t + pltpu.roll(wide, half, 1) * sin_t).astype(low)
        v_ref[rows, :] = block[:, 2 * HEAD_DIM :]
    leaving = fetch((qr_ref, qm_ref, kr_ref, v_ref), saved[:4], out_sems)

    def fold(scores, values):
        old_max = max_s[...]
        new_max = jnp.maximum(old_max, jnp.max(scores, 1, keepdims=True))
        spread = jnp.concatenate([new_max] * (scores.shape[1] // HEAD_DIM), 1)
        weights = jnp.exp2((scores - spread) * scale2)
        shrink = jnp.exp2((old_max - new_max) * scale2)
        sum_s[...] = sum_s[...] * shrink + jnp.sum(weights, 1, keepdims=True)
        acc_s[...] = acc_s[...] * shrink + dot_nn(weights.astype(low), values)
        max_s[...] = new_max

    def tile(index, carry):
        rows = pl.ds(pl.multiple_of(index * rows_q, rows_q), rows_q)
        query = qr_ref[rows, :]
        max_s[...] = jnp.full_like(max_s, NEG_FILL)
        sum_s[...] = jnp.zeros_like(sum_s)
        acc_s[...] = jnp.zeros_like(acc_s)

        def earlier(block, inner):
            keys = pl.ds(pl.multiple_of(block * rows_q, rows_q), rows_q)
            fold(dot_nt(query, kr_ref[keys, :]), v_ref[keys, :])
            return inner

        lax.fori_loop(0, index, earlier, 0)
        scores = dot_nt(query, kr_ref[rows, :])
        row_i = lax.broadcasted_iota(jnp.int32, scores.shape, 0)
        col_i = lax.broadcasted_iota(jnp.int32, scores.shape, 1)
        fold(jnp.where(col_i <= row_i, scores, NEG_FILL), v_ref[rows, :])

        @pl.when(flag > 0)
        def _():
            plain = qm_ref[rows, :]
            for at in range(0, mkey.shape[0], rows_q):
                fold(dot_nt(plain, mkey[at : at + rows_q, :]), mval[at : at + rows_q, :])

        total = sum_s[...]
        att_ref[rows, :] = (acc_s[...] / total).astype(low)
        lse = max_s[...] * scale2 + jnp.log(total) * LOG2E
        lse_ref[:, rows] = jnp.transpose(lse)[:8]
        return carry

    lax.fori_loop(0, tiles, tile, 0)

    for rel in range(4 * n_kept // max(n_kept, 1)):
        rows = place_rows(quarter, rel, rows_q)
        for at, source in enumerate((*kept, att_ref)):
            if n_kept:
                outs[rel][:, at * HEAD_DIM : (at + 1) * HEAD_DIM] = source[rows, :]
    for at, (source, target) in enumerate(((att_ref, saved[4]), (lse_ref, saved[5]))):
        copy = pltpu.make_async_copy(source, target, out_sems.at[4 + at])
        copy.start()
        leaving.append(copy)
    for copy in leaving:
        copy.wait()


def attend(head, place, blocks, memory, mem_rows, cos_t, sin_t, kept=(), first=()):
    rows_q = blocks[0].shape[0]
    length = cos_t.shape[0]
    low = jnp.bfloat16
    given = (*blocks, *memory, cos_t, sin_t, *kept)
    saved = [((length, HEAD_DIM), low)] * 5 + [((8, length), jnp.float32)]
    part = jax.ShapeDtypeStruct((rows_q, (len(kept) + 1) * HEAD_DIM), low)
    n_out = 4 if kept else 0
    return pl.pallas_call(
        functools.partial(attend_kernel, head, len(given), len(first)),
        out_shape=[jax.ShapeDtypeStruct(*kind) for kind in saved] + [part] * n_out,
        in_specs=[smem()] + hbm(len(given) + len(first)),
        out_specs=hbm(6) + whole(n_out),
        scratch_shapes=[pltpu.VMEM(array.shape, array.dtype) for array in given]
        + [pltpu.VMEM(*kind) for kind in saved]
        + [pltpu.VMEM((rows_q, HEAD_DIM), jnp.float32)] * 3
        + [pltpu.VMEM((mem_rows, HEAD_DIM), low)] * 2
        + [pltpu.SemaphoreType.DMA((len(given),)), pltpu.SemaphoreType.DMA((6,))],
        compiler_params=pltpu.CompilerParams(vmem_limit_bytes=24 << 20),
        cost_estimate=pl.CostEstimate(flops=1, bytes_accessed=1, transcendentals=0),
        name="attend",
    )(place, *given, *first)


def attend_back_kernel(head, n_in, n_first, *refs):
    place = refs[0]
    given, refs = refs[1 : 1 + n_in], refs[1 + n_in + n_first :]
    g0, g1, g2, g3 = refs[:4]
    held, refs = refs[4 : 4 + n_in], refs[4 + n_in :]
    qr_ref, qm_ref, kr_ref, v_ref, att_ref, lse_ref = held[:6]
    d0, d1, d2, d3, m0, m1, m2, m3, cos_ref, sin_ref = held[6:]
    datt, dkey, dval, dqr, dqm, grads, mkey, mval, in_sems = refs
    coming = fetch(given, held, in_sems)
    quarter, flag = place[0], place[1]
    rows_q = d0.shape[0]
    tiles = qr_ref.shape[0] // rows_q
    scale = 1.0 / math.sqrt(HEAD_DIM)
    scale2 = LOG2E * scale
    half = HEAD_DIM // 2
    low = jnp.bfloat16

    def unrotate(grad, index):
        turned = place_rows(quarter, index, rows_q)
        return grad * cos_ref[turned, :] - pltpu.roll(grad, half, 1) * sin_ref[turned, :]

    for copy in coming:
        copy.wait()
    stack_memory((m0, m1, m2, m3), head, mkey, mval)
    cols = slice(head * HEAD_DIM, (head + 1) * HEAD_DIM)
    for rel, block in enumerate((d0, d1, d2, d3)):
        datt[place_rows(quarter, rel, rows_q), :] = block[:, cols]
    dkey[...] = jnp.zeros_like(dkey)
    dval[...] = jnp.zeros_like(dval)

    def tile(index, carry):
        rows = pl.ds(pl.multiple_of(index * rows_q, rows_q), rows_q)
        query = qr_ref[rows, :]
        d_out = datt[rows, :]
        delta = jnp.sum(
            jnp.transpose(d_out.astype(jnp.float32) * att_ref[rows, :].astype(jnp.float32)),
            0,
            keepdims=True,
        )
        lse = lse_ref[0:1, rows]
        dqr[...] = jnp.zeros_like(dqr)
        dqm[...] = jnp.zeros_like(dqm)

        def block_grads(keys, values, queries, masked):
            power = dot_nt(keys, queries) * scale2 - lse
            if masked:
                key_i = lax.broadcasted_iota(jnp.int32, power.shape, 0)
                query_i = lax.broadcasted_iota(jnp.int32, power.shape, 1)
                power = jnp.where(key_i <= query_i, power, NEG_FILL)
            probs = jnp.exp2(power)
            d_scores = probs * (dot_nt(values, d_out) - delta)
            return probs.astype(low), d_scores.astype(low)

        def local(keys_at, masked):
            keys = kr_ref[keys_at, :]
            probs, d_scores = block_grads(keys, v_ref[keys_at, :], query, masked)
            dval[keys_at, :] += dot_nn(probs, d_out)
            dkey[keys_at, :] += dot_nn(d_scores, query)
            dqr[...] += dot_tn(d_scores, keys)

        def earlier(block, inner):
            local(pl.ds(pl.multiple_of(block * rows_q, rows_q), rows_q), False)
            return inner

        lax.fori_loop(0, index, earlier, 0)
        local(rows, True)

        @pl.when(flag > 0)
        def _():
            plain = qm_ref[rows, :]
            for at in range(0, mkey.shape[0], rows_q):
                keys = mkey[at : at + rows_q, :]
                _, d_scores = block_grads(keys, mval[at : at + rows_q, :], plain, False)
                dqm[...] += dot_tn(d_scores, keys)

        grads[rows, :HEAD_DIM] = ((unrotate(dqr[...], index) + dqm[...]) * scale).astype(low)
        return carry

    lax.fori_loop(0, tiles, tile, 0)
    for index in range(tiles):
        rows = pl.ds(index * rows_q, rows_q)
        grads[rows, HEAD_DIM : 2 * HEAD_DIM] = (unrotate(dkey[rows, :], index) * scale).astype(low)
        grads[rows, 2 * HEAD_DIM :] = dval[rows, :].astype(low)

    for rel, out in enumerate((g0, g1, g2, g3)):
        out[...] = grads[place_rows(quarter, rel, rows_q), :]


def attend_back(head, place, saved, d_blocks, memory, mem_rows, cos_t, sin_t, first=()):
    rows_q = d_blocks[0].shape[0]
    length = cos_t.shape[0]
    low, wide = jnp.bfloat16, jnp.float32
    given = (*saved, *d_blocks, *memory, cos_t, sin_t)
    return pl.pallas_call(
        functools.partial(attend_back_kernel, head, len(given), len(first)),
        out_shape=[jax.ShapeDtypeStruct((rows_q, 3 * HEAD_DIM), low)] * 4,
        in_specs=[smem()] + hbm(len(given) + len(first)),
        out_specs=whole(4),
        scratch_shapes=[pltpu.VMEM(array.shape, array.dtype) for array in given]
        + [
            pltpu.VMEM((length, HEAD_DIM), low),
            pltpu.VMEM((length, HEAD_DIM), wide),
            pltpu.VMEM((length, HEAD_DIM), wide),
            pltpu.VMEM((rows_q, HEAD_DIM), wide),
            pltpu.VMEM((rows_q, HEAD_DIM), wide),
            pltpu.VMEM((length, 3 * HEAD_DIM), low),
            pltpu.VMEM((mem_rows, HEAD_DIM), low),
            pltpu.VMEM((mem_rows, HEAD_DIM), low),
            pltpu.SemaphoreType.DMA((len(given),)),
        ],
        compiler_params=pltpu.CompilerParams(vmem_limit_bytes=28 << 20),
        cost_estimate=pl.CostEstimate(flops=1, bytes_accessed=1, transcendentals=0),
        name="attend_back",
    )(place, *given, *first)


def deal_kernel(n_heads, n_owners, wq, wk, wv, gains, out):
    at = 0
    for head in range(n_heads):
        for owner in range(n_owners):
            left = (owner * n_heads + head) * HEAD_DIM
            for weight in (wq, wk, wv):
                out[:, at : at + HEAD_DIM] = weight[:, left : left + HEAD_DIM]
                at += HEAD_DIM
    out[:, at:] = gains[...]


def deal(n_heads, n_owners, wq, wk, wv, gains):
    rows, width = wq.shape
    return pl.pallas_call(
        functools.partial(deal_kernel, n_heads, n_owners),
        out_shape=jax.ShapeDtypeStruct((rows, 3 * width + gains.shape[1]), wq.dtype),
        in_specs=whole(4),
        out_specs=whole(1)[0],
        compiler_params=pltpu.CompilerParams(vmem_limit_bytes=4 << 20),
        cost_estimate=pl.CostEstimate(flops=1, bytes_accessed=1, transcendentals=0),
        name="deal",
    )(wq, wk, wv, gains)


def join_kernel(turn, *refs):
    where, blocks, out, sems = refs[0], refs[1:-2], refs[-2], refs[-1]
    size = blocks[0].shape[1]
    targets = [
        out.at[:, pl.ds(pl.multiple_of((where[0] ^ flip) * size, HEAD_DIM), size)] for flip in turn
    ]
    for copy in fetch(blocks, targets, sems):
        copy.wait()


def join(where, turn, blocks):
    rows, size = blocks[0].shape
    return pl.pallas_call(
        functools.partial(join_kernel, turn),
        out_shape=jax.ShapeDtypeStruct((rows, len(blocks) * size), blocks[0].dtype),
        in_specs=[smem()] + hbm(len(blocks)),
        out_specs=hbm(1)[0],
        scratch_shapes=[pltpu.SemaphoreType.DMA((len(blocks),))],
        compiler_params=pltpu.CompilerParams(vmem_limit_bytes=4 << 20),
        cost_estimate=pl.CostEstimate(flops=1, bytes_accessed=1, transcendentals=0),
        name="join",
    )(where, *blocks)


def settle_kernel(rels, widths, chunks, *refs):
    where = refs[0]
    pieces = refs[1 : 1 + len(rels)]
    outs = refs[1 + len(rels) : 1 + len(rels) + len(widths)]
    sems = refs[-1]
    rows = pieces[0].shape[0]
    count = rows // chunks
    copies = []
    for piece, rel in zip(pieces, rels):
        rel, half = rel if isinstance(rel, tuple) else (rel, 0)
        hops = piece.shape[0] // count
        for hop in range(hops):
            chunk = (where[1] + chunks - half * hops - hop) % chunks
            start = pl.multiple_of((where[0] ^ rel) * rows + chunk * count, 16)
            left = 0
            for out, width in zip(outs, widths):
                copy = pltpu.make_async_copy(
                    piece.at[pl.ds(hop * count, count), pl.ds(left, width)],
                    out.at[pl.ds(start, count), :],
                    sems.at[len(copies)],
                )
                copy.start()
                copies.append(copy)
                left += width
    for copy in copies:
        copy.wait()


def settle(where, rels, pieces, widths, chunks):
    low = jnp.bfloat16
    total = sum(piece.shape[0] for piece in pieces)
    return pl.pallas_call(
        functools.partial(settle_kernel, rels, widths, chunks),
        out_shape=[jax.ShapeDtypeStruct((total, width), low) for width in widths],
        in_specs=[smem()] + hbm(len(pieces)),
        out_specs=hbm(len(widths)),
        scratch_shapes=[pltpu.SemaphoreType.DMA((len(pieces) * chunks * len(widths),))],
        compiler_params=pltpu.CompilerParams(vmem_limit_bytes=4 << 20),
        cost_estimate=pl.CostEstimate(flops=1, bytes_accessed=1, transcendentals=0),
        name="settle",
    )(where, *pieces)


def segment_pairs(n_doc, n_seq):
    places = [(d, z) for d in range(n_doc) for z in range(n_seq)]

    def route(target):
        pairs = [(d * n_seq + z, target(d, z)[0] * n_seq + target(d, z)[1]) for d, z in places]
        return [(source, goal) for source, goal in pairs if source != goal]

    def regroup(rel):
        def target(d, z):
            spot = z ^ rel
            return ((d & ~1) | (spot >> 1), 2 * (d & 1) + (spot & 1))

        return target

    routes = {
        "core": route(lambda d, z: (d ^ 1, z)),
        "x": route(lambda d, z: (d ^ 2, z)),
        "y": route(lambda d, z: (d ^ 4, z)),
        "xy": route(lambda d, z: (d ^ 6, z)),
        "z1": route(lambda d, z: (d, (z + 1) % n_seq)),
        "z2": route(lambda d, z: (d, (z + 2) % n_seq)),
        "z3": route(lambda d, z: (d, (z + 3) % n_seq)),
    }
    for rel in range(n_seq):
        routes["group", rel] = route(regroup(rel))
        routes["part", rel] = route(
            lambda d, z, rel=rel: (d ^ (rel >> 1), z ^ (rel & 1))
        )
    return routes


def later(values, *others):
    return lax.optimization_barrier((values, others))[0]


def on_pair(
    routes,
    tokens,
    w_query,
    w_key,
    w_value,
    w_out,
    w_gate,
    w_up,
    w_down,
    gain_attn,
    gain_ffn,
    cache_keys,
    cache_values,
    memory_flags,
    memory_source,
    positions,
    out_grad,
):
    low, wide = jnp.bfloat16, jnp.float32
    n_doc, n_seq = lax.axis_size("doc"), lax.axis_size("seq")
    d, z = lax.axis_index("doc"), lax.axis_index("seq")
    core, odd, pair, plane = d & 1, z & 1, z >> 1, d >> 1
    quarter = 2 * core + odd
    heads_at = 2 * odd + core
    turn = (0, 2, 1, 3)
    width = tokens.shape[2]
    ff_width = w_gate.shape[1]
    share = width // n_seq
    n_heads = share // HEAD_DIM
    where = jnp.stack([d, z]).astype(jnp.int32)
    mem_rows = 2 * n_seq * cache_keys.shape[1]

    def move(array, name):
        return lax.ppermute(array, LINE, routes[name])

    def to_group(array, rel=0):
        moved = move(array, ("group", rel))
        return moved if rel else jnp.where(pair == core, array, moved)

    def pick(array, index, axis=0):
        return lax.dynamic_index_in_dim(array, index, axis, keepdims=False)

    def plus(*terms):
        total = terms[0].astype(wide)
        for term in terms[1:]:
            total = total + term.astype(wide)
        return total.astype(low)

    def along_z(shard):
        return [shard] + [move(shard, f"z{hop}") for hop in range(1, n_seq)]

    def in_plane(block):
        return [block, move(block, "x"), move(block, "y"), move(block, "xy")]

    def swap_halves(pieces):
        cut = pieces[1].shape[0] // 2
        return [move(pieces[1][:cut], "y"), move(pieces[2][cut:], "x")]

    def other_core(pieces):
        return pieces + [move(piece, "core") for piece in pieces]

    rels = (0, 2, 4, 6, 1, 3, 5, 7)

    def part_for(array, rel, size):
        return lax.dynamic_slice_in_dim(array, (heads_at ^ turn[rel]) * size, size, 1)

    heads_where = heads_at.astype(jnp.int32).reshape(1)

    def spread(blocks):
        return join(heads_where, turn, blocks)

    def exchange(blocks):
        return [blocks[0]] + [move(blocks[rel], ("part", rel)) for rel in range(1, n_seq)]

    gains = jnp.concatenate([gain_attn[:, None], gain_ffn[:, None]], 1)
    gains = jnp.pad(gains, ((0, 0), (0, HEAD_DIM - 2)))
    lines = along_z(deal(n_heads, n_seq, w_query, w_key, w_value, gains))

    own_kv = jnp.concatenate([cache_keys[0], cache_values[0]], 1)
    two = jnp.stack([own_kv, move(own_kv, "x")])
    notes = jnp.concatenate([memory_flags, memory_source])
    notes_core, notes_y = later((move(notes, "core"), move(notes, "y")), two)
    flag = jnp.where(pair == core, notes[0], notes_core[0])
    source, source_y = notes[1], notes_y[1]
    place = jnp.stack([quarter, flag]).astype(jnp.int32)
    pos = [to_group(later(positions[0], two), rel) for rel in range(n_seq)]

    four = jnp.concatenate([two, move(two, "core")])

    def spot(src):
        return 2 * ((src ^ d) & 1) + (((src ^ d) >> 1) & 1)

    for_y = pick(four, spot(source_y))
    from_y = move(for_y, "y")
    block = jnp.concatenate(later(lines, for_y))
    rows = block.shape[0]
    projections = in_plane(block)
    lines_ab = along_z(later(jnp.concatenate([w_out, w_gate, w_up], 1), block))
    from_y = later(from_y, block)
    src_kv = jnp.where(((source ^ d) >> 2) == 0, pick(four, spot(source)), from_y)

    def heads_for(rel):
        to = z ^ rel
        at = (2 * (to & 1) + (to >> 1)) * share
        picked = [
            lax.dynamic_slice_in_dim(kv, side * width + at, share, 1)
            for kv in (own_kv, src_kv)
            for side in (0, 1)
        ]
        return jnp.concatenate(picked, 1)

    parts = [heads_for(rel) for rel in range(n_seq)]
    cos_h, sin_h = rotary_tables(jnp.concatenate(later(pos, parts)))
    cos_t = jnp.concatenate([cos_h, cos_h], -1)
    sin_t = jnp.concatenate([-sin_h, sin_h], -1)
    block_ab = jnp.concatenate(later(lines_ab, cos_t, sin_t))
    tok = to_group(later(tokens[0], block_ab))
    projections = later(projections, block_ab)
    pieces_ab = in_plane(later(block_ab, projections))[:3]
    *w_heads, gain_cols = settle(
        where,
        rels,
        other_core(projections),
        (3 * n_seq * HEAD_DIM,) * n_heads + (HEAD_DIM,),
        n_seq,
    )
    gain_a = gain_cols[:, 0].astype(wide)
    gain_f = gain_cols[:, 1].astype(wide)

    inputs = later(tok, w_heads).astype(wide)
    factor_one = rms_factor(inputs)
    normed_one = inputs * factor_one
    attn_in = (normed_one * gain_a).astype(low)

    def projected(head, *others):
        weight = later(w_heads[head], *others) if others else w_heads[head]
        qkv = dot_nn(attn_in, weight).astype(low)
        return [part_for(qkv, rel, 3 * HEAD_DIM) for rel in range(n_seq)]

    first = projected(0)
    first_own = first[0]
    first = exchange(first)
    parts = later(parts, first_own)
    memory = [to_group(part, rel) for rel, part in enumerate(parts)]
    second = projected(1, parts)
    second_own = second[0]
    second = exchange(second)
    pieces_ab = later(pieces_ab, second_own)
    far_ab = swap_halves(pieces_ab)
    first, memory = later((first, memory), pieces_ab)
    saved_0 = attend(0, place, first, memory, mem_rows, cos_t, sin_t)
    att_0 = saved_0[4]
    lines_c = along_z(later(w_down, att_0))
    *saved_1, o0, o1, o2, o3 = attend(
        1, place, later(second, att_0), memory, mem_rows, cos_t, sin_t, (att_0,)
    )
    block_c = jnp.stack(later(lines_c, o0))
    block_c = jnp.concatenate([pick(block_c, (z - at) % n_seq) for at in range(n_seq)])
    rows_c = block_c.shape[0]
    att = exchange(later([o0, o1, o2, o3], block_c))
    far_ab = later(far_ab, block_c)
    pieces_c = in_plane(later(block_c, far_ab))
    w_out_f, w_gate_f, w_up_f = settle(
        where,
        (0, 2, 4, 1, 3, 5, (6, 0), (6, 1), (7, 0), (7, 1)),
        other_core(later(pieces_ab, block_c)) + other_core(far_ab),
        (width, ff_width, ff_width),
        n_seq,
    )
    attn_low = spread(later(att, w_out_f))
    grad_y = to_group(later(out_grad[0], attn_low))
    resid_mid = inputs + dot_nn(attn_low, w_out_f)
    factor_two = rms_factor(resid_mid)
    normed_two = resid_mid * factor_two
    ffn_in = (normed_two * gain_f).astype(low)
    gate_act = dot_nn(ffn_in, w_gate_f)
    up_act = dot_nn(ffn_in, w_up_f)
    sig_gate = jax.nn.sigmoid(gate_act)
    silu_gate = gate_act * sig_gate
    hidden = (silu_gate * up_act).astype(low)
    grad_y, pieces_c = later((grad_y, pieces_c), hidden)

    def side(array, which, turned=True):
        return jnp.concatenate(
            [
                lax.dynamic_slice_in_dim(
                    array, (2 * (plane ^ rel if turned else rel) + which) * rows, rows, 1
                )
                for rel in range(n_doc // 2)
            ],
            1,
        )

    def plane_parts(both):
        size = both.shape[0] // (n_doc // 2)
        return [both[rel * size : (rel + 1) * size] for rel in range(n_doc // 2)]

    def over_plane(parts):
        return [parts[0]] + [
            move(part, name) for part, name in zip(parts[1:], ("x", "y", "xy"))
        ]

    def met_in_plane(both):
        return over_plane(plane_parts(both))

    def finish_by_hops(total):
        chunks = total.reshape(n_seq, -1, total.shape[1])
        return sum(
            (
                move(pick(chunks, (z + hop) % n_seq), f"z{hop}").astype(wide)
                for hop in range(1, n_seq)
            ),
            pick(chunks, z).astype(wide),
        )

    def kept(mine, array, met):
        return (dot_tn(mine, array) + met.astype(wide)).astype(low)

    pieces_c = other_core(pieces_c)
    grad_down = dot_tn(hidden, grad_y).astype(low).reshape(n_doc // 2, 2, rows_c, width)
    down_sent = pick(grad_down, 1 - core, 1)
    met_down = move(down_sent, "core")
    (w_down_f,) = settle(where, rels, later(pieces_c, down_sent), (width,), 1)
    layer_out = (resid_mid + dot_nn(hidden, w_down_f)).astype(low)
    layer_moved = to_group(layer_out)
    d_hidden = dot_nt(later(grad_y, layer_out), w_down_f)
    d_gate = (d_hidden * up_act * (sig_gate * (1.0 + gate_act * (1.0 - sig_gate)))).astype(low)
    d_up = (d_hidden * silu_gate).astype(low)
    d_ffn_in = dot_nt(d_gate, w_gate_f) + dot_nt(d_up, w_up_f)
    d_mid = grad_y.astype(wide) + norm_back(d_ffn_in * gain_f, normed_two, factor_two)
    layer_out = later(layer_moved, d_ffn_in)
    d_branch = later(d_mid, layer_out).astype(low)
    d_att = dot_nt(d_branch, w_out_f).astype(low)
    d_blocks = [part_for(d_att, rel, share) for rel in range(n_seq)]
    d_sent = d_blocks[0]
    d_blocks = exchange(d_blocks)
    met_down = later(met_down, d_sent)
    both_down = plus(pick(grad_down, core, 1), met_down)
    down_parts = [pick(both_down, plane ^ rel) for rel in range(n_doc // 2)]
    total_down = over_plane(down_parts)
    away, home = side(ffn_in, 1 - core), side(ffn_in, core)
    away_gate = dot_tn(away, d_gate).astype(low)
    met_gate = move(away_gate, "core")
    away_up = dot_tn(later(away, away_gate), d_up).astype(low)
    met_up = move(away_up, "core")
    d_blocks = later(d_blocks, away_up)
    g_0 = attend_back(
        0, place, saved_0, d_blocks, memory, mem_rows, cos_t, sin_t, down_parts[1:]
    )
    d_set_0 = exchange(g_0)
    both_gate = kept(home, d_gate, later(met_gate, g_0))
    both_up = kept(home, d_up, later(met_up, both_gate))
    total_down = later(total_down, both_up)
    gate_parts = plane_parts(later(both_gate, total_down))
    total_gate = over_plane(gate_parts)
    g_1 = attend_back(
        1, place, saved_1, later(d_blocks, both_up), memory, mem_rows, cos_t, sin_t,
        (both_up, *total_down[1:], *gate_parts[1:]),
    )
    g_1 = later(g_1, d_set_0)
    d_set_1 = exchange(g_1)

    away, home_in = side(attn_in, 1 - core), side(attn_in, core)
    d_qkv_0 = spread(later(d_set_0, g_1))
    away_0 = dot_tn(away, d_qkv_0).astype(low)
    met_0 = move(away_0, "core")
    total_gate = later(total_gate, away_0)
    total_up = met_in_plane(later(both_up, total_gate))
    d_set_1 = later(d_set_1, total_gate)
    d_qkv_1 = spread(d_set_1)
    away_1 = dot_tn(away, d_qkv_1).astype(low)
    met_1 = move(away_1, "core")
    out_down = finish_by_hops(plus(*later(total_down, away_1)))
    both_0 = kept(home_in, d_qkv_0, later(met_0, away_1))
    away_out = dot_tn(later(side(attn_low, 1 - core), both_0), d_branch).astype(low)
    met_out = move(away_out, "core")
    both_1 = kept(home_in, d_qkv_1, later(met_1, away_out))
    both_out = kept(side(attn_low, core), later(d_branch, both_1), later(met_out, both_1))
    both = jnp.concatenate([both_0, both_1, both_out], 1)
    total_gate = plus(*later(total_gate, both))
    out_gate = finish_by_hops(total_gate)
    total_up = later(total_up, total_gate)
    last = met_in_plane(later(both, total_up))
    d_attn_in = dot_nt(later(d_qkv_0, total_up), w_heads[0]) + dot_nt(
        later(d_qkv_1, total_up), w_heads[1]
    )
    grad_in = d_mid + norm_back(d_attn_in * gain_a, normed_one, factor_one)
    grad_in = grad_in.astype(low)
    grad_tokens = to_group(grad_in).astype(wide)
    out_up = finish_by_hops(plus(*later(total_up, grad_in)))
    both = finish_by_hops(plus(*later(last, grad_in)))
    out_out = both[:, 3 * width :]
    split = both[:, : 3 * width].reshape(-1, n_heads, n_seq, 3, HEAD_DIM)
    split = jnp.swapaxes(split, 1, 2)
    out_q, out_k, out_v = (split[:, :, :, which].reshape(-1, width) for which in range(3))

    def gain_grad(gain, pairs):
        total = sum(jnp.sum(weight.astype(wide) * grad, 1) for weight, grad in pairs)
        return total / gain.astype(wide)

    return (
        layer_out[None],
        grad_tokens[None],
        out_q,
        out_k,
        out_v,
        out_out,
        out_gate,
        out_up,
        out_down,
        gain_grad(gain_attn, ((w_query, out_q), (w_key, out_k), (w_value, out_v))),
        gain_grad(gain_ffn, ((w_gate, out_gate), (w_up, out_up))),
    )


def solution(mesh):
    in_specs = (
        P("doc", "seq", None),
        P(("doc", "seq"), None),
        P(("doc", "seq"), None),
        P(("doc", "seq"), None),
        P(("doc", "seq"), None),
        P(("doc", "seq"), None),
        P(("doc", "seq"), None),
        P(("doc", "seq"), None),
        P(("doc", "seq")),
        P(("doc", "seq")),
        P("doc", "seq", None),
        P("doc", "seq", None),
        P("doc"),
        P("doc"),
        P("doc", "seq"),
        P("doc", "seq", None),
    )
    out_specs = (
        P("doc", "seq", None),
        P("doc", "seq", None),
        P(("doc", "seq"), None),
        P(("doc", "seq"), None),
        P(("doc", "seq"), None),
        P(("doc", "seq"), None),
        P(("doc", "seq"), None),
        P(("doc", "seq"), None),
        P(("doc", "seq"), None),
        P(("doc", "seq")),
        P(("doc", "seq")),
    )
    n_doc, n_seq = mesh.shape["doc"], mesh.shape["seq"]
    step = on_device
    if (n_doc, n_seq) == (8, 4):
        step = functools.partial(on_pair, segment_pairs(n_doc, n_seq))
    return jax.shard_map(
        step, mesh=mesh, in_specs=in_specs, out_specs=out_specs, check_vma=False
    )
```

```python
import functools
import math

import jax
import jax.numpy as jnp
from jax import lax
from jax.experimental import pallas as pl
from jax.experimental.pallas import tpu as pltpu
from jax.sharding import PartitionSpec as P

HEADS = 8
HEAD_DIM = 128


EPS_NORM = 1e-05
NEG_FILL = -1e30


def rms_factor(values):
    return lax.rsqrt(jnp.mean(values * values, -1, keepdims=True) + EPS_NORM)


def rotary_tables(token_pos):
    half_dim = HEAD_DIM // 2
    frequency = jnp.exp(
        jnp.arange(half_dim, dtype=jnp.float32) * (-2.0 * math.log(10000.0) / HEAD_DIM)
    )
    angles = token_pos.astype(jnp.float32)[..., None] * frequency
    return (jnp.cos(angles), jnp.sin(angles))


def rotate(values, cos_vals, sin_vals):
    half_dim = values.shape[-1] // 2
    first_half = values[..., :half_dim]
    second_half = values[..., half_dim:]
    cos_b = cos_vals[..., None, :]
    sin_b = sin_vals[..., None, :]
    return jnp.concatenate(
        [first_half * cos_b - second_half * sin_b, second_half * cos_b + first_half * sin_b], -1
    )


def rotate_back(grads, cos_vals, sin_vals):
    half_dim = grads.shape[-1] // 2
    first_half = grads[..., :half_dim]
    second_half = grads[..., half_dim:]
    cos_b = cos_vals[..., None, :]
    sin_b = sin_vals[..., None, :]
    return jnp.concatenate(
        [first_half * cos_b + second_half * sin_b, second_half * cos_b - first_half * sin_b], -1
    )


def online_step(fold_state, scores, allowed, value_heads):
    row_max, row_sum, weighted = fold_state
    masked = jnp.where(allowed, scores, NEG_FILL)
    new_max = jnp.maximum(row_max, jnp.max(masked, -1))
    weights_p = jnp.where(allowed, jnp.exp(scores - new_max[..., None]), 0.0)
    rescale = jnp.exp(row_max - new_max)
    row_sum = row_sum * rescale + jnp.sum(weights_p, -1)
    weighted = weighted * jnp.transpose(rescale, (0, 2, 1))[..., None] + jnp.einsum(
        "shqk,skhd->sqhd",
        weights_p.astype(jnp.bfloat16),
        value_heads,
        preferred_element_type=jnp.float32,
    )
    return (new_max, row_sum, weighted)


def norm_back(d_normed, normed, factor):
    return factor * (d_normed - normed * jnp.mean(d_normed * normed, -1, keepdims=True))


def on_device(
    tokens,
    w_query,
    w_key,
    w_value,
    w_out,
    w_gate,
    w_up,
    w_down,
    gain_attn,
    gain_ffn,
    cache_keys,
    cache_values,
    memory_flags,
    memory_source,
    positions,
    out_grad,
):
    fwd_weights = (
        lax.all_gather(w_query, ("doc", "seq"), axis=0, tiled=True),
        lax.all_gather(w_key, ("doc", "seq"), axis=0, tiled=True),
        lax.all_gather(w_value, ("doc", "seq"), axis=0, tiled=True),
        lax.all_gather(w_out, ("doc", "seq"), axis=0, tiled=True),
        lax.all_gather(w_gate, ("doc", "seq"), axis=0, tiled=True),
        lax.all_gather(w_up, ("doc", "seq"), axis=0, tiled=True),
        lax.all_gather(w_down, ("doc", "seq"), axis=0, tiled=True),
        lax.all_gather(gain_attn, ("doc", "seq"), axis=0, tiled=True),
        lax.all_gather(gain_ffn, ("doc", "seq"), axis=0, tiled=True),
    )
    seg_count, tok_local, model_width = tokens.shape
    ff_width = w_gate.shape[1]
    flat_rows = seg_count * tok_local
    score_scale = 1.0 / math.sqrt(HEAD_DIM)
    total_len = tok_local * lax.axis_size("seq")
    state_shape = (seg_count, HEADS, tok_local)
    head_shape = (seg_count, tok_local, HEADS, HEAD_DIM)
    inputs = tokens.astype(jnp.float32)
    factor_one = rms_factor(inputs)
    normed_one = inputs * factor_one
    attn_in = (normed_one * fwd_weights[7].astype(jnp.float32)).astype(jnp.bfloat16)
    query_f = jnp.dot(attn_in, fwd_weights[0], preferred_element_type=jnp.float32)
    keys_f = jnp.dot(attn_in, fwd_weights[1], preferred_element_type=jnp.float32)
    v_low = jnp.dot(attn_in, fwd_weights[2], preferred_element_type=jnp.float32).astype(
        jnp.bfloat16
    )
    cos_vals, sin_vals = rotary_tables(positions)
    q_heads = query_f.reshape(head_shape)
    q_rot = rotate(q_heads, cos_vals, sin_vals).astype(jnp.bfloat16)
    q_mem = q_heads.astype(jnp.bfloat16)
    k_rot = (
        rotate(keys_f.reshape(head_shape), cos_vals, sin_vals)
        .astype(jnp.bfloat16)
        .reshape(seg_count, tok_local, model_width)
    )
    query_rows = lax.axis_index("seq") * tok_local + jnp.arange(tok_local, dtype=jnp.int32)
    initial = (
        jnp.full(state_shape, NEG_FILL, jnp.float32),
        jnp.zeros(state_shape, jnp.float32),
        jnp.zeros(head_shape, jnp.float32),
    )
    key_part = lax.all_gather(k_rot, "seq", axis=1, tiled=True)
    value_part = lax.all_gather(v_low, "seq", axis=1, tiled=True)
    key_span = key_part.shape[1]
    key_heads = key_part.reshape(seg_count, key_span, HEADS, HEAD_DIM)
    scores = (
        jnp.einsum("sqhd,skhd->shqk", q_rot, key_heads, preferred_element_type=jnp.float32)
        * score_scale
    )
    key_cols = jnp.arange(key_span, dtype=jnp.int32)
    allowed = (key_cols[None, :] <= query_rows[:, None])[None, None]
    fold_state = online_step(
        initial, scores, allowed, value_part.reshape(seg_count, key_span, HEADS, HEAD_DIM)
    )
    every_keys, every_values = (
        lax.all_gather(cache_keys, "doc", axis=0, tiled=True),
        lax.all_gather(cache_values, "doc", axis=0, tiled=True),
    )
    mem_keys = jnp.concatenate([cache_keys, jnp.take(every_keys, memory_source, axis=0)], 1)
    mem_values = jnp.concatenate([cache_values, jnp.take(every_values, memory_source, axis=0)], 1)
    flag_on = (memory_flags > 0)[:, None, None, None]
    key_part = lax.all_gather(mem_keys, "seq", axis=1, tiled=True)
    value_part = lax.all_gather(mem_values, "seq", axis=1, tiled=True)
    key_span = key_part.shape[1]
    key_heads = key_part.reshape(seg_count, key_span, HEADS, HEAD_DIM)
    scores = (
        jnp.einsum("sqhd,skhd->shqk", q_mem, key_heads, preferred_element_type=jnp.float32)
        * score_scale
    )
    row_max, row_sum, weighted = online_step(
        fold_state, scores, flag_on, value_part.reshape(seg_count, key_span, HEADS, HEAD_DIM)
    )
    log_total = row_max + jnp.log(row_sum)
    attended = weighted / jnp.transpose(row_sum, (0, 2, 1))[..., None]
    attn_low = attended.reshape(flat_rows, model_width).astype(jnp.bfloat16)
    resid_mid = inputs.reshape(flat_rows, model_width) + jnp.dot(
        attn_low, fwd_weights[3], preferred_element_type=jnp.float32
    )
    factor_two = rms_factor(resid_mid)
    normed_two = resid_mid * factor_two
    ffn_in = (normed_two * fwd_weights[8].astype(jnp.float32)).astype(jnp.bfloat16)
    gate_act = jnp.dot(ffn_in, fwd_weights[4], preferred_element_type=jnp.float32)
    up_act = jnp.dot(ffn_in, fwd_weights[5], preferred_element_type=jnp.float32)
    sig_gate = jax.nn.sigmoid(gate_act)
    silu_gate = jax.nn.silu(gate_act)
    hidden = (silu_gate * up_act).astype(jnp.bfloat16)
    result = (
        resid_mid + jnp.dot(hidden, fwd_weights[6], preferred_element_type=jnp.float32)
    ).astype(jnp.bfloat16)
    back_weights = (
        lax.all_gather(w_query, ("doc", "seq"), axis=0, tiled=True),
        lax.all_gather(w_key, ("doc", "seq"), axis=0, tiled=True),
        lax.all_gather(w_value, ("doc", "seq"), axis=0, tiled=True),
        lax.all_gather(w_out, ("doc", "seq"), axis=0, tiled=True),
        lax.all_gather(w_gate, ("doc", "seq"), axis=0, tiled=True),
        lax.all_gather(w_up, ("doc", "seq"), axis=0, tiled=True),
        lax.all_gather(w_down, ("doc", "seq"), axis=0, tiled=True),
        lax.all_gather(gain_attn, ("doc", "seq"), axis=0, tiled=True),
        lax.all_gather(gain_ffn, ("doc", "seq"), axis=0, tiled=True),
    )
    grad_y = out_grad.reshape(flat_rows, model_width)
    d_hidden = jnp.einsum("td,fd->tf", grad_y, back_weights[6], preferred_element_type=jnp.float32)
    d_gate = (d_hidden * up_act * (sig_gate * (1.0 + gate_act * (1.0 - sig_gate)))).astype(
        jnp.bfloat16
    )
    d_up = (d_hidden * silu_gate).astype(jnp.bfloat16)
    d_ffn_in = jnp.einsum(
        "tf,df->td", d_gate, back_weights[4], preferred_element_type=jnp.float32
    ) + jnp.einsum("tf,df->td", d_up, back_weights[5], preferred_element_type=jnp.float32)
    g_gain_ffn = jnp.sum(d_ffn_in * normed_two, 0)
    d_mid = grad_y.astype(jnp.float32) + norm_back(
        d_ffn_in * back_weights[8].astype(jnp.float32), normed_two, factor_two
    )
    d_branch = d_mid.astype(jnp.bfloat16)
    d_att = (
        jnp.einsum("te,de->td", d_branch, back_weights[3], preferred_element_type=jnp.float32)
        .astype(jnp.bfloat16)
        .reshape(head_shape)
    )
    delta_rows = jnp.transpose(jnp.sum(d_att.astype(jnp.float32) * attended, -1), (0, 2, 1))
    gathered_keys, gathered_values = (
        lax.all_gather(k_rot, "seq", axis=1, tiled=True),
        lax.all_gather(v_low, "seq", axis=1, tiled=True),
    )
    block_len = min(512, total_len)
    n_blocks = total_len // block_len
    key_blocks = jnp.transpose(
        gathered_keys.reshape(seg_count, n_blocks, block_len, HEADS, HEAD_DIM), (1, 0, 2, 3, 4)
    )
    value_blocks = jnp.transpose(
        gathered_values.reshape(seg_count, n_blocks, block_len, HEADS, HEAD_DIM), (1, 0, 2, 3, 4)
    )

    def block_grads(key_heads, value_heads, block_num):
        scores = (
            jnp.einsum("sqhd,skhd->shqk", q_rot, key_heads, preferred_element_type=jnp.float32)
            * score_scale
        )
        key_cols = block_num * block_len + jnp.arange(block_len, dtype=jnp.int32)
        allowed = (key_cols[None, :] <= query_rows[:, None])[None, None]
        probabilities = jnp.where(allowed, jnp.exp(scores - log_total[..., None]), 0.0)
        d_probs = jnp.einsum(
            "sqhd,skhd->shqk", d_att, value_heads, preferred_element_type=jnp.float32
        )
        d_scores = (probabilities * (d_probs - delta_rows[..., None])).astype(jnp.bfloat16)
        return (probabilities, d_scores)

    def query_step(d_query_acc, block_inputs):
        key_heads, value_heads, block_num = block_inputs
        probabilities, d_scores = block_grads(key_heads, value_heads, block_num)
        return (
            d_query_acc
            + jnp.einsum(
                "shqk,skhd->sqhd", d_scores, key_heads, preferred_element_type=jnp.float32
            ),
            None,
        )

    d_qrot, unused_out = lax.scan(
        query_step,
        jnp.zeros(head_shape, jnp.float32),
        (key_blocks, value_blocks, jnp.arange(n_blocks, dtype=jnp.int32)),
    )
    own_keys = k_rot.reshape(head_shape)
    own_values = v_low.reshape(head_shape)
    lse_rows = jnp.transpose(log_total, (0, 2, 1))
    delta_tok = jnp.transpose(delta_rows, (0, 2, 1))
    q_part = lax.all_gather(q_rot, "seq", axis=1, tiled=True)
    datt_part = lax.all_gather(d_att, "seq", axis=1, tiled=True)
    lse_part = lax.all_gather(lse_rows.astype(jnp.bfloat16), "seq", axis=1, tiled=True).astype(
        jnp.float32
    )
    delta_part = lax.all_gather(delta_tok.astype(jnp.bfloat16), "seq", axis=1, tiled=True).astype(
        jnp.float32
    )
    row_span = q_part.shape[1]
    scores = (
        jnp.einsum("sqhd,skhd->shqk", q_part, own_keys, preferred_element_type=jnp.float32)
        * score_scale
    )
    visit_rows = jnp.arange(row_span, dtype=jnp.int32)
    allowed = (query_rows[None, :] <= visit_rows[:, None])[None, None]
    lse_heads = jnp.transpose(lse_part, (0, 2, 1))
    delta_heads = jnp.transpose(delta_part, (0, 2, 1))
    probabilities = jnp.where(allowed, jnp.exp(scores - lse_heads[..., None]), 0.0)
    d_probs = jnp.einsum(
        "sqhd,skhd->shqk", datt_part, own_values, preferred_element_type=jnp.float32
    )
    d_scores = (probabilities * (d_probs - delta_heads[..., None])).astype(jnp.bfloat16)
    key_acc = jnp.einsum("shqk,sqhd->skhd", d_scores, q_part, preferred_element_type=jnp.float32)
    value_acc = jnp.einsum(
        "shqk,sqhd->skhd",
        probabilities.astype(jnp.bfloat16),
        datt_part,
        preferred_element_type=jnp.float32,
    )
    key_acc, value_acc = (key_acc, value_acc)
    key_sum = key_acc.reshape(seg_count, tok_local, model_width)
    value_sum = value_acc.reshape(seg_count, tok_local, model_width)
    key_part = lax.all_gather(mem_keys, "seq", axis=1, tiled=True)
    value_part = lax.all_gather(mem_values, "seq", axis=1, tiled=True)
    key_span = key_part.shape[1]
    key_heads = key_part.reshape(seg_count, key_span, HEADS, HEAD_DIM)
    value_heads = value_part.reshape(seg_count, key_span, HEADS, HEAD_DIM)
    scores = (
        jnp.einsum("sqhd,skhd->shqk", q_mem, key_heads, preferred_element_type=jnp.float32)
        * score_scale
    )
    probabilities = jnp.where(flag_on, jnp.exp(scores - log_total[..., None]), 0.0)
    d_probs = jnp.einsum("sqhd,skhd->shqk", d_att, value_heads, preferred_element_type=jnp.float32)
    d_scores = (probabilities * (d_probs - delta_rows[..., None])).astype(jnp.bfloat16)
    d_qmem = jnp.einsum("shqk,skhd->sqhd", d_scores, key_heads, preferred_element_type=jnp.float32)
    d_query = (
        ((rotate_back(d_qrot, cos_vals, sin_vals) + d_qmem) * score_scale)
        .astype(jnp.bfloat16)
        .reshape(flat_rows, model_width)
    )
    d_key = (
        (rotate_back(key_sum.reshape(head_shape), cos_vals, sin_vals) * score_scale)
        .astype(jnp.bfloat16)
        .reshape(flat_rows, model_width)
    )
    d_value = value_sum.astype(jnp.bfloat16).reshape(flat_rows, model_width)
    attn_in_flat = attn_in.reshape(flat_rows, model_width)
    d_attn_in = jnp.einsum(
        "te,de->td", d_query, back_weights[0], preferred_element_type=jnp.float32
    )
    d_attn_in = d_attn_in + jnp.einsum(
        "te,de->td", d_key, back_weights[1], preferred_element_type=jnp.float32
    )
    d_attn_in = d_attn_in + jnp.einsum(
        "te,de->td", d_value, back_weights[2], preferred_element_type=jnp.float32
    )
    normed_flat = normed_one.reshape(flat_rows, model_width)
    g_gain_attn = jnp.sum(d_attn_in * normed_flat, 0)
    grad_in = d_mid + norm_back(
        d_attn_in * back_weights[7].astype(jnp.float32),
        normed_flat,
        factor_one.reshape(flat_rows, 1),
    )
    grad_tokens = grad_in.reshape(seg_count, tok_local, model_width)
    gate_part = jnp.einsum("td,tf->df", ffn_in, d_gate, preferred_element_type=jnp.float32)
    up_part = jnp.einsum("td,tf->df", ffn_in, d_up, preferred_element_type=jnp.float32)
    both_parts = lax.psum_scatter(
        jnp.concatenate([gate_part, up_part], 1), ("doc", "seq"), scatter_dimension=0, tiled=True
    )
    down_part = lax.psum_scatter(
        jnp.einsum("tf,td->fd", hidden, grad_y, preferred_element_type=jnp.float32),
        ("doc", "seq"),
        scatter_dimension=0,
        tiled=True,
    )
    query_part = jnp.einsum("td,te->de", attn_in_flat, d_query, preferred_element_type=jnp.float32)
    key_part = jnp.einsum("td,te->de", attn_in_flat, d_key, preferred_element_type=jnp.float32)
    value_part = jnp.einsum("td,te->de", attn_in_flat, d_value, preferred_element_type=jnp.float32)
    out_part = jnp.einsum("td,te->de", attn_low, d_branch, preferred_element_type=jnp.float32)
    attn_sums = lax.psum_scatter(
        jnp.concatenate([query_part, key_part, value_part, out_part], 1),
        ("doc", "seq"),
        scatter_dimension=0,
        tiled=True,
    )
    gain_attn_sum, gain_ffn_sum = (
        lax.psum_scatter(g_gain_attn, ("doc", "seq"), scatter_dimension=0, tiled=True),
        lax.psum_scatter(g_gain_ffn, ("doc", "seq"), scatter_dimension=0, tiled=True),
    )
    layer_out = result.reshape(seg_count, tok_local, model_width)
    return (
        layer_out,
        grad_tokens,
        attn_sums[:, :model_width],
        attn_sums[:, model_width : 2 * model_width],
        attn_sums[:, 2 * model_width : 3 * model_width],
        attn_sums[:, 3 * model_width :],
        both_parts[:, :ff_width],
        both_parts[:, ff_width:],
        down_part,
        gain_attn_sum,
        gain_ffn_sum,
    )


LINE = ("doc", "seq")
MXU = dict(preferred_element_type=jnp.float32)
LOG2E = 1.4426950408889634


def dot_nt(left, right):
    return lax.dot_general(left, right, (((1,), (1,)), ((), ())), **MXU)


def dot_tn(left, right):
    return lax.dot_general(left, right, (((0,), (0,)), ((), ())), **MXU)


def dot_nn(left, right):
    return jnp.dot(left, right, **MXU)


def whole(count):
    return [pl.BlockSpec(memory_space=pltpu.VMEM)] * count


def hbm(count):
    return [pl.BlockSpec(memory_space=pl.ANY)] * count


def smem():
    return pl.BlockSpec(memory_space=pltpu.SMEM)


def place_rows(quarter, rel, rows_q):
    return pl.ds(pl.multiple_of((quarter ^ rel) * rows_q, rows_q), rows_q)


def stack_memory(pieces, head, keys_ref, vals_ref):
    count = keys_ref.shape[0] // (2 * len(pieces))
    span = pieces[0].shape[1] // 4
    at = 0
    for piece in pieces:
        for part in (0, 2):
            left = part * span + head * HEAD_DIM
            keys_ref[at : at + count, :] = piece[:count, left : left + HEAD_DIM]
            vals_ref[at : at + count, :] = piece[:count, left + span : left + span + HEAD_DIM]
            at += count


def fetch(sources, targets, sems):
    copies = [
        pltpu.make_async_copy(source, target, sems.at[index])
        for index, (source, target) in enumerate(zip(sources, targets))
    ]
    for copy in copies:
        copy.start()
    return copies


def attend_kernel(head, n_in, n_first, *refs):
    place = refs[0]
    given, refs = refs[1 : 1 + n_in], refs[1 + n_in + n_first :]
    n_kept = n_in - 10
    saved, outs, refs = refs[:6], refs[6 : 6 + 4 * n_kept], refs[6 + 4 * n_kept :]
    held, refs = refs[:n_in], refs[n_in:]
    b0, b1, b2, b3, m0, m1, m2, m3, cos_ref, sin_ref = held[:10]
    kept = held[10:]
    qr_ref, qm_ref, kr_ref, v_ref, att_ref, lse_ref = refs[:6]
    max_s, sum_s, acc_s, mkey, mval, in_sems, out_sems = refs[6:]
    quarter, flag = place[0], place[1]
    rows_q = b0.shape[0]
    tiles = qr_ref.shape[0] // rows_q
    scale2 = LOG2E / math.sqrt(HEAD_DIM)
    half = HEAD_DIM // 2
    low = jnp.bfloat16

    for copy in fetch(given, held, in_sems):
        copy.wait()
    stack_memory((m0, m1, m2, m3), head, mkey, mval)
    for rel, block in enumerate((b0, b1, b2, b3)):
        rows = place_rows(quarter, rel, rows_q)
        turned = pl.ds(rel * rows_q, rows_q)
        cos_t, sin_t = cos_ref[turned, :], sin_ref[turned, :]
        query = block[:, :HEAD_DIM]
        qm_ref[rows, :] = query
        wide = query.astype(jnp.float32)
        qr_ref[rows, :] = (wide * cos_t + pltpu.roll(wide, half, 1) * sin_t).astype(low)
        wide = block[:, HEAD_DIM : 2 * HEAD_DIM].astype(jnp.float32)
        kr_ref[rows, :] = (wide * cos_t + pltpu.roll(wide, half, 1) * sin_t).astype(low)
        v_ref[rows, :] = block[:, 2 * HEAD_DIM :]
    leaving = fetch((qr_ref, qm_ref, kr_ref, v_ref), saved[:4], out_sems)

    def fold(scores, values):
        old_max = max_s[...]
        new_max = jnp.maximum(old_max, jnp.max(scores, 1, keepdims=True))
        spread = jnp.concatenate([new_max] * (scores.shape[1] // HEAD_DIM), 1)
        weights = jnp.exp2((scores - spread) * scale2)
        shrink = jnp.exp2((old_max - new_max) * scale2)
        sum_s[...] = sum_s[...] * shrink + jnp.sum(weights, 1, keepdims=True)
        acc_s[...] = acc_s[...] * shrink + dot_nn(weights.astype(low), values)
        max_s[...] = new_max

    def tile(index, carry):
        rows = pl.ds(pl.multiple_of(index * rows_q, rows_q), rows_q)
        query = qr_ref[rows, :]
        max_s[...] = jnp.full_like(max_s, NEG_FILL)
        sum_s[...] = jnp.zeros_like(sum_s)
        acc_s[...] = jnp.zeros_like(acc_s)

        def earlier(block, inner):
            keys = pl.ds(pl.multiple_of(block * rows_q, rows_q), rows_q)
            fold(dot_nt(query, kr_ref[keys, :]), v_ref[keys, :])
            return inner

        lax.fori_loop(0, index, earlier, 0)
        scores = dot_nt(query, kr_ref[rows, :])
        row_i = lax.broadcasted_iota(jnp.int32, scores.shape, 0)
        col_i = lax.broadcasted_iota(jnp.int32, scores.shape, 1)
        fold(jnp.where(col_i <= row_i, scores, NEG_FILL), v_ref[rows, :])

        @pl.when(flag > 0)
        def _():
            plain = qm_ref[rows, :]
            for at in range(0, mkey.shape[0], rows_q):
                fold(dot_nt(plain, mkey[at : at + rows_q, :]), mval[at : at + rows_q, :])

        total = sum_s[...]
        att_ref[rows, :] = (acc_s[...] / total).astype(low)
        lse = max_s[...] * scale2 + jnp.log(total) * LOG2E
        lse_ref[:, rows] = jnp.transpose(lse)[:8]
        return carry

    lax.fori_loop(0, tiles, tile, 0)

    for rel in range(4 * n_kept // max(n_kept, 1)):
        rows = place_rows(quarter, rel, rows_q)
        for at, source in enumerate((*kept, att_ref)):
            if n_kept:
                outs[rel][:, at * HEAD_DIM : (at + 1) * HEAD_DIM] = source[rows, :]
    for at, (source, target) in enumerate(((att_ref, saved[4]), (lse_ref, saved[5]))):
        copy = pltpu.make_async_copy(source, target, out_sems.at[4 + at])
        copy.start()
        leaving.append(copy)
    for copy in leaving:
        copy.wait()


def attend(head, place, blocks, memory, mem_rows, cos_t, sin_t, kept=(), first=()):
    rows_q = blocks[0].shape[0]
    length = cos_t.shape[0]
    low = jnp.bfloat16
    given = (*blocks, *memory, cos_t, sin_t, *kept)
    saved = [((length, HEAD_DIM), low)] * 5 + [((8, length), jnp.float32)]
    part = jax.ShapeDtypeStruct((rows_q, (len(kept) + 1) * HEAD_DIM), low)
    n_out = 4 if kept else 0
    return pl.pallas_call(
        functools.partial(attend_kernel, head, len(given), len(first)),
        out_shape=[jax.ShapeDtypeStruct(*kind) for kind in saved] + [part] * n_out,
        in_specs=[smem()] + hbm(len(given) + len(first)),
        out_specs=hbm(6) + whole(n_out),
        scratch_shapes=[pltpu.VMEM(array.shape, array.dtype) for array in given]
        + [pltpu.VMEM(*kind) for kind in saved]
        + [pltpu.VMEM((rows_q, HEAD_DIM), jnp.float32)] * 3
        + [pltpu.VMEM((mem_rows, HEAD_DIM), low)] * 2
        + [pltpu.SemaphoreType.DMA((len(given),)), pltpu.SemaphoreType.DMA((6,))],
        compiler_params=pltpu.CompilerParams(vmem_limit_bytes=24 << 20),
        cost_estimate=pl.CostEstimate(flops=1, bytes_accessed=1, transcendentals=0),
        name="attend",
    )(place, *given, *first)


def attend_back_kernel(head, n_in, n_first, *refs):
    place = refs[0]
    given, refs = refs[1 : 1 + n_in], refs[1 + n_in + n_first :]
    g0, g1, g2, g3 = refs[:4]
    held, refs = refs[4 : 4 + n_in], refs[4 + n_in :]
    qr_ref, qm_ref, kr_ref, v_ref, att_ref, lse_ref = held[:6]
    d0, d1, d2, d3, m0, m1, m2, m3, cos_ref, sin_ref = held[6:]
    datt, dkey, dval, dqr, dqm, grads, mkey, mval, in_sems = refs
    coming = fetch(given, held, in_sems)
    quarter, flag = place[0], place[1]
    rows_q = d0.shape[0]
    tiles = qr_ref.shape[0] // rows_q
    scale = 1.0 / math.sqrt(HEAD_DIM)
    scale2 = LOG2E * scale
    half = HEAD_DIM // 2
    low = jnp.bfloat16

    def unrotate(grad, index):
        turned = place_rows(quarter, index, rows_q)
        return grad * cos_ref[turned, :] - pltpu.roll(grad, half, 1) * sin_ref[turned, :]

    for copy in coming:
        copy.wait()
    stack_memory((m0, m1, m2, m3), head, mkey, mval)
    cols = slice(head * HEAD_DIM, (head + 1) * HEAD_DIM)
    for rel, block in enumerate((d0, d1, d2, d3)):
        datt[place_rows(quarter, rel, rows_q), :] = block[:, cols]
    dkey[...] = jnp.zeros_like(dkey)
    dval[...] = jnp.zeros_like(dval)

    def tile(index, carry):
        rows = pl.ds(index * rows_q, rows_q)
        query = qr_ref[rows, :]
        d_out = datt[rows, :]
        delta = jnp.sum(
            jnp.transpose(d_out.astype(jnp.float32) * att_ref[rows, :].astype(jnp.float32)),
            0,
            keepdims=True,
        )
        lse = lse_ref[0:1, rows]
        dqr[...] = jnp.zeros_like(dqr)
        dqm[...] = jnp.zeros_like(dqm)

        def block_grads(keys, values, queries, masked):
            power = dot_nt(keys, queries) * scale2 - lse
            if masked:
                key_i = lax.broadcasted_iota(jnp.int32, power.shape, 0)
                query_i = lax.broadcasted_iota(jnp.int32, power.shape, 1)
                power = jnp.where(key_i <= query_i, power, NEG_FILL)
            probs = jnp.exp2(power)
            d_scores = probs * (dot_nt(values, d_out) - delta)
            return probs.astype(low), d_scores.astype(low)

        def local(keys_at, masked):
            keys = kr_ref[keys_at, :]
            probs, d_scores = block_grads(keys, v_ref[keys_at, :], query, masked)
            dval[keys_at, :] += dot_nn(probs, d_out)
            dkey[keys_at, :] += dot_nn(d_scores, query)
            dqr[...] += dot_tn(d_scores, keys)

        def earlier(block, inner):
            local(pl.ds(block * rows_q, rows_q), False)
            return inner

        for block in range(index):
            earlier(block, 0)
        local(rows, True)

        @pl.when(flag > 0)
        def _():
            plain = qm_ref[rows, :]
            for at in range(0, mkey.shape[0], rows_q):
                keys = mkey[at : at + rows_q, :]
                _, d_scores = block_grads(keys, mval[at : at + rows_q, :], plain, False)
                dqm[...] += dot_tn(d_scores, keys)

        grads[rows, :HEAD_DIM] = ((unrotate(dqr[...], index) + dqm[...]) * scale).astype(low)
        return carry

    for index in range(tiles):
        tile(index, 0)
    for index in range(tiles):
        rows = pl.ds(index * rows_q, rows_q)
        grads[rows, HEAD_DIM : 2 * HEAD_DIM] = (unrotate(dkey[rows, :], index) * scale).astype(low)
        grads[rows, 2 * HEAD_DIM :] = dval[rows, :].astype(low)

    for rel, out in enumerate((g0, g1, g2, g3)):
        out[...] = grads[place_rows(quarter, rel, rows_q), :]


def attend_back(head, place, saved, d_blocks, memory, mem_rows, cos_t, sin_t, first=()):
    rows_q = d_blocks[0].shape[0]
    length = cos_t.shape[0]
    low, wide = jnp.bfloat16, jnp.float32
    given = (*saved, *d_blocks, *memory, cos_t, sin_t)
    return pl.pallas_call(
        functools.partial(attend_back_kernel, head, len(given), len(first)),
        out_shape=[jax.ShapeDtypeStruct((rows_q, 3 * HEAD_DIM), low)] * 4,
        in_specs=[smem()] + hbm(len(given) + len(first)),
        out_specs=whole(4),
        scratch_shapes=[pltpu.VMEM(array.shape, array.dtype) for array in given]
        + [
            pltpu.VMEM((length, HEAD_DIM), low),
            pltpu.VMEM((length, HEAD_DIM), wide),
            pltpu.VMEM((length, HEAD_DIM), wide),
            pltpu.VMEM((rows_q, HEAD_DIM), wide),
            pltpu.VMEM((rows_q, HEAD_DIM), wide),
            pltpu.VMEM((length, 3 * HEAD_DIM), low),
            pltpu.VMEM((mem_rows, HEAD_DIM), low),
            pltpu.VMEM((mem_rows, HEAD_DIM), low),
            pltpu.SemaphoreType.DMA((len(given),)),
        ],
        compiler_params=pltpu.CompilerParams(vmem_limit_bytes=28 << 20),
        cost_estimate=pl.CostEstimate(flops=1, bytes_accessed=1, transcendentals=0),
        name="attend_back",
    )(place, *given, *first)


def deal_kernel(n_heads, n_owners, wq, wk, wv, gains, out):
    at = 0
    for head in range(n_heads):
        for owner in range(n_owners):
            left = (owner * n_heads + head) * HEAD_DIM
            for weight in (wq, wk, wv):
                out[:, at : at + HEAD_DIM] = weight[:, left : left + HEAD_DIM]
                at += HEAD_DIM
    out[:, at:] = gains[...]


def deal(n_heads, n_owners, wq, wk, wv, gains):
    rows, width = wq.shape
    return pl.pallas_call(
        functools.partial(deal_kernel, n_heads, n_owners),
        out_shape=jax.ShapeDtypeStruct((rows, 3 * width + gains.shape[1]), wq.dtype),
        in_specs=whole(4),
        out_specs=whole(1)[0],
        compiler_params=pltpu.CompilerParams(vmem_limit_bytes=4 << 20),
        cost_estimate=pl.CostEstimate(flops=1, bytes_accessed=1, transcendentals=0),
        name="deal",
    )(wq, wk, wv, gains)


def join_kernel(turn, *refs):
    where, blocks, out, sems = refs[0], refs[1:-2], refs[-2], refs[-1]
    size = blocks[0].shape[1]
    targets = [
        out.at[:, pl.ds(pl.multiple_of((where[0] ^ flip) * size, HEAD_DIM), size)] for flip in turn
    ]
    for copy in fetch(blocks, targets, sems):
        copy.wait()


def join(where, turn, blocks):
    rows, size = blocks[0].shape
    return pl.pallas_call(
        functools.partial(join_kernel, turn),
        out_shape=jax.ShapeDtypeStruct((rows, len(blocks) * size), blocks[0].dtype),
        in_specs=[smem()] + hbm(len(blocks)),
        out_specs=hbm(1)[0],
        scratch_shapes=[pltpu.SemaphoreType.DMA((len(blocks),))],
        compiler_params=pltpu.CompilerParams(vmem_limit_bytes=4 << 20),
        cost_estimate=pl.CostEstimate(flops=1, bytes_accessed=1, transcendentals=0),
        name="join",
    )(where, *blocks)


def settle_kernel(rels, widths, chunks, *refs):
    where = refs[0]
    pieces = refs[1 : 1 + len(rels)]
    outs = refs[1 + len(rels) : 1 + len(rels) + len(widths)]
    sems = refs[-1]
    rows = pieces[0].shape[0]
    count = rows // chunks
    copies = []
    for piece, rel in zip(pieces, rels):
        rel, half = rel if isinstance(rel, tuple) else (rel, 0)
        hops = piece.shape[0] // count
        for hop in range(hops):
            chunk = (where[1] + chunks - half * hops - hop) % chunks
            start = pl.multiple_of((where[0] ^ rel) * rows + chunk * count, 16)
            left = 0
            for out, width in zip(outs, widths):
                copy = pltpu.make_async_copy(
                    piece.at[pl.ds(hop * count, count), pl.ds(left, width)],
                    out.at[pl.ds(start, count), :],
                    sems.at[len(copies)],
                )
                copy.start()
                copies.append(copy)
                left += width
    for copy in copies:
        copy.wait()


def settle(where, rels, pieces, widths, chunks):
    low = jnp.bfloat16
    total = sum(piece.shape[0] for piece in pieces)
    return pl.pallas_call(
        functools.partial(settle_kernel, rels, widths, chunks),
        out_shape=[jax.ShapeDtypeStruct((total, width), low) for width in widths],
        in_specs=[smem()] + hbm(len(pieces)),
        out_specs=hbm(len(widths)),
        scratch_shapes=[pltpu.SemaphoreType.DMA((len(pieces) * chunks * len(widths),))],
        compiler_params=pltpu.CompilerParams(vmem_limit_bytes=4 << 20),
        cost_estimate=pl.CostEstimate(flops=1, bytes_accessed=1, transcendentals=0),
        name="settle",
    )(where, *pieces)


def segment_pairs(n_doc, n_seq):
    places = [(d, z) for d in range(n_doc) for z in range(n_seq)]

    def route(target):
        pairs = [(d * n_seq + z, target(d, z)[0] * n_seq + target(d, z)[1]) for d, z in places]
        return [(source, goal) for source, goal in pairs if source != goal]

    def regroup(rel):
        def target(d, z):
            spot = z ^ rel
            return ((d & ~1) | (spot >> 1), 2 * (d & 1) + (spot & 1))

        return target

    routes = {
        "core": route(lambda d, z: (d ^ 1, z)),
        "x": route(lambda d, z: (d ^ 2, z)),
        "y": route(lambda d, z: (d ^ 4, z)),
        "xy": route(lambda d, z: (d ^ 6, z)),
        "z1": route(lambda d, z: (d, (z + 1) % n_seq)),
        "z2": route(lambda d, z: (d, (z + 2) % n_seq)),
        "z3": route(lambda d, z: (d, (z + 3) % n_seq)),
    }
    for rel in range(n_seq):
        routes["group", rel] = route(regroup(rel))
        routes["part", rel] = route(
            lambda d, z, rel=rel: (d ^ (rel >> 1), z ^ (rel & 1))
        )
    return routes


def later(values, *others):
    return lax.optimization_barrier((values, others))[0]


def on_pair(
    routes,
    tokens,
    w_query,
    w_key,
    w_value,
    w_out,
    w_gate,
    w_up,
    w_down,
    gain_attn,
    gain_ffn,
    cache_keys,
    cache_values,
    memory_flags,
    memory_source,
    positions,
    out_grad,
):
    low, wide = jnp.bfloat16, jnp.float32
    n_doc, n_seq = lax.axis_size("doc"), lax.axis_size("seq")
    d, z = lax.axis_index("doc"), lax.axis_index("seq")
    core, odd, pair, plane = d & 1, z & 1, z >> 1, d >> 1
    quarter = 2 * core + odd
    heads_at = 2 * odd + core
    turn = (0, 2, 1, 3)
    width = tokens.shape[2]
    ff_width = w_gate.shape[1]
    share = width // n_seq
    n_heads = share // HEAD_DIM
    where = jnp.stack([d, z]).astype(jnp.int32)
    mem_rows = 2 * n_seq * cache_keys.shape[1]

    def move(array, name):
        return lax.ppermute(array, LINE, routes[name])

    def to_group(array, rel=0):
        moved = move(array, ("group", rel))
        return moved if rel else jnp.where(pair == core, array, moved)

    def pick(array, index, axis=0):
        return lax.dynamic_index_in_dim(array, index, axis, keepdims=False)

    def plus(*terms):
        total = terms[0].astype(wide)
        for term in terms[1:]:
            total = total + term.astype(wide)
        return total.astype(low)

    def along_z(shard):
        return [shard] + [move(shard, f"z{hop}") for hop in range(1, n_seq)]

    def in_plane(block):
        return [block, move(block, "x"), move(block, "y"), move(block, "xy")]

    def swap_halves(pieces):
        cut = pieces[1].shape[0] // 2
        return [move(pieces[1][:cut], "y"), move(pieces[2][cut:], "x")]

    def other_core(pieces):
        return pieces + [move(piece, "core") for piece in pieces]

    rels = (0, 2, 4, 6, 1, 3, 5, 7)

    def part_for(array, rel, size):
        return lax.dynamic_slice_in_dim(array, (heads_at ^ turn[rel]) * size, size, 1)

    heads_where = heads_at.astype(jnp.int32).reshape(1)

    def spread(blocks):
        return join(heads_where, turn, blocks)

    def exchange(blocks):
        return [blocks[0]] + [move(blocks[rel], ("part", rel)) for rel in range(1, n_seq)]

    gains = jnp.concatenate([gain_attn[:, None], gain_ffn[:, None]], 1)
    gains = jnp.pad(gains, ((0, 0), (0, HEAD_DIM - 2)))
    lines = along_z(deal(n_heads, n_seq, w_query, w_key, w_value, gains))

    own_kv = jnp.concatenate([cache_keys[0], cache_values[0]], 1)
    two = jnp.stack([own_kv, move(own_kv, "x")])
    notes = jnp.concatenate([memory_flags, memory_source])
    notes_core, notes_y = later((move(notes, "core"), move(notes, "y")), two)
    flag = jnp.where(pair == core, notes[0], notes_core[0])
    source, source_y = notes[1], notes_y[1]
    place = jnp.stack([quarter, flag]).astype(jnp.int32)
    pos = [to_group(later(positions[0], two), rel) for rel in range(n_seq)]

    four = jnp.concatenate([two, move(two, "core")])

    def spot(src):
        return 2 * ((src ^ d) & 1) + (((src ^ d) >> 1) & 1)

    for_y = pick(four, spot(source_y))
    from_y = move(for_y, "y")
    block = jnp.concatenate(later(lines, for_y))
    rows = block.shape[0]
    projections = in_plane(block)
    lines_ab = along_z(later(jnp.concatenate([w_out, w_gate, w_up], 1), block))
    from_y = later(from_y, block)
    src_kv = jnp.where(((source ^ d) >> 2) == 0, pick(four, spot(source)), from_y)

    def heads_for(rel):
        to = z ^ rel
        at = (2 * (to & 1) + (to >> 1)) * share
        picked = [
            lax.dynamic_slice_in_dim(kv, side * width + at, share, 1)
            for kv in (own_kv, src_kv)
            for side in (0, 1)
        ]
        return jnp.concatenate(picked, 1)

    parts = [heads_for(rel) for rel in range(n_seq)]
    cos_h, sin_h = rotary_tables(jnp.concatenate(later(pos, parts)))
    cos_t = jnp.concatenate([cos_h, cos_h], -1)
    sin_t = jnp.concatenate([-sin_h, sin_h], -1)
    block_ab = jnp.concatenate(later(lines_ab, cos_t, sin_t))
    tok = to_group(later(tokens[0], block_ab))
    projections = later(projections, block_ab)
    pieces_ab = in_plane(later(block_ab, projections))[:3]
    *w_heads, gain_cols = settle(
        where,
        rels,
        other_core(projections),
        (3 * n_seq * HEAD_DIM,) * n_heads + (HEAD_DIM,),
        n_seq,
    )
    gain_a = gain_cols[:, 0].astype(wide)
    gain_f = gain_cols[:, 1].astype(wide)

    inputs = later(tok, w_heads).astype(wide)
    factor_one = rms_factor(inputs)
    normed_one = inputs * factor_one
    attn_in = (normed_one * gain_a).astype(low)

    def projected(head, *others):
        weight = later(w_heads[head], *others) if others else w_heads[head]
        qkv = dot_nn(attn_in, weight).astype(low)
        return [part_for(qkv, rel, 3 * HEAD_DIM) for rel in range(n_seq)]

    first = projected(0)
    first_own = first[0]
    first = exchange(first)
    parts = later(parts, first_own)
    memory = [to_group(part, rel) for rel, part in enumerate(parts)]
    second = projected(1, parts)
    second_own = second[0]
    second = exchange(second)
    pieces_ab = later(pieces_ab, second_own)
    far_ab = swap_halves(pieces_ab)
    first, memory = later((first, memory), pieces_ab)
    saved_0 = attend(0, place, first, memory, mem_rows, cos_t, sin_t)
    att_0 = saved_0[4]
    lines_c = along_z(later(w_down, att_0))
    *saved_1, o0, o1, o2, o3 = attend(
        1, place, later(second, att_0), memory, mem_rows, cos_t, sin_t, (att_0,)
    )
    block_c = jnp.stack(later(lines_c, o0))
    block_c = jnp.concatenate([pick(block_c, (z - at) % n_seq) for at in range(n_seq)])
    rows_c = block_c.shape[0]
    att = exchange(later([o0, o1, o2, o3], block_c))
    far_ab = later(far_ab, block_c)
    pieces_c = in_plane(later(block_c, far_ab))
    w_out_f, w_gate_f, w_up_f = settle(
        where,
        (0, 2, 4, 1, 3, 5, (6, 0), (6, 1), (7, 0), (7, 1)),
        other_core(later(pieces_ab, block_c)) + other_core(far_ab),
        (width, ff_width, ff_width),
        n_seq,
    )
    attn_low = spread(later(att, w_out_f))
    grad_y = to_group(later(out_grad[0], attn_low))
    resid_mid = inputs + dot_nn(attn_low, w_out_f)
    factor_two = rms_factor(resid_mid)
    normed_two = resid_mid * factor_two
    ffn_in = (normed_two * gain_f).astype(low)
    gate_act = dot_nn(ffn_in, w_gate_f)
    up_act = dot_nn(ffn_in, w_up_f)
    sig_gate = jax.nn.sigmoid(gate_act)
    silu_gate = gate_act * sig_gate
    hidden = (silu_gate * up_act).astype(low)
    grad_y, pieces_c = later((grad_y, pieces_c), hidden)

    def side(array, which, turned=True):
        return jnp.concatenate(
            [
                lax.dynamic_slice_in_dim(
                    array, (2 * (plane ^ rel if turned else rel) + which) * rows, rows, 1
                )
                for rel in range(n_doc // 2)
            ],
            1,
        )

    def plane_parts(both):
        size = both.shape[0] // (n_doc // 2)
        return [both[rel * size : (rel + 1) * size] for rel in range(n_doc // 2)]

    def over_plane(parts):
        return [parts[0]] + [
            move(part, name) for part, name in zip(parts[1:], ("x", "y", "xy"))
        ]

    def met_in_plane(both):
        return over_plane(plane_parts(both))

    def finish_by_hops(total):
        chunks = total.reshape(n_seq, -1, total.shape[1])
        return sum(
            (
                move(pick(chunks, (z + hop) % n_seq), f"z{hop}").astype(wide)
                for hop in range(1, n_seq)
            ),
            pick(chunks, z).astype(wide),
        )

    def kept(mine, array, met):
        return (dot_tn(mine, array) + met.astype(wide)).astype(low)

    pieces_c = other_core(pieces_c)
    grad_down = dot_tn(hidden, grad_y).astype(low).reshape(n_doc // 2, 2, rows_c, width)
    down_sent = pick(grad_down, 1 - core, 1)
    met_down = move(down_sent, "core")
    (w_down_f,) = settle(where, rels, later(pieces_c, down_sent), (width,), 1)
    layer_out = (resid_mid + dot_nn(hidden, w_down_f)).astype(low)
    layer_moved = to_group(layer_out)
    d_hidden = dot_nt(later(grad_y, layer_out), w_down_f)
    d_gate = (d_hidden * up_act * (sig_gate * (1.0 + gate_act * (1.0 - sig_gate)))).astype(low)
    d_up = (d_hidden * silu_gate).astype(low)
    d_ffn_in = dot_nt(d_gate, w_gate_f) + dot_nt(d_up, w_up_f)
    d_mid = grad_y.astype(wide) + norm_back(d_ffn_in * gain_f, normed_two, factor_two)
    layer_out = later(layer_moved, d_ffn_in)
    d_branch = later(d_mid, layer_out).astype(low)
    d_att = dot_nt(d_branch, w_out_f).astype(low)
    d_blocks = [part_for(d_att, rel, share) for rel in range(n_seq)]
    d_sent = d_blocks[0]
    d_blocks = exchange(d_blocks)
    met_down = later(met_down, d_sent)
    both_down = plus(pick(grad_down, core, 1), met_down)
    down_parts = [pick(both_down, plane ^ rel) for rel in range(n_doc // 2)]
    total_down = over_plane(down_parts)
    away, home = side(ffn_in, 1 - core), side(ffn_in, core)
    away_gate = dot_tn(away, d_gate).astype(low)
    met_gate = move(away_gate, "core")
    away_up = dot_tn(later(away, away_gate), d_up).astype(low)
    met_up = move(away_up, "core")
    d_blocks = later(d_blocks, away_up)
    g_0 = attend_back(
        0, place, saved_0, d_blocks, memory, mem_rows, cos_t, sin_t, down_parts[1:]
    )
    d_set_0 = exchange(g_0)
    both_gate = kept(home, d_gate, later(met_gate, g_0))
    both_up = kept(home, d_up, later(met_up, both_gate))
    total_down = later(total_down, both_up)
    gate_parts = plane_parts(later(both_gate, total_down))
    total_gate = over_plane(gate_parts)
    g_1 = attend_back(
        1, place, saved_1, later(d_blocks, both_up), memory, mem_rows, cos_t, sin_t,
        (both_up, *total_down[1:], *gate_parts[1:]),
    )
    g_1 = later(g_1, d_set_0)
    d_set_1 = exchange(g_1)

    away, home_in = side(attn_in, 1 - core), side(attn_in, core)
    d_qkv_0 = spread(later(d_set_0, g_1))
    away_0 = dot_tn(away, d_qkv_0).astype(low)
    met_0 = move(away_0, "core")
    total_gate = later(total_gate, away_0)
    total_up = met_in_plane(later(both_up, total_gate))
    d_set_1 = later(d_set_1, total_gate)
    d_qkv_1 = spread(d_set_1)
    away_1 = dot_tn(away, d_qkv_1).astype(low)
    met_1 = move(away_1, "core")
    out_down = finish_by_hops(plus(*later(total_down, away_1)))
    both_0 = kept(home_in, d_qkv_0, later(met_0, away_1))
    away_out = dot_tn(later(side(attn_low, 1 - core), both_0), d_branch).astype(low)
    met_out = move(away_out, "core")
    both_1 = kept(home_in, d_qkv_1, later(met_1, away_out))
    both_out = kept(side(attn_low, core), later(d_branch, both_1), later(met_out, both_1))
    both = jnp.concatenate([both_0, both_1, both_out], 1)
    total_gate = plus(*later(total_gate, both))
    out_gate = finish_by_hops(total_gate)
    total_up = later(total_up, total_gate)
    last = met_in_plane(later(both, total_up))
    d_attn_in = dot_nt(later(d_qkv_0, total_up), w_heads[0]) + dot_nt(
        later(d_qkv_1, total_up), w_heads[1]
    )
    grad_in = d_mid + norm_back(d_attn_in * gain_a, normed_one, factor_one)
    grad_in = grad_in.astype(low)
    grad_tokens = to_group(grad_in).astype(wide)
    out_up = finish_by_hops(plus(*later(total_up, grad_in)))
    both = finish_by_hops(plus(*later(last, grad_in)))
    out_out = both[:, 3 * width :]
    split = both[:, : 3 * width].reshape(-1, n_heads, n_seq, 3, HEAD_DIM)
    split = jnp.swapaxes(split, 1, 2)
    out_q, out_k, out_v = (split[:, :, :, which].reshape(-1, width) for which in range(3))

    def gain_grad(gain, pairs):
        total = sum(jnp.sum(weight.astype(wide) * grad, 1) for weight, grad in pairs)
        return total / gain.astype(wide)

    return (
        layer_out[None],
        grad_tokens[None],
        out_q,
        out_k,
        out_v,
        out_out,
        out_gate,
        out_up,
        out_down,
        gain_grad(gain_attn, ((w_query, out_q), (w_key, out_k), (w_value, out_v))),
        gain_grad(gain_ffn, ((w_gate, out_gate), (w_up, out_up))),
    )


def solution(mesh):
    in_specs = (
        P("doc", "seq", None),
        P(("doc", "seq"), None),
        P(("doc", "seq"), None),
        P(("doc", "seq"), None),
        P(("doc", "seq"), None),
        P(("doc", "seq"), None),
        P(("doc", "seq"), None),
        P(("doc", "seq"), None),
        P(("doc", "seq")),
        P(("doc", "seq")),
        P("doc", "seq", None),
        P("doc", "seq", None),
        P("doc"),
        P("doc"),
        P("doc", "seq"),
        P("doc", "seq", None),
    )
    out_specs = (
        P("doc", "seq", None),
        P("doc", "seq", None),
        P(("doc", "seq"), None),
        P(("doc", "seq"), None),
        P(("doc", "seq"), None),
        P(("doc", "seq"), None),
        P(("doc", "seq"), None),
        P(("doc", "seq"), None),
        P(("doc", "seq"), None),
        P(("doc", "seq")),
        P(("doc", "seq")),
    )
    n_doc, n_seq = mesh.shape["doc"], mesh.shape["seq"]
    step = on_device
    if (n_doc, n_seq) == (8, 4):
        step = functools.partial(on_pair, segment_pairs(n_doc, n_seq))
    return jax.shard_map(
        step, mesh=mesh, in_specs=in_specs, out_specs=out_specs, check_vma=False
    )
```
